32 devices in a mesh: ctx: 16 (over z, y, x), wt: 2 (over core).
Axes of the slice: x: 2, y: 2, z: 4, core: 2. Of those that a mesh axis runs over, the one named last changes fastest.
Arguments:
- block_input: bfloat16 [4, 2304, 768], P('wt', 'ctx'), may hold values from -6 to 6
- span_order: int32 [16, 2], replicated, may hold values from 0 to 31, as said below
- doc_lengths: int32 [4, 4], P('wt'), may hold values from 1 to 1152, 2304 in all within a row
- ln1_gain: bfloat16 [768], P('wt'), may hold values from 0.5 to 1.5
- ln1_bias: bfloat16 [768], P('wt'), may hold values from -1.796875 to 1.796875
- w_qkv: bfloat16 [768, 2304], P('wt'), may hold values from -0.21875 to 0.21875
- qv_bias: bfloat16 [2, 768], P(None, 'wt'), may hold values from -0.59765625 to 0.59765625
- w_out: bfloat16 [768, 768], P('wt'), may hold values from -12 to 12
- out_bias: bfloat16 [768], P('wt'), may hold values from -6 to 6
- ln2_gain: bfloat16 [768], P('wt'), may hold values from 0.5 to 1.5
- ln2_bias: bfloat16 [768], P('wt'), may hold values from -1.796875 to 1.796875
- w_fc: bfloat16 [768, 3072], P('wt'), may hold values from -0.21875 to 0.21875
- fc_bias: bfloat16 [3072], P('wt'), may hold values from -3 to 3
- w_proj: bfloat16 [3072, 768], P('wt'), may hold values from -0.75 to 0.75
- proj_bias: bfloat16 [768], P('wt'), may hold values from -6 to 6
- d_out: bfloat16 [4, 2304, 768], P('wt', 'ctx'), may hold values from -6 to 6
Outputs:
- block_out: bfloat16 [4, 2304, 768], P('wt', 'ctx')
- d_input: float32 [4, 2304, 768], P('wt', 'ctx')
- grad_ln1_gain: float32 [768], P('wt')
- grad_ln1_bias: float32 [768], P('wt')
- grad_w_qkv: float32 [768, 2304], P('wt')
- grad_qv_bias: float32 [2, 768], P(None, 'wt')
- grad_w_out: float32 [768, 768], P('wt')
- grad_out_bias: float32 [768], P('wt')
- grad_ln2_gain: float32 [768], P('wt')
- grad_ln2_bias: float32 [768], P('wt')
- grad_w_fc: float32 [768, 3072], P('wt')
- grad_fc_bias: float32 [3072], P('wt')
- grad_w_proj: float32 [3072, 768], P('wt')
- grad_proj_bias: float32 [768], P('wt')
The draws below stay inside these ranges and needn't reach their ends.
Inputs may be any that keep to these rules, and one draw needn't show every extreme that they name: `span_order`: row i names two spans j and 31 - j, in either order; every span of 0 to 31 is named exactly once. `doc_lengths`: each row sums to 2304, and its largest entry is 1152.
All inputs are finite; a program needn't handle non-finite values.
Results may differ from the reference program's by a relative error of at most 0.015.
Values may be sent and summed in bfloat16 or wider, within the bound.
No kernel may reach another device: no remote copies, remote signals or barrier semaphores. Data moves between devices by JAX's collectives and lax.ppermute only.
A program may use at most 320 MiB of HBM per device.

```python
import math
import jax
import jax.numpy as jnp
import numpy as np
from jax import lax

D = 768
HEADS = 12
HEAD_DIM = 64
FF = 3072
SEQ_DEV = 144
NDOCS = 4
SEQS = 4
SEQ_LEN = 2304
SPAN = 72
SPANS = 32
LONGEST = 1152


def draw_span_order(key, part):
    pair_key, flip_key = jax.random.split(key)
    pairs = jax.random.permutation(pair_key, SPANS // 2).astype(jnp.int32)
    flips = jax.random.randint(flip_key, (SPANS // 2,), 0, 2, dtype=jnp.int32)
    first = jnp.where(flips == 1, SPANS - 1 - pairs, pairs).astype(jnp.int32)
    return jnp.stack([first, SPANS - 1 - first], axis=1).astype(jnp.int32)


def steps_of(rng, dims, cuts, low, largest):
    level = 1.0
    for position, blocks in cuts:
        heights = jax.random.uniform(jax.random.fold_in(jax.random.fold_in(rng, 6), position), (blocks,), jnp.float32, low / len(cuts), largest / len(cuts))
        level = level * jnp.repeat(jnp.exp(heights), dims[position] // blocks).reshape((-1,) + (1,) * (len(dims) - 1 - position))
    return level


def length_profile(count, total, bound, slope):
    portions = [(1 << 20) // math.isqrt(rank ** slope) + 1 for rank in range(2, count + 1)]
    rest, holding = total - bound - (count - 1), [1] * (count - 1)
    while rest > 0:
        candidates = [i for i in range(count - 1) if holding[i] < bound]
        mass, left = sum([portions[i] for i in candidates]), rest
        for i in candidates:
            addition = min(bound - holding[i], max(1, left * portions[i] // mass), rest)
            holding[i] = holding[i] + addition
            rest = rest - addition
    return np.array([bound] + holding)


def ragged_sizes(own_key, count, total, most, slope):
    if count == 2:
        one = jax.random.randint(own_key, (), max(1, total - most), min(most, total - 1) + 1)
        return jnp.stack([one, total - one])
    lengths = jnp.asarray(length_profile(count, total, most, slope), jnp.int32)
    couples = (count - 1) // 2
    source_of, receiver = lengths[1:1 + 2 * couples:2], lengths[2:2 + 2 * couples:2]
    margin = jnp.minimum(source_of - 1, most - receiver)
    shifted = jax.random.randint(jax.random.fold_in(own_key, 1), (couples,), 0, 1 << 20) % (margin + 1)
    lengths = lengths.at[1:1 + 2 * couples:2].set(source_of - shifted).at[2:2 + 2 * couples:2].set(receiver + shifted)
    return lengths[jax.random.permutation(jax.random.fold_in(own_key, 2), count)]


def noise(rng, dims, width, reach, shards=(), held_as=jnp.bfloat16):
    values = jax.random.normal(rng, dims, jnp.float32) * width
    if len(shards) > 0:
        values = steps_of(rng, dims, shards, -0.22, 0.18) * values
    return jnp.clip(values, min=-reach, max=reach).astype(held_as)


def setup_inputs(seed: int = 0) -> dict:
    keys = jax.random.split(jax.random.key(seed), 17)
    return {
        "block_input": noise(keys[0], (SEQS, SEQ_LEN, D), 1.0, 6.0, ((0, 2), (1, 16))),
        "span_order": draw_span_order(jax.random.fold_in(keys[16], 71), 0),
        "doc_lengths": jax.vmap(lambda own: ragged_sizes(own, NDOCS, SEQ_LEN, LONGEST, 2))(jax.random.split(keys[2], SEQS)).reshape((SEQS, NDOCS)).astype(jnp.int32),
        "ln1_gain": jnp.clip(1.0 + 0.1 * jax.random.normal(keys[3], (D,), jnp.float32), 0.5, 1.5).astype(jnp.bfloat16),
        "ln1_bias": noise(keys[4], (D,), 0.3, 1.796875, ((0, 2),)),
        "w_qkv": noise(keys[5], (D, 3 * D), D ** -0.5, 0.21875, ((0, 2),)),
        "qv_bias": noise(keys[6], (2, D), 0.1, 0.59765625, ((1, 2),)),
        "w_out": noise(keys[7], (D, D), 2.0, 12.0, ((0, 2),)),
        "out_bias": noise(keys[8], (D,), 1.0, 6.0, ((0, 2),)),
        "ln2_gain": jnp.clip(1.0 + 0.1 * jax.random.normal(keys[9], (D,), jnp.float32), 0.5, 1.5).astype(jnp.bfloat16),
        "ln2_bias": noise(keys[10], (D,), 0.3, 1.796875, ((0, 2),)),
        "w_fc": noise(keys[11], (D, FF), D ** -0.5, 0.21875, ((0, 2),)),
        "fc_bias": noise(keys[12], (FF,), 0.5, 3.0, ((0, 2),)),
        "w_proj": noise(keys[13], (FF, D), (FF // 48) ** -0.5, 0.75, ((0, 2),)),
        "proj_bias": noise(keys[14], (D,), 1.0, 6.0, ((0, 2),)),
        "d_out": noise(keys[15], (SEQS, SEQ_LEN, D), 1.0, 6.0, ((0, 2), (1, 16))),
    }


branch_scale = 0.14433756729740643
neg_large = -1e+30

@jax.custom_vjp
def low(v):
    return lax.optimization_barrier(v.astype(jnp.bfloat16)).astype(jnp.float32)

@jax.custom_vjp
def low_back(v):
    return v

def low_keep(v):
    return (low(v), None)

def low_pass(kept, grad):
    return (grad,)

def back_keep(v):
    return (v, None)

def back_low(kept, grad):
    return (low(grad),)
low.defvjp(low_keep, low_pass)
low_back.defvjp(back_keep, back_low)

def layer_norm(values, gain, shift):
    center = lax.optimization_barrier(jnp.mean(values, axis=-1, keepdims=True))
    moved = values - center
    spread = lax.optimization_barrier(jnp.mean(moved * moved, axis=-1, keepdims=True))
    return moved * lax.rsqrt(spread + 1e-05) * gain + shift

def gelu_tanh(values):
    return 0.5 * values * (1.0 + jnp.tanh(0.7978845608028654 * (values + 0.044715 * values * values * values)))

def matmul_high(left, right):
    return jnp.dot(left, right, precision=lax.Precision.HIGHEST)

def split_count(row_total, limit):
    pieces = 1
    while row_total % pieces != 0 or row_total // pieces > limit:
        pieces += 1
    return pieces

def seq_positions(order_table):
    rows_all = jnp.arange(SEQ_LEN, dtype=jnp.int32)
    device_of = rows_all // SEQ_DEV
    half_of = rows_all % SEQ_DEV // SPAN
    return (order_table[device_of, half_of] * SPAN + rows_all % SPAN).astype(jnp.int32)

def doc_of(positions, lengths_row):
    ends_at = jnp.cumsum(lengths_row).astype(jnp.int32)
    inner_ends = ends_at[:-1]
    return lax.optimization_barrier(jnp.sum((positions[:, None] >= inner_ends[None, :]).astype(jnp.int32), axis=1)).astype(jnp.int32)

def attend(query_block, query_pos, query_doc, keys_all, values_all, key_pos, key_doc, score_scale):
    scores = jnp.einsum('qhd,khd->qhk', query_block, keys_all, precision=lax.Precision.HIGHEST) * score_scale
    allowed = ((key_pos[None, :] <= query_pos[:, None]) & (key_doc[None, :] == query_doc[:, None]))[:, None, :]
    scores = low_back(jnp.where(allowed, scores, neg_large))
    top_score = lax.optimization_barrier(jnp.max(scores, axis=-1, keepdims=True))
    weights = jnp.exp(scores - top_score)
    probs = weights / lax.optimization_barrier(jnp.sum(weights, axis=-1, keepdims=True))
    return jnp.einsum('qhk,khd->qhd', low(probs), values_all, precision=lax.Precision.HIGHEST)

def one_sequence(tokens, lengths_row, order_table, params):
    gain_one, shift_one, weight_qkv, bias_pair, weight_out, bias_out, gain_two, shift_two, weight_fc, bias_fc, weight_proj, bias_proj = params
    positions = seq_positions(order_table)
    documents = doc_of(positions, lengths_row)
    normed_one = low(layer_norm(tokens, gain_one, shift_one))
    qkv_bias = jnp.concatenate([bias_pair[0], jnp.zeros_like(bias_pair[0]), bias_pair[1]])
    projected = low(low_back(matmul_high(normed_one, weight_qkv) + qkv_bias))
    queries = projected[:, :D].reshape(SEQ_LEN, HEADS, HEAD_DIM)
    keys_all = projected[:, D:2 * D].reshape(SEQ_LEN, HEADS, HEAD_DIM)
    values_all = projected[:, 2 * D:].reshape(SEQ_LEN, HEADS, HEAD_DIM)
    score_scale = HEAD_DIM ** (-0.5)
    block_count = split_count(SEQ_LEN, 1024)
    block_rows = SEQ_LEN // block_count

    def block_fn(block_args):
        return attend(block_args[0], block_args[1], block_args[2], keys_all, values_all, positions, documents, score_scale)
    attended = lax.map(jax.checkpoint(block_fn), (queries.reshape(block_count, block_rows, HEADS, HEAD_DIM), positions.reshape(block_count, block_rows), documents.reshape(block_count, block_rows)))
    attended = low(low_back(attended.reshape(SEQ_LEN, D)))
    branch_attn = low_back(matmul_high(attended, weight_out) + bias_out)
    resid_one = tokens + branch_scale * branch_attn
    normed_two = low(layer_norm(resid_one, gain_two, shift_two))
    hidden_pre = low_back(matmul_high(normed_two, weight_fc) + bias_fc)
    hidden_act = low(gelu_tanh(hidden_pre))
    branch_mlp = low_back(matmul_high(hidden_act, weight_proj) + bias_proj)
    return resid_one + branch_scale * branch_mlp

def reference(block_input, span_order, doc_lengths, ln1_gain, ln1_bias, w_qkv, qv_bias, w_out, out_bias, ln2_gain, ln2_bias, w_fc, fc_bias, w_proj, proj_bias, d_out):
    floats = tuple((arr.astype(jnp.float32) for arr in (ln1_gain, ln1_bias, w_qkv, qv_bias, w_out, out_bias, ln2_gain, ln2_bias, w_fc, fc_bias, w_proj, proj_bias)))

    def forward(tokens, *params):

        def per_seq(seq_item):
            return one_sequence(seq_item[0], seq_item[1], span_order, params)
        return lax.map(per_seq, (tokens, doc_lengths))
    block_out, pull_back = jax.vjp(forward, block_input.astype(jnp.float32), *floats)
    gradients = pull_back(d_out.astype(jnp.float32))
    return (block_out.astype(jnp.bfloat16), gradients[0], gradients[1], gradients[2], gradients[3], gradients[4], gradients[5], gradients[6], gradients[7], gradients[8], gradients[9], gradients[10], gradients[11], gradients[12])
```

```python
import functools

import jax
import jax.numpy as jnp
from jax import lax
from jax.experimental import pallas as pl
from jax.experimental.pallas import tpu as pltpu
from jax.sharding import PartitionSpec as P

HEADS = 12

branch_scale = 0.14433756729740643
neg_large = -1e30
f32 = jnp.float32
bf16 = jnp.bfloat16
VMEM = pltpu.VMEM
vmem_cap = 56 << 20

GROUPS = 4
TILE = 128
PAD = 256

pair = [(0, 1), (1, 0)]
x_pairs = [(i, i ^ 1) for i in range(16)]
y_pairs = [(i, i ^ 2) for i in range(16)]


def z_shift(step):
    return [(i, (i // 4 + step) % 4 * 4 + i % 4) for i in range(16)]


def other_core(value):
    return lax.ppermute(value, "wt", pair)


def send_x(value):
    return lax.ppermute(value, "ctx", x_pairs)


def send_y(value):
    return lax.ppermute(value, "ctx", y_pairs)


def send_z(value, step):
    return lax.ppermute(value, "ctx", z_shift(step))


def row(value, index):
    return lax.dynamic_index_in_dim(value, index, 0, keepdims=False)


def sum_low(*terms):
    total = terms[0].astype(f32)
    for term in terms[1:]:
        total = total + term.astype(f32)
    return total.astype(bf16)


def full_spec(shape):
    zeros = (0,) * len(shape)
    return pl.BlockSpec(shape, lambda *unused: zeros)


def dot(left, right, dims):
    return lax.dot_general(left, right, (dims, ((), ())), preferred_element_type=f32)


def norm_parts(rows):
    center = jnp.mean(rows, axis=-1, keepdims=True)
    moved = rows - center
    spread = jnp.mean(moved * moved, axis=-1, keepdims=True)
    inverse = lax.rsqrt(spread + 1e-05)
    return moved * inverse, inverse


def project_kernel(
    order_ref, a_ref, b_ref, c_ref, d_ref, gain_ref, shift_ref, weight_ref, bias_ref,
    h_ref, q_ref, kv_ref,
):
    rows = jnp.concatenate([r[0].astype(f32) for r in (a_ref, b_ref, c_ref, d_ref)], axis=0)
    normed, unused = norm_parts(rows)
    low = (normed * gain_ref[...] + shift_ref[...]).astype(bf16)
    h_ref[...] = low
    out = dot(low, weight_ref[...], ((1,), (0,))) + bias_ref[...]
    q_ref[...] = (out[:, :PAD].astype(bf16) * 0.125).astype(bf16)
    kv_ref[...] = out[:, PAD:].astype(bf16)


def span_specs(span_rows, width):
    return [
        pl.BlockSpec((1, span_rows, width), lambda i, order, t=t: (order[4 * i + t], 0, 0))
        for t in range(4)
    ]


def project(order, pieces, gain, shift, weight, bias):
    spans, span_rows, width = pieces.shape
    rows = spans * span_rows
    step = 4 * span_rows
    grid_spec = pltpu.PrefetchScalarGridSpec(
        num_scalar_prefetch=1,
        grid=(spans // 4,),
        in_specs=span_specs(span_rows, width)
        + [
            full_spec((1, width)),
            full_spec((1, width)),
            full_spec((width, 3 * PAD)),
            full_spec((1, 3 * PAD)),
        ],
        out_specs=[
            pl.BlockSpec((step, width), lambda i, order: (i, 0)),
            pl.BlockSpec((step, PAD), lambda i, order: (i, 0)),
            pl.BlockSpec((step, 2 * PAD), lambda i, order: (i, 0)),
        ],
    )
    return pl.pallas_call(
        project_kernel,
        grid_spec=grid_spec,
        out_shape=[
            jax.ShapeDtypeStruct((rows, width), bf16),
            jax.ShapeDtypeStruct((rows, PAD), bf16),
            jax.ShapeDtypeStruct((rows, 2 * PAD), bf16),
        ],
        compiler_params=pltpu.CompilerParams(vmem_limit_bytes=vmem_cap),
        cost_estimate=pl.CostEstimate(
            flops=2 * rows * width * 3 * PAD, bytes_accessed=6 << 20, transcendentals=0
        ),
        name="project",
    )(order, pieces, pieces, pieces, pieces, gain, shift, weight, bias)


def by_head(tile):
    lane = lax.broadcasted_iota(jnp.int32, tile.shape, 1)
    zero = jnp.zeros_like(tile)
    return jnp.concatenate(
        [jnp.where((lane >= 64 * h) & (lane < 64 * h + 64), tile, zero) for h in range(3)], axis=0
    )


def visible_tile(kpos_ref, tile_row, meta_ref):
    rows = pl.ds(tile_row, TILE)
    keys = jnp.concatenate([kpos_ref[0, rows, :], kpos_ref[1, rows, :]], axis=0)
    return (keys <= meta_ref[0, 0:1, :]) & (keys >= meta_ref[0, 1:2, :])


def attend_kernel(
    low_ref, high_ref, slot_ref, q_ref, own_ref, oth_ref, kpos_ref, meta_ref,
    o_ref, lse_ref, out_ref,
    vown, voth, stack, acc, top,
):
    i = pl.program_id(0)
    spans, span_rows, feats = out_ref.shape

    @pl.when(i == 0)
    def _():
        vown[...] = own_ref[:, PAD:].T
        voth[...] = oth_ref[:, PAD:].T

    stack[...] = by_head(q_ref[...])
    acc[...] = jnp.zeros_like(acc)
    top[...] = jnp.full_like(top, neg_large)

    def one(j, carry):
        first = pl.multiple_of(j * TILE, TILE)
        rows = pl.ds(first, TILE)
        keys = jnp.concatenate([own_ref[rows, :PAD], oth_ref[rows, :PAD]], axis=0)
        scores = dot(keys, stack[...], ((1,), (1,)))
        allowed = visible_tile(kpos_ref, first, meta_ref)
        allowed = jnp.concatenate([allowed, allowed, allowed], axis=1)
        scores = jnp.where(allowed, scores, neg_large)
        old = top[...]
        new = jnp.maximum(old, jnp.max(scores, axis=0, keepdims=True))
        probs = jnp.exp(scores - new).astype(bf16)
        vals = jnp.concatenate([vown[:, rows], voth[:, rows]], axis=1)
        acc[...] = acc[...] * jnp.exp(old - new) + dot(vals, probs, ((1,), (0,)))
        top[...] = new
        return carry

    lax.fori_loop(low_ref[i], high_ref[i], one, 0)
    total = acc[192:193, :]
    lse_ref[0] = top[...] + jnp.log(total)
    parts = [
        acc[64 * h : 64 * h + 64, TILE * h : TILE * h + TILE] / total[:, TILE * h : TILE * h + TILE]
        for h in range(3)
    ]
    heads_t = jnp.concatenate(parts + [jnp.zeros((64, TILE), f32)], axis=0)
    o_ref[pl.ds(pl.multiple_of(i * TILE, TILE), TILE), :] = heads_t.T

    @pl.when(i == pl.num_programs(0) - 1)
    def _():
        for a in range(spans):
            out_ref[slot_ref[a]] = o_ref[span_rows * a : span_rows * (a + 1), :feats].astype(bf16)


def attend(low, high, slot, q, own, oth, kpos, meta, spans):
    rows = q.shape[0]
    tiles = rows // TILE
    wide = 3 * TILE
    grid_spec = pltpu.PrefetchScalarGridSpec(
        num_scalar_prefetch=3,
        grid=(tiles,),
        in_specs=[
            pl.BlockSpec((TILE, PAD), lambda i, *unused: (i, 0)),
            full_spec((rows, 2 * PAD)),
            full_spec((rows, 2 * PAD)),
            full_spec((2, rows, TILE)),
            pl.BlockSpec((1, 2, TILE), lambda i, *unused: (i, 0, 0)),
        ],
        out_specs=[
            full_spec((rows, PAD)),
            pl.BlockSpec((1, 1, wide), lambda i, *unused: (i, 0, 0)),
            full_spec((spans, rows // spans, 192)),
        ],
        scratch_shapes=[
            VMEM((PAD, rows), bf16),
            VMEM((PAD, rows), bf16),
            VMEM((wide, PAD), bf16),
            VMEM((PAD, wide), f32),
            VMEM((1, wide), f32),
        ],
    )
    return pl.pallas_call(
        attend_kernel,
        grid_spec=grid_spec,
        out_shape=[
            jax.ShapeDtypeStruct((rows, PAD), f32),
            jax.ShapeDtypeStruct((tiles, 1, wide), f32),
            jax.ShapeDtypeStruct((spans, rows // spans, 192), bf16),
        ],
        compiler_params=pltpu.CompilerParams(vmem_limit_bytes=vmem_cap),
        cost_estimate=pl.CostEstimate(
            flops=2 * wide * rows * PAD * tiles, bytes_accessed=8 << 20, transcendentals=rows * rows
        ),
        name="attend",
    )(low, high, slot, q, own, oth, kpos, meta)


def attend_back_kernel(
    low_ref, high_ref, slot_ref, q_ref, own_ref, oth_ref, kpos_ref, meta_ref, grad_ref, o_ref, lse_ref,
    dq_ref, down_ref, doth_ref,
    grads, kown, koth, acc_own, acc_oth, stack, gstack, dq_t,
):
    i = pl.program_id(0)
    spans, span_rows, feats = grad_ref.shape

    @pl.when(i == 0)
    def _():
        kown[...] = own_ref[:, :PAD].T
        koth[...] = oth_ref[:, :PAD].T
        acc_own[...] = jnp.zeros_like(acc_own)
        acc_oth[...] = jnp.zeros_like(acc_oth)
        grads[...] = jnp.zeros_like(grads)
        for a in range(spans):
            grads[span_rows * a : span_rows * (a + 1), :feats] = grad_ref[slot_ref[a]].astype(f32)

    here = pl.ds(pl.multiple_of(i * TILE, TILE), TILE)
    grad = grads[here, :]
    stack[...] = by_head(q_ref[...])
    gstack[...] = by_head(grad.astype(bf16))
    product = (grad * o_ref[...]).T
    delta = jnp.concatenate(
        [jnp.sum(product[64 * h : 64 * h + 64], axis=0, keepdims=True) for h in range(3)], axis=1
    )
    lse = lse_ref[0]
    dq_t[...] = jnp.zeros_like(dq_t)

    def one(j, carry):
        first = pl.multiple_of(j * TILE, TILE)
        rows = pl.ds(first, TILE)
        keys = jnp.concatenate([own_ref[rows, :PAD], oth_ref[rows, :PAD]], axis=0)
        vals = jnp.concatenate([own_ref[rows, PAD:], oth_ref[rows, PAD:]], axis=0)
        scores = dot(keys, stack[...], ((1,), (1,)))
        allowed = visible_tile(kpos_ref, first, meta_ref)
        allowed = jnp.concatenate([allowed, allowed, allowed], axis=1)
        probs = jnp.where(allowed, jnp.exp(scores - lse), 0.0)
        d_probs = dot(vals, gstack[...], ((1,), (1,)))
        d_scores = (probs * (d_probs - delta)).astype(bf16)
        d_vals = dot(probs.astype(bf16), gstack[...], ((1,), (0,)))
        d_keys = dot(d_scores, stack[...], ((1,), (0,)))
        acc_own[rows, :PAD] += d_keys[:TILE]
        acc_own[rows, PAD:] += d_vals[:TILE]
        acc_oth[rows, :PAD] += d_keys[TILE:]
        acc_oth[rows, PAD:] += d_vals[TILE:]
        keys_t = jnp.concatenate([kown[:, rows], koth[:, rows]], axis=1)
        dq_t[...] += dot(keys_t, d_scores, ((1,), (0,)))
        return carry

    lax.fori_loop(low_ref[i], high_ref[i], one, 0)
    parts = [dq_t[64 * h : 64 * h + 64, TILE * h : TILE * h + TILE] for h in range(3)]
    heads_t = jnp.concatenate(parts + [jnp.zeros((64, TILE), f32)], axis=0) * 0.125
    dq_ref[...] = heads_t.T.astype(bf16)

    @pl.when(i == pl.num_programs(0) - 1)
    def _():
        down_ref[...] = acc_own[...]
        doth_ref[...] = acc_oth[...].astype(bf16)


def attend_back(low, high, slot, q, own, oth, kpos, meta, grad, o, lse):
    rows = q.shape[0]
    tiles = rows // TILE
    wide = 3 * TILE
    grid_spec = pltpu.PrefetchScalarGridSpec(
        num_scalar_prefetch=3,
        grid=(tiles,),
        in_specs=[
            pl.BlockSpec((TILE, PAD), lambda i, *unused: (i, 0)),
            full_spec((rows, 2 * PAD)),
            full_spec((rows, 2 * PAD)),
            full_spec((2, rows, TILE)),
            pl.BlockSpec((1, 2, TILE), lambda i, *unused: (i, 0, 0)),
            full_spec(grad.shape),
            pl.BlockSpec((TILE, PAD), lambda i, *unused: (i, 0)),
            pl.BlockSpec((1, 1, wide), lambda i, *unused: (i, 0, 0)),
        ],
        out_specs=[
            pl.BlockSpec((TILE, PAD), lambda i, *unused: (i, 0)),
            full_spec((rows, 2 * PAD)),
            full_spec((rows, 2 * PAD)),
        ],
        scratch_shapes=[
            VMEM((rows, PAD), f32),
            VMEM((PAD, rows), bf16),
            VMEM((PAD, rows), bf16),
            VMEM((rows, 2 * PAD), f32),
            VMEM((rows, 2 * PAD), f32),
            VMEM((wide, PAD), bf16),
            VMEM((wide, PAD), bf16),
            VMEM((PAD, wide), f32),
        ],
    )
    return pl.pallas_call(
        attend_back_kernel,
        grid_spec=grid_spec,
        out_shape=[
            jax.ShapeDtypeStruct((rows, PAD), bf16),
            jax.ShapeDtypeStruct((rows, 2 * PAD), f32),
            jax.ShapeDtypeStruct((rows, 2 * PAD), bf16),
        ],
        compiler_params=pltpu.CompilerParams(vmem_limit_bytes=vmem_cap),
        cost_estimate=pl.CostEstimate(
            flops=5 * wide * rows * PAD * tiles, bytes_accessed=12 << 20, transcendentals=rows * rows
        ),
        name="attend_back",
    )(low, high, slot, q, own, oth, kpos, meta, grad, o, lse)


def unproject_kernel(
    order_ref, a_ref, b_ref, c_ref, d_ref, dq_ref, down_ref, doth_ref, weight_ref,
    pieces_ref, grad_ref, gain_ref, shift_ref, bias_ref,
):
    i = pl.program_id(0)
    span_rows = a_ref.shape[1]

    @pl.when(i == 0)
    def _():
        gain_ref[...] = jnp.zeros_like(gain_ref)
        shift_ref[...] = jnp.zeros_like(shift_ref)
        bias_ref[...] = jnp.zeros_like(bias_ref)

    rows = jnp.concatenate([r[0].astype(f32) for r in (a_ref, b_ref, c_ref, d_ref)], axis=0)
    normed, unused = norm_parts(rows)
    dkv = (down_ref[...] + doth_ref[...].astype(f32)).astype(bf16)
    grad = jnp.concatenate([dq_ref[...], dkv], axis=1)
    grad_ref[...] = grad
    bias_ref[...] += jnp.sum(grad.astype(f32), axis=0, keepdims=True)
    back = dot(grad, weight_ref[...], ((1,), (1,)))
    gain_ref[...] += jnp.sum(back * normed, axis=0, keepdims=True)
    shift_ref[...] += jnp.sum(back, axis=0, keepdims=True)
    for t in range(4):
        pieces_ref[order_ref[4 * i + t]] = back[span_rows * t : span_rows * (t + 1)].astype(bf16)


def unproject(order, pieces, dq, down, doth, weight):
    spans, span_rows, width = pieces.shape
    rows = spans * span_rows
    step = 4 * span_rows
    grid_spec = pltpu.PrefetchScalarGridSpec(
        num_scalar_prefetch=1,
        grid=(spans // 4,),
        in_specs=span_specs(span_rows, width)
        + [
            pl.BlockSpec((step, PAD), lambda i, order: (i, 0)),
            pl.BlockSpec((step, 2 * PAD), lambda i, order: (i, 0)),
            pl.BlockSpec((step, 2 * PAD), lambda i, order: (i, 0)),
            full_spec((width, 3 * PAD)),
        ],
        out_specs=[
            full_spec(pieces.shape),
            pl.BlockSpec((step, 3 * PAD), lambda i, order: (i, 0)),
            full_spec((1, width)),
            full_spec((1, width)),
            full_spec((1, 3 * PAD)),
        ],
    )
    return pl.pallas_call(
        unproject_kernel,
        grid_spec=grid_spec,
        out_shape=[
            jax.ShapeDtypeStruct(pieces.shape, bf16),
            jax.ShapeDtypeStruct((rows, 3 * PAD), bf16),
            jax.ShapeDtypeStruct((1, width), f32),
            jax.ShapeDtypeStruct((1, width), f32),
            jax.ShapeDtypeStruct((1, 3 * PAD), f32),
        ],
        compiler_params=pltpu.CompilerParams(vmem_limit_bytes=vmem_cap),
        cost_estimate=pl.CostEstimate(
            flops=2 * rows * width * 3 * PAD, bytes_accessed=9 << 20, transcendentals=0
        ),
        name="unproject",
    )(order, pieces, pieces, pieces, pieces, dq, down, doth, weight)


def reduce_plane(value, bits, sends):
    for bit, send in zip(bits, sends):
        value = value.reshape(2, value.shape[0] // 2, value.shape[1])
        value = sum_low(row(value, bit), send(row(value, 1 - bit)))
    return value


def reduce_z(value, z):
    value = value.reshape(4, value.shape[0] // 4, value.shape[1])
    got = [send_z(row(value, (z + k) % 4), k) for k in (1, 2, 3)]
    return sum_low(row(value, z), *got)


def reduce_pair(left, right, where):
    z, y, x = where
    left = reduce_plane(left, (x, y), (send_x, send_y))
    right = reduce_plane(right, (y, x), (send_y, send_x))
    both = reduce_z(jnp.concatenate([left, right], axis=1), z)
    return both


def gather_pair(both, where):
    half = both.shape[1] // 2
    stack = jnp.stack([both] + [send_z(both, k) for k in (1, 2, 3)])
    left, right = stack[:, :, :half], stack[:, :, half:]
    left_y, left_x = send_y(left), send_x(left)
    right_x, right_y = send_x(right), send_y(right)
    return place_pair(
        (left, left_x, left_y, send_x(left_y)), (right, right_x, right_y, send_y(right_x)), where
    )


def place_kernel(where_ref, *refs):
    lefts, rights, out_ref = refs[:4], refs[4:8], refs[8]
    z, y, x = where_ref[0], where_ref[1], where_ref[2]
    rows, half = lefts[0].shape[1:]
    for index in range(4):
        part_x = x ^ (index & 1)
        part_y = y ^ (index >> 1)
        for k in range(4):
            block_z = (z - k) & 3
            at = pl.multiple_of(((part_x * 2 + part_y) * 4 + block_z) * rows, 8)
            out_ref[pl.ds(at, rows), :half] = lefts[index][k].astype(f32)
            at = pl.multiple_of(((part_y * 2 + part_x) * 4 + block_z) * rows, 8)
            out_ref[pl.ds(at, rows), half:] = rights[index][k].astype(f32)


def place_pair(lefts, rights, where):
    blocks, rows, half = lefts[0].shape
    shape = (16 * rows, 2 * half)
    return pl.pallas_call(
        place_kernel,
        grid_spec=pltpu.PrefetchScalarGridSpec(
            num_scalar_prefetch=1,
            grid=(1,),
            in_specs=[full_spec((blocks, rows, half))] * 8,
            out_specs=full_spec(shape),
        ),
        out_shape=jax.ShapeDtypeStruct(shape, f32),
        compiler_params=pltpu.CompilerParams(vmem_limit_bytes=vmem_cap),
        cost_estimate=pl.CostEstimate(
            flops=shape[0] * shape[1], bytes_accessed=6 * shape[0] * shape[1], transcendentals=0
        ),
        name="place",
    )(jnp.stack(where).astype(jnp.int32), *lefts, *rights)


def sum_everywhere(value):
    value = value + other_core(value)
    for send in (send_x, send_y):
        value = value + send(value)
    return value + send_z(value, 1) + send_z(value, 2) + send_z(value, 3)


def split_halves(value, w, axis):
    half = value.shape[axis] // 2
    own = lax.dynamic_slice_in_dim(value, w * half, half, axis)
    oth = lax.dynamic_slice_in_dim(value, (1 - w) * half, half, axis)
    return own, oth


def own_rows_sum(left, right, w):
    own, oth = split_halves(left, w, 1)
    got = other_core(dot(oth, right, ((0,), (0,))).astype(bf16))
    return (dot(own, right, ((0,), (0,))) + got.astype(f32)).astype(bf16)


def column_halves(value):
    half = value.shape[1] // 2
    return value[:, :half], value[:, half:]


def gelu_tanh(values):
    return (
        0.5
        * values
        * (1.0 + jnp.tanh(0.7978845608028654 * (values + 0.044715 * values * values * values)))
    )


def layer_norm(values, gain, shift):
    center = jnp.mean(values, axis=-1, keepdims=True)
    moved = values - center
    spread = jnp.mean(moved * moved, axis=-1, keepdims=True)
    return moved * lax.rsqrt(spread + 1e-05) * gain + shift


def norm_back(grad, rows, gain):
    normed, inverse = norm_parts(rows)
    scaled = grad * gain
    part = scaled - jnp.mean(scaled, axis=-1, keepdims=True)
    part = part - normed * jnp.mean(scaled * normed, axis=-1, keepdims=True)
    return inverse * part, normed


def by_owner(
    block_input, span_order, doc_lengths, ln1_gain, ln1_bias, w_qkv, qv_bias, w_out, out_bias,
    ln2_gain, ln2_bias, w_fc, fc_bias, w_proj, proj_bias, d_out,
):
    seq_group, seq_dev, width = block_input.shape
    seqs = 2 * seq_group
    span_rows = seq_dev // 2
    chips = span_order.shape[0]
    rows = chips * span_rows
    me = lax.axis_index("ctx")
    w = lax.axis_index("wt")
    z, y, x = me // 4, me // 2 % 2, me % 2
    where = (z, y, x)
    group = me % 4

    second = (row(span_order, me)[0] % 2) != w

    def take_spans(value):
        value = value.reshape(seq_group, 2, span_rows, width)
        keep = jnp.where(second, value[:, 1], value[:, 0])
        give = jnp.where(second, value[:, 0], value[:, 1])
        got = other_core(give)
        return jnp.where(
            w == 0, jnp.concatenate([keep, got], axis=0), jnp.concatenate([got, keep], axis=0)
        )

    def give_spans(value):
        low, high = value[:seq_group], value[seq_group:]
        keep = jnp.where(w == 0, low, high)
        got = other_core(jnp.where(w == 0, high, low))
        first = jnp.where(second, got, keep)
        last = jnp.where(second, keep, got)
        return jnp.concatenate([first, last], axis=1)

    tokens_low = take_spans(block_input)
    kept = [row(tokens_low, z)] + [send_z(row(tokens_low, (z + k) % 4), k) for k in (1, 2, 3)]
    left, right = jnp.stack(kept[:2]), jnp.stack(kept[2:])
    left = jnp.concatenate([left, send_x(left)], axis=0)
    right = jnp.concatenate([right, send_y(right)], axis=0)
    pieces = jnp.concatenate([left, send_y(left), right, send_x(right)], axis=0)
    cot_low = take_spans(d_out)

    chip_ids = jnp.arange(chips, dtype=jnp.int32)
    span_here = jnp.where(span_order[:, 0] % 2 == w, span_order[:, 0], span_order[:, 1]) // 2
    span_ids = jnp.arange(chips, dtype=jnp.int32)
    holder = jnp.sum(
        jnp.where(span_here[None, :] == span_ids[:, None], chip_ids[None, :], 0), axis=1
    ).astype(jnp.int32)
    back_z = (z - holder // 4) % 4
    flip_y = (y ^ (holder // 2 % 2)).astype(jnp.int32)
    flip_x = (x ^ (holder % 2)).astype(jnp.int32)
    order = jnp.where(
        back_z < 2, flip_y * 4 + flip_x * 2 + back_z, 8 + flip_x * 4 + flip_y * 2 + back_z - 2
    ).astype(jnp.int32)

    lengths_oth = other_core(doc_lengths)
    lengths = jnp.where(
        w == 0,
        jnp.concatenate([doc_lengths, lengths_oth], axis=0),
        jnp.concatenate([lengths_oth, doc_lengths], axis=0),
    )
    lengths = row(lengths, z)
    ends = jnp.cumsum(lengths)[:-1]
    ranks = jnp.arange(rows, dtype=jnp.int32)
    even_pos = 2 * span_rows * (ranks // span_rows) + ranks % span_rows
    own_pos = even_pos + span_rows * w
    oth_pos = even_pos + span_rows * (1 - w)
    starts = jnp.sum(
        jnp.where(own_pos[:, None] >= ends[None, :], lengths[None, :-1], 0), axis=1
    ).astype(jnp.int32)
    tiles = rows // TILE
    own_tiles = own_pos.reshape(tiles, TILE)
    start_tiles = starts.reshape(tiles, TILE)
    meta = jnp.stack([own_tiles, start_tiles], axis=1).astype(jnp.int32)
    kpos = jnp.broadcast_to(jnp.stack([own_pos, oth_pos])[:, :, None], (2, rows, TILE)).astype(jnp.int32)
    even_tiles = even_pos.reshape(tiles, TILE)
    low = jnp.sum(
        (even_tiles[None, :, -1] + span_rows < start_tiles[:, 0:1]).astype(jnp.int32), axis=1
    ).astype(jnp.int32)
    high = jnp.sum(
        (even_tiles[None, :, 0] <= own_tiles[:, -1:]).astype(jnp.int32), axis=1
    ).astype(jnp.int32)

    def join(own, axis=0):
        got = other_core(own)
        return jnp.where(
            w == 0,
            jnp.concatenate([own, got], axis=axis),
            jnp.concatenate([got, own], axis=axis),
        )

    feats = width // GROUPS

    def pad_cols(value, fill=0.0):
        return jnp.pad(value, [(0, 0)] * (value.ndim - 1) + [(0, PAD - feats)], constant_values=fill)

    columns = w_qkv.reshape(w_qkv.shape[0], 3, GROUPS, feats)
    columns = lax.dynamic_index_in_dim(columns, group, 2, keepdims=False)
    weight_in = join(pad_cols(columns).reshape(w_qkv.shape[0], 3 * PAD))
    small = jnp.concatenate(
        [ln1_gain, ln1_bias, qv_bias[0], qv_bias[1], out_bias, ln2_gain, ln2_bias, proj_bias, fc_bias]
    )
    small_oth = other_core(small)
    small_pair = jnp.where(w == 0, jnp.stack([small, small_oth]), jnp.stack([small_oth, small])).astype(f32)
    half = width // 2

    def vector(index, size=half):
        return small_pair[:, index * half : index * half + size].reshape(1, 2 * size)

    gain_one, shift_one, bias_q, bias_v, bias_out, gain_two, shift_two, bias_proj = (
        vector(i) for i in range(8)
    )
    bias_fc = vector(8, fc_bias.shape[0])
    bias_q = lax.dynamic_slice_in_dim(bias_q, group * feats, feats, 1)
    bias_v = lax.dynamic_slice_in_dim(bias_v, group * feats, feats, 1)
    ones_tail = (jnp.arange(PAD) == feats).astype(f32)[None, :]
    bias_in = jnp.concatenate(
        [pad_cols(bias_q), jnp.zeros((1, PAD), f32), pad_cols(bias_v) + ones_tail], axis=1
    )
    weight_out = lax.all_gather(w_out, "wt", axis=0, tiled=True)
    weight_fc = lax.all_gather(w_fc, "wt", axis=0, tiled=True)
    weight_proj = lax.all_gather(w_proj, "wt", axis=0, tiled=True)

    normed_one, query, kv_own = project(order, pieces, gain_one, shift_one, weight_in, bias_in)
    kv_oth = other_core(kv_own)
    attn, lse, attn_send = attend(low, high, holder, query, kv_own, kv_oth, kpos, meta, chips)
    attn_got = lax.all_to_all(attn_send, "ctx", 0, 0, tiled=True)
    attn_low = (
        attn_got.reshape(seqs, GROUPS, span_rows, feats)
        .transpose(0, 2, 1, 3)
        .reshape(seqs * span_rows, width)
    )

    tokens = tokens_low.reshape(seqs * span_rows, width).astype(f32)
    cotangent = cot_low.reshape(seqs * span_rows, width).astype(f32)
    branch = dot(attn_low, weight_out, ((1,), (0,))) + bias_out
    resid = tokens + branch_scale * branch
    normed_two = layer_norm(resid, gain_two, shift_two).astype(bf16)
    hidden = dot(normed_two, weight_fc, ((1,), (0,))) + bias_fc
    hidden_low = gelu_tanh(hidden).astype(bf16)
    d_mlp = (branch_scale * cotangent).astype(bf16)
    grad_proj = own_rows_sum(hidden_low, d_mlp, w)
    mlp = dot(hidden_low, weight_proj, ((1,), (0,))) + bias_proj
    block_out = (resid + branch_scale * mlp).astype(bf16)

    d_hidden = dot(d_mlp, weight_proj, ((1,), (1,)))
    gelu_unused, gelu_pull = jax.vjp(gelu_tanh, hidden)
    d_pre = gelu_pull(d_hidden)[0].astype(bf16)
    d_normed_two = dot(d_pre, weight_fc, ((1,), (1,)))
    d_part, unit_two = norm_back(d_normed_two, resid, gain_two)
    d_resid = cotangent + d_part
    d_branch = (branch_scale * d_resid).astype(bf16)
    d_attn = dot(d_branch, weight_out, ((1,), (1,))).astype(bf16)
    d_send = (
        d_attn.reshape(seqs, span_rows, GROUPS, feats)
        .transpose(0, 2, 1, 3)
        .reshape(chips, span_rows, feats)
    )
    d_got = lax.all_to_all(d_send, "ctx", 0, 0, tiled=True)
    grad_fc = own_rows_sum(normed_two, d_pre, w)
    grad_out = own_rows_sum(attn_low, d_branch, w)

    def total(value):
        return jnp.sum(value.astype(f32), axis=0)

    sums = jnp.concatenate(
        [
            total(d_branch),
            total(d_normed_two * unit_two),
            total(d_normed_two),
            total(d_mlp),
            total(d_pre),
        ]
    )
    sums = sum_everywhere(sums.reshape(-1, 128)).reshape(-1)

    grad_proj = gather_pair(reduce_pair(*column_halves(grad_proj), where), where)
    grad_fc = gather_pair(reduce_pair(*column_halves(grad_fc), where), where)
    grad_out = gather_pair(reduce_pair(*column_halves(grad_out), where), where)

    d_query, d_own, d_oth = attend_back(
        low, high, holder, query, kv_own, kv_oth, kpos, meta, d_got, attn, lse
    )
    d_recv = other_core(d_oth)
    d_pieces, d_qkv, part_gain, part_shift, part_bias = unproject(
        order, pieces, d_query, d_own, d_recv, weight_in
    )
    grad_in = own_rows_sum(normed_one, d_qkv, w)
    grad_in = jnp.concatenate([grad_in[:, PAD * i : PAD * i + feats] for i in range(3)], axis=1)
    shard = reduce_z(grad_in, z)
    shards = [shard] + [send_z(shard, k) for k in (1, 2, 3)]
    block = jnp.concatenate([row(jnp.stack(shards), (z - i) % 4) for i in range(4)], axis=0)
    top, bottom = block[: half // 2], block[half // 2 :]
    top_x, bottom_y = send_x(top), send_y(bottom)
    top_y, bottom_x = send_y(top), send_x(bottom)
    top_xy, bottom_xy = send_y(top_x), send_x(bottom_y)
    tops = jnp.stack([top, top_x, top_y, top_xy])
    bottoms = jnp.stack([bottom, bottom_x, bottom_y, bottom_xy])
    by_group = [
        jnp.concatenate([row(tops, group ^ g), row(bottoms, group ^ g)], axis=0) for g in range(GROUPS)
    ]
    grad_w_qkv = jnp.concatenate(
        [by_group[g][:, feats * i : feats * (i + 1)] for i in range(3) for g in range(GROUPS)], axis=1
    ).astype(f32)
    zeros = jnp.zeros((1, width), f32)
    parts = jnp.concatenate(
        [
            part_gain,
            part_shift,
            lax.dynamic_update_slice(zeros, part_bias[:, :feats], (0, group * feats)),
            lax.dynamic_update_slice(zeros, part_bias[:, 2 * PAD : 2 * PAD + feats], (0, group * feats)),
        ],
        axis=0,
    )
    parts = sum_everywhere(parts.reshape(-1, 128)).reshape(4, width)

    left, right = d_pieces[:8], d_pieces[8:]
    left = sum_low(left[:4], send_y(left[4:]))
    right = sum_low(right[:4], send_x(right[4:]))
    left = sum_low(left[:2], send_x(left[2:]))
    right = sum_low(right[:2], send_y(right[2:]))
    got = [left[0], send_z(left[1], 3), send_z(right[0], 2), send_z(right[1], 1)]
    got = jnp.stack(got)
    d_normed_one = jnp.stack([row(got, (s - z) % 4) for s in range(seqs)])
    d_normed_one = d_normed_one.reshape(seqs * span_rows, width).astype(f32)
    d_first, unused = norm_back(d_normed_one, tokens, gain_one)
    d_input = d_resid + d_first

    def mine(value, size=half):
        return lax.dynamic_slice_in_dim(value, w * size, size, 0)

    return (
        give_spans(block_out.reshape(seqs, span_rows, width)),
        give_spans(d_input.reshape(seqs, span_rows, width)),
        mine(parts[0]),
        mine(parts[1]),
        grad_w_qkv,
        jnp.stack([mine(parts[2]), mine(parts[3])]),
        grad_out,
        mine(sums[:width]),
        mine(sums[width : 2 * width]),
        mine(sums[2 * width : 3 * width]),
        grad_fc,
        mine(sums[4 * width :], fc_bias.shape[0]),
        grad_proj,
        mine(sums[3 * width : 4 * width]),
    )


def split_count(row_total, limit):
    pieces = 1
    while row_total % pieces != 0 or row_total // pieces > limit:
        pieces += 1
    return pieces


def row_positions(order_table, first_index, row_total, seq_dev, span_rows):
    rows_here = first_index + jnp.arange(row_total, dtype=jnp.int32)
    device_of = rows_here // seq_dev
    half_of = rows_here % seq_dev // span_rows
    slot_index = device_of * 2 + half_of
    flat_order = order_table.reshape(-1)
    table_slots = jnp.arange(flat_order.shape[0], dtype=jnp.int32)
    picked = jnp.sum(
        jnp.where(slot_index[:, None] == table_slots[None, :], flat_order[None, :], 0), axis=1
    )
    return picked * span_rows + rows_here % span_rows


def doc_of(positions, lengths_row):
    ends_at = jnp.cumsum(lengths_row)
    inner_ends = ends_at[:-1]
    return jnp.sum((positions[:, None] >= inner_ends[None, :]).astype(jnp.int32), axis=1)


def visible(query_pos, query_doc, key_pos, key_doc):
    causal = key_pos[None, None, :] <= query_pos[None, :, None]
    same_doc = key_doc[:, None, :] == query_doc[:, :, None]
    return (causal & same_doc)[:, :, None, :]


def per_device(
    block_input,
    span_order,
    doc_lengths,
    ln1_gain,
    ln1_bias,
    w_qkv,
    qv_bias,
    w_out,
    out_bias,
    ln2_gain,
    ln2_bias,
    w_fc,
    fc_bias,
    w_proj,
    proj_bias,
    d_out,
):
    seq_group, seq_dev, width = block_input.shape
    heads = HEADS
    head_dim = width // heads
    span_rows = seq_dev // 2
    score_scale = head_dim ** (-0.5)

    def docs_for(positions):
        return jax.vmap(doc_of, in_axes=(None, 0))(positions, doc_lengths)

    weights_all = (
        lax.all_gather(ln1_gain, "wt", axis=0, tiled=True),
        lax.all_gather(ln1_bias, "wt", axis=0, tiled=True),
        lax.all_gather(w_qkv, "wt", axis=0, tiled=True),
        lax.all_gather(qv_bias, "wt", axis=1, tiled=True),
        lax.all_gather(w_out, "wt", axis=0, tiled=True),
        lax.all_gather(out_bias, "wt", axis=0, tiled=True),
        lax.all_gather(ln2_gain, "wt", axis=0, tiled=True),
        lax.all_gather(ln2_bias, "wt", axis=0, tiled=True),
        lax.all_gather(w_fc, "wt", axis=0, tiled=True),
        lax.all_gather(fc_bias, "wt", axis=0, tiled=True),
        lax.all_gather(w_proj, "wt", axis=0, tiled=True),
        lax.all_gather(proj_bias, "wt", axis=0, tiled=True),
    )
    gain_one = weights_all[0].astype(jnp.float32)
    shift_one = weights_all[1].astype(jnp.float32)
    bias_pair = weights_all[3].astype(jnp.float32)
    bias_out = weights_all[5].astype(jnp.float32)
    gain_two = weights_all[6].astype(jnp.float32)
    shift_two = weights_all[7].astype(jnp.float32)
    bias_fc = weights_all[9].astype(jnp.float32)
    bias_proj = weights_all[11].astype(jnp.float32)
    me_ctx = lax.axis_index("ctx")
    local_pos = row_positions(span_order, me_ctx * seq_dev, seq_dev, seq_dev, span_rows)
    local_doc = docs_for(local_pos)
    tokens_in = block_input.astype(jnp.float32)
    normed_one = layer_norm(tokens_in, gain_one, shift_one).astype(jnp.bfloat16)
    qkv_bias = jnp.concatenate([bias_pair[0], jnp.zeros((width,), jnp.float32), bias_pair[1]])
    projected = (
        jnp.einsum("btd,de->bte", normed_one, weights_all[2], preferred_element_type=jnp.float32)
        + qkv_bias
    )
    projected_low = projected.astype(jnp.bfloat16)
    query_low = projected_low[..., :width]
    key_low = projected_low[..., width : 2 * width]
    value_low = projected_low[..., 2 * width :]
    query_heads = query_low.reshape(seq_group, seq_dev, heads, head_dim)
    key_heads = key_low.reshape(seq_group, seq_dev, heads, head_dim)
    value_heads = value_low.reshape(seq_group, seq_dev, heads, head_dim)
    start_state = (
        jnp.zeros((seq_group, seq_dev, heads, head_dim), jnp.float32),
        jnp.full((seq_group, seq_dev, heads), neg_large, jnp.float32),
        jnp.zeros((seq_group, seq_dev, heads), jnp.float32),
    )
    key_piece = lax.all_gather(key_low, "ctx", axis=1, tiled=True)
    value_piece = lax.all_gather(value_low, "ctx", axis=1, tiled=True)
    piece_rows = key_piece.shape[1]
    key_pos = row_positions(span_order, jnp.int32(0), piece_rows, seq_dev, span_rows)
    key_doc = docs_for(key_pos)
    block_rows = piece_rows // split_count(piece_rows, 1024)

    def one_block(block_index, running):
        acc_sum, run_max, run_total = running
        first_row = block_index * block_rows
        key_block = lax.dynamic_slice_in_dim(key_piece, first_row, block_rows, 1).reshape(
            seq_group, block_rows, heads, head_dim
        )
        value_block = lax.dynamic_slice_in_dim(value_piece, first_row, block_rows, 1).reshape(
            seq_group, block_rows, heads, head_dim
        )
        allowed = visible(
            local_pos,
            local_doc,
            lax.dynamic_slice_in_dim(key_pos, first_row, block_rows, 0),
            lax.dynamic_slice_in_dim(key_doc, first_row, block_rows, 1),
        )
        scores = (
            jnp.einsum(
                "bqhd,bkhd->bqhk", query_heads, key_block, preferred_element_type=jnp.float32
            )
            * score_scale
        )
        scores = jnp.where(allowed, scores, neg_large)
        new_max = jnp.maximum(run_max, jnp.max(scores, axis=-1))
        weights = jnp.where(allowed, jnp.exp(scores - new_max[..., None]), 0.0)
        rescale = jnp.exp(run_max - new_max)
        run_total = run_total * rescale + jnp.sum(weights, axis=-1)
        acc_sum = acc_sum * rescale[..., None] + jnp.einsum(
            "bqhk,bkhd->bqhd",
            weights.astype(jnp.bfloat16),
            value_block,
            preferred_element_type=jnp.float32,
        )
        return (acc_sum, new_max, run_total)

    acc_sum, run_max, run_total = lax.fori_loop(0, piece_rows // block_rows, one_block, start_state)
    attn_heads = acc_sum / run_total[..., None]
    log_total = run_max + jnp.log(run_total)
    attn_out = attn_heads.reshape(seq_group, seq_dev, width)
    attn_low = attn_out.astype(jnp.bfloat16)
    branch_pre = (
        jnp.einsum("btd,de->bte", attn_low, weights_all[4], preferred_element_type=jnp.float32)
        + bias_out
    )
    resid_one = tokens_in + branch_scale * branch_pre
    normed_two = layer_norm(resid_one, gain_two, shift_two).astype(jnp.bfloat16)
    hidden_pre = (
        jnp.einsum("btd,df->btf", normed_two, weights_all[8], preferred_element_type=jnp.float32)
        + bias_fc
    )
    hidden_low = gelu_tanh(hidden_pre).astype(jnp.bfloat16)
    mlp_pre = (
        jnp.einsum("btf,fd->btd", hidden_low, weights_all[10], preferred_element_type=jnp.float32)
        + bias_proj
    )
    block_out = (resid_one + branch_scale * mlp_pre).astype(jnp.bfloat16)
    weights_back = (
        lax.all_gather(ln1_gain, "wt", axis=0, tiled=True),
        lax.all_gather(ln1_bias, "wt", axis=0, tiled=True),
        lax.all_gather(w_qkv, "wt", axis=0, tiled=True),
        lax.all_gather(qv_bias, "wt", axis=1, tiled=True),
        lax.all_gather(w_out, "wt", axis=0, tiled=True),
        lax.all_gather(out_bias, "wt", axis=0, tiled=True),
        lax.all_gather(ln2_gain, "wt", axis=0, tiled=True),
        lax.all_gather(ln2_bias, "wt", axis=0, tiled=True),
        lax.all_gather(w_fc, "wt", axis=0, tiled=True),
        lax.all_gather(fc_bias, "wt", axis=0, tiled=True),
        lax.all_gather(w_proj, "wt", axis=0, tiled=True),
        lax.all_gather(proj_bias, "wt", axis=0, tiled=True),
    )
    back_gain_one = weights_back[0].astype(jnp.float32)
    back_shift_one = weights_back[1].astype(jnp.float32)
    back_gain_two = weights_back[6].astype(jnp.float32)
    back_shift_two = weights_back[7].astype(jnp.float32)
    cotangent = d_out.astype(jnp.float32)
    d_mlp = (branch_scale * cotangent).astype(jnp.bfloat16)
    grad_w_proj = jnp.einsum("btf,btd->fd", hidden_low, d_mlp, preferred_element_type=jnp.float32)
    grad_proj_bias = jnp.sum(d_mlp.astype(jnp.float32), axis=(0, 1))
    d_hidden = jnp.einsum(
        "btd,fd->btf", d_mlp, weights_back[10], preferred_element_type=jnp.float32
    )
    gelu_unused, gelu_pull = jax.vjp(gelu_tanh, hidden_pre)
    d_pre = gelu_pull(d_hidden)[0].astype(jnp.bfloat16)
    grad_w_fc = jnp.einsum("btd,btf->df", normed_two, d_pre, preferred_element_type=jnp.float32)
    grad_fc_bias = jnp.sum(d_pre.astype(jnp.float32), axis=(0, 1))
    d_normed_two = jnp.einsum(
        "btf,df->btd", d_pre, weights_back[8], preferred_element_type=jnp.float32
    )
    norm_unused, norm_pull = jax.vjp(layer_norm, resid_one, back_gain_two, back_shift_two)
    d_resid_part, grad_ln2_gain, grad_ln2_bias = norm_pull(d_normed_two)
    d_resid = cotangent + d_resid_part
    d_branch = (branch_scale * d_resid).astype(jnp.bfloat16)
    grad_w_out = jnp.einsum("btd,bte->de", attn_low, d_branch, preferred_element_type=jnp.float32)
    grad_out_bias = jnp.sum(d_branch.astype(jnp.float32), axis=(0, 1))
    d_attn_low = jnp.einsum(
        "bte,de->btd", d_branch, weights_back[4], preferred_element_type=jnp.float32
    ).astype(jnp.bfloat16)
    d_attn_heads = d_attn_low.reshape(seq_group, seq_dev, heads, head_dim)
    delta = jnp.sum(d_attn_heads.astype(jnp.float32) * attn_heads, axis=-1)
    fold_key_piece = lax.all_gather(key_low, "ctx", axis=1, tiled=True)
    fold_value_piece = lax.all_gather(value_low, "ctx", axis=1, tiled=True)
    piece_rows = fold_key_piece.shape[1]
    fold_key_pos = row_positions(span_order, jnp.int32(0), piece_rows, seq_dev, span_rows)
    fold_key_doc = docs_for(fold_key_pos)
    fold_block_rows = piece_rows // split_count(piece_rows, 1024)

    def one_block(block_index, grad_query):
        first_row = block_index * fold_block_rows
        key_block = lax.dynamic_slice_in_dim(fold_key_piece, first_row, fold_block_rows, 1).reshape(
            seq_group, fold_block_rows, heads, head_dim
        )
        value_block = lax.dynamic_slice_in_dim(
            fold_value_piece, first_row, fold_block_rows, 1
        ).reshape(seq_group, fold_block_rows, heads, head_dim)
        allowed = visible(
            local_pos,
            local_doc,
            lax.dynamic_slice_in_dim(fold_key_pos, first_row, fold_block_rows, 0),
            lax.dynamic_slice_in_dim(fold_key_doc, first_row, fold_block_rows, 1),
        )
        scores = (
            jnp.einsum(
                "bqhd,bkhd->bqhk", query_heads, key_block, preferred_element_type=jnp.float32
            )
            * score_scale
        )
        probs = jnp.where(allowed, jnp.exp(scores - log_total[..., None]), 0.0)
        d_probs = jnp.einsum(
            "bqhd,bkhd->bqhk", d_attn_heads, value_block, preferred_element_type=jnp.float32
        )
        d_scores = (probs * (d_probs - delta[..., None])).astype(jnp.bfloat16)
        return (
            grad_query
            + jnp.einsum("bqhk,bkhd->bqhd", d_scores, key_block, preferred_element_type=jnp.float32)
            * score_scale
        )

    grad_query = lax.fori_loop(
        0,
        piece_rows // fold_block_rows,
        one_block,
        jnp.zeros((seq_group, seq_dev, heads, head_dim), jnp.float32),
    )
    stats_all = (
        lax.all_gather(log_total, "ctx", axis=1, tiled=True),
        lax.all_gather(delta, "ctx", axis=1, tiled=True),
    )
    totals_every = stats_all[0]
    deltas_every = stats_all[1]

    def fold_keys(carried, received, first_index):
        query_piece, grad_piece = received
        piece_rows = query_piece.shape[1]
        query_pos = row_positions(span_order, first_index, piece_rows, seq_dev, span_rows)
        query_doc = docs_for(query_pos)
        block_rows = piece_rows // split_count(piece_rows, 1024)

        def one_block(block_index, running):
            grad_key, grad_value = running
            first_row = block_index * block_rows
            query_block = lax.dynamic_slice_in_dim(query_piece, first_row, block_rows, 1).reshape(
                seq_group, block_rows, heads, head_dim
            )
            grad_block = lax.dynamic_slice_in_dim(grad_piece, first_row, block_rows, 1).reshape(
                seq_group, block_rows, heads, head_dim
            )
            total_block = lax.dynamic_slice_in_dim(totals_every, first_row, block_rows, 1)
            delta_block = lax.dynamic_slice_in_dim(deltas_every, first_row, block_rows, 1)
            allowed = visible(
                lax.dynamic_slice_in_dim(query_pos, first_row, block_rows, 0),
                lax.dynamic_slice_in_dim(query_doc, first_row, block_rows, 1),
                local_pos,
                local_doc,
            )
            scores = (
                jnp.einsum(
                    "bqhd,bkhd->bqhk", query_block, key_heads, preferred_element_type=jnp.float32
                )
                * score_scale
            )
            probs = jnp.where(allowed, jnp.exp(scores - total_block[..., None]), 0.0)
            grad_value = grad_value + jnp.einsum(
                "bqhk,bqhd->bkhd",
                probs.astype(jnp.bfloat16),
                grad_block,
                preferred_element_type=jnp.float32,
            )
            d_probs = jnp.einsum(
                "bqhd,bkhd->bqhk", grad_block, value_heads, preferred_element_type=jnp.float32
            )
            d_scores = (probs * (d_probs - delta_block[..., None])).astype(jnp.bfloat16)
            grad_key = (
                grad_key
                + jnp.einsum(
                    "bqhk,bqhd->bkhd", d_scores, query_block, preferred_element_type=jnp.float32
                )
                * score_scale
            )
            return (grad_key, grad_value)

        return lax.fori_loop(0, piece_rows // block_rows, one_block, carried)

    zero_heads = jnp.zeros((seq_group, seq_dev, heads, head_dim), jnp.float32)
    grad_key, grad_value = fold_keys(
        (zero_heads, zero_heads),
        (
            lax.all_gather(query_low, "ctx", axis=1, tiled=True),
            lax.all_gather(d_attn_low, "ctx", axis=1, tiled=True),
        ),
        jnp.int32(0),
    )
    d_projected = jnp.concatenate(
        [
            grad_query.reshape(seq_group, seq_dev, width),
            grad_key.reshape(seq_group, seq_dev, width),
            grad_value.reshape(seq_group, seq_dev, width),
        ],
        axis=-1,
    ).astype(jnp.bfloat16)
    grad_w_qkv = jnp.einsum(
        "btd,bte->de", normed_one, d_projected, preferred_element_type=jnp.float32
    )
    column_sums = jnp.sum(d_projected.astype(jnp.float32), axis=(0, 1))
    grad_qv_bias = jnp.stack([column_sums[:width], column_sums[2 * width :]])
    d_normed_one = jnp.einsum(
        "bte,de->btd", d_projected, weights_back[2], preferred_element_type=jnp.float32
    )
    first_unused, first_pull = jax.vjp(layer_norm, tokens_in, back_gain_one, back_shift_one)
    d_input_part, grad_ln1_gain, grad_ln1_bias = first_pull(d_normed_one)
    d_input = d_resid + d_input_part
    shares = (
        lax.psum_scatter(
            grad_ln1_gain.astype(jnp.bfloat16), "wt", scatter_dimension=0, tiled=True
        ).astype(jnp.float32),
        lax.psum_scatter(
            grad_ln1_bias.astype(jnp.bfloat16), "wt", scatter_dimension=0, tiled=True
        ).astype(jnp.float32),
        lax.psum_scatter(
            grad_w_qkv.astype(jnp.bfloat16), "wt", scatter_dimension=0, tiled=True
        ).astype(jnp.float32),
        lax.psum_scatter(
            grad_qv_bias.astype(jnp.bfloat16), "wt", scatter_dimension=1, tiled=True
        ).astype(jnp.float32),
        lax.psum_scatter(
            grad_w_out.astype(jnp.bfloat16), "wt", scatter_dimension=0, tiled=True
        ).astype(jnp.float32),
        lax.psum_scatter(
            grad_out_bias.astype(jnp.bfloat16), "wt", scatter_dimension=0, tiled=True
        ).astype(jnp.float32),
        lax.psum_scatter(
            grad_ln2_gain.astype(jnp.bfloat16), "wt", scatter_dimension=0, tiled=True
        ).astype(jnp.float32),
        lax.psum_scatter(
            grad_ln2_bias.astype(jnp.bfloat16), "wt", scatter_dimension=0, tiled=True
        ).astype(jnp.float32),
        lax.psum_scatter(
            grad_w_fc.astype(jnp.bfloat16), "wt", scatter_dimension=0, tiled=True
        ).astype(jnp.float32),
        lax.psum_scatter(
            grad_fc_bias.astype(jnp.bfloat16), "wt", scatter_dimension=0, tiled=True
        ).astype(jnp.float32),
        lax.psum_scatter(
            grad_w_proj.astype(jnp.bfloat16), "wt", scatter_dimension=0, tiled=True
        ).astype(jnp.float32),
        lax.psum_scatter(
            grad_proj_bias.astype(jnp.bfloat16), "wt", scatter_dimension=0, tiled=True
        ).astype(jnp.float32),
    )
    totals = lax.psum(
        (
            shares[0],
            shares[1],
            shares[2],
            shares[3],
            shares[4],
            shares[5],
            shares[6],
            shares[7],
            shares[8],
            shares[9],
            shares[10],
            shares[11],
        ),
        "ctx",
    )
    return (
        block_out,
        d_input,
        totals[0],
        totals[1],
        totals[2],
        totals[3],
        totals[4],
        totals[5],
        totals[6],
        totals[7],
        totals[8],
        totals[9],
        totals[10],
        totals[11],
    )


def solution(mesh):
    placed = (
        P("wt", "ctx", None),
        P(),
        P("wt", None),
        P("wt"),
        P("wt"),
        P("wt", None),
        P(None, "wt"),
        P("wt", None),
        P("wt"),
        P("wt"),
        P("wt"),
        P("wt", None),
        P("wt"),
        P("wt", None),
        P("wt"),
        P("wt", "ctx", None),
    )
    fast = dict(mesh.shape) == {"ctx": 16, "wt": 2}
    return jax.shard_map(
        by_owner if fast else per_device,
        mesh=mesh,
        in_specs=placed,
        out_specs=(
            P("wt", "ctx", None),
            P("wt", "ctx", None),
            P("wt"),
            P("wt"),
            P("wt", None),
            P(None, "wt"),
            P("wt", None),
            P("wt"),
            P("wt"),
            P("wt"),
            P("wt", None),
            P("wt"),
            P("wt", None),
            P("wt"),
        ),
        check_vma=False,
    )
```

```python
import functools

import jax
import jax.numpy as jnp
from jax import lax
from jax.experimental import pallas as pl
from jax.experimental.pallas import tpu as pltpu
from jax.sharding import PartitionSpec as P

HEADS = 12

branch_scale = 0.14433756729740643
neg_large = -1e30
f32 = jnp.float32
bf16 = jnp.bfloat16
VMEM = pltpu.VMEM
vmem_cap = 56 << 20

GROUPS = 4
TILE = 128
PAD = 256
PACK = 640

pair = [(0, 1), (1, 0)]
flips = [[(i, i ^ flip) for i in range(16)] for flip in range(16)]


def z_shift(step):
    return [(i, (i // 4 + step) % 4 * 4 + i % 4) for i in range(16)]


def other_core(value):
    return lax.ppermute(value, "wt", pair)


def send_flip(value, flip):
    return lax.ppermute(value, "ctx", flips[flip])


def send_z(value, step):
    return lax.ppermute(value, "ctx", z_shift(step))


planes = [[4 * i + j for j in range(4)] for i in range(4)]


def swap_plane(value):
    return lax.all_to_all(value, "ctx", 0, 0, axis_index_groups=planes, tiled=True)


def row(value, index):
    return lax.dynamic_index_in_dim(value, index, 0, keepdims=False)


def sum_low(*terms):
    total = terms[0].astype(f32)
    for term in terms[1:]:
        total = total + term.astype(f32)
    return total.astype(bf16)


def after(value, *others):
    return lax.optimization_barrier((value,) + others)[0]


def work(micros):
    return pl.CostEstimate(flops=int(micros * 1e6), bytes_accessed=1 << 12, transcendentals=0)


def full_spec(shape):
    zeros = (0,) * len(shape)
    return pl.BlockSpec(shape, lambda *unused: zeros)


def dot(left, right, dims):
    return lax.dot_general(left, right, (dims, ((), ())), preferred_element_type=f32)


def norm_parts(rows):
    center = jnp.mean(rows, axis=-1, keepdims=True)
    moved = rows - center
    spread = jnp.mean(moved * moved, axis=-1, keepdims=True)
    inverse = lax.rsqrt(spread + 1e-05)
    return moved * inverse, inverse


def joined(own, oth, core):
    return jnp.concatenate([jnp.where(core == 0, own, oth), jnp.where(core == 0, oth, own)], axis=1)


def of_group(vector, group):
    picked = jnp.zeros((1, 192), f32)
    for g in range(GROUPS):
        picked = jnp.where(group == g, vector[:, 192 * g : 192 * (g + 1)], picked)
    return picked


def project_kernel(
    order_ref, where_ref, a_ref, b_ref, c_ref, d_ref, own_ref, oth_ref, small_own_ref, small_oth_ref,
    h_ref, q_ref, kv_ref, weight_ref,
):
    group, core = where_ref[1], where_ref[2]
    half = own_ref.shape[0]

    @pl.when(pl.program_id(0) == 0)
    def _():
        for source, at in ((own_ref, core), (oth_ref, 1 - core)):
            rows = pl.ds(pl.multiple_of(at * half, half), half)
            for i in range(3):
                window = source[:, 384 * i : 384 * (i + 1)].astype(f32)
                part = jnp.where(group % 2 == 0, window[:, :192], window[:, 192:])
                weight_ref[rows, PAD * i : PAD * (i + 1)] = jnp.concatenate(
                    [part, jnp.zeros((half, PAD - 192), f32)], axis=1
                ).astype(bf16)

    small = joined(small_own_ref[0:4, :], small_oth_ref[0:4, :], core)
    lane = lax.broadcasted_iota(jnp.int32, (1, PAD - 192), 1)
    none = jnp.zeros((1, PAD - 192), f32)
    bias = jnp.concatenate(
        [
            of_group(small[2:3], group), none, jnp.zeros((1, PAD), f32),
            of_group(small[3:4], group), (lane == 0).astype(f32),
        ],
        axis=1,
    )
    rows = jnp.concatenate([r[0].astype(f32) for r in (a_ref, b_ref, c_ref, d_ref)], axis=0)
    normed, unused = norm_parts(rows)
    low = (normed * small[0:1] + small[1:2]).astype(bf16)
    h_ref[...] = low
    out = dot(low, weight_ref[...], ((1,), (0,))) + bias
    q_ref[...] = (out[:, :PAD].astype(bf16) * 0.125).astype(bf16)
    kv_ref[...] = out[:, PAD:].astype(bf16)


def span_specs(span_rows, width):
    return [
        pl.BlockSpec((1, span_rows, width), lambda i, order, *unused, t=t: (order[4 * i + t], 0, 0))
        for t in range(4)
    ]


def project(order, where, pieces, own, oth, small_own, small_oth):
    spans, span_rows, width = pieces.shape
    rows = spans * span_rows
    step = 4 * span_rows
    grid_spec = pltpu.PrefetchScalarGridSpec(
        num_scalar_prefetch=2,
        grid=(spans // 4,),
        in_specs=span_specs(span_rows, width)
        + [full_spec(v.shape) for v in (own, oth, small_own, small_oth)],
        out_specs=[
            pl.BlockSpec((step, width), lambda i, *unused: (i, 0)),
            pl.BlockSpec((step, PAD), lambda i, *unused: (i, 0)),
            pl.BlockSpec((step, 2 * PAD), lambda i, *unused: (i, 0)),
            full_spec((width, 3 * PAD)),
        ],
    )
    return pl.pallas_call(
        project_kernel,
        grid_spec=grid_spec,
        out_shape=[
            jax.ShapeDtypeStruct((rows, width), bf16),
            jax.ShapeDtypeStruct((rows, PAD), bf16),
            jax.ShapeDtypeStruct((rows, 2 * PAD), bf16),
            jax.ShapeDtypeStruct((width, 3 * PAD), bf16),
        ],
        compiler_params=pltpu.CompilerParams(vmem_limit_bytes=vmem_cap),
        cost_estimate=work(6),
        name="project",
    )(order, where, pieces, pieces, pieces, pieces, own, oth, small_own, small_oth)


def pack_kernel(where_ref, gain_ref, shift_ref, bias_ref, *refs):
    sums, own_ref, oth_ref = refs[:5], refs[5], refs[6]
    group, core = where_ref[1], where_ref[2]
    half = own_ref.shape[1]

    def spread(part):
        none = jnp.zeros((1, 192), f32)
        return jnp.concatenate([jnp.where(group == g, part, none) for g in range(GROUPS)], axis=1)

    vectors = [
        gain_ref[...], shift_ref[...],
        spread(bias_ref[:, :192]), spread(bias_ref[:, 2 * PAD : 2 * PAD + 192]),
    ]
    vectors += [r[...] for r in sums[:4]]
    for index, vector in enumerate(vectors):
        low, high = vector[:, :half], vector[:, half:]
        own_ref[index : index + 1, :] = jnp.where(core == 0, low, high)
        oth_ref[index : index + 1, :] = jnp.where(core == 0, high, low)
    wide = sums[4][...]
    for index in range(4):
        low = wide[:, half * index : half * (index + 1)]
        high = wide[:, half * (index + 4) : half * (index + 5)]
        own_ref[8 + index : 9 + index, :] = jnp.where(core == 0, low, high)
        oth_ref[8 + index : 9 + index, :] = jnp.where(core == 0, high, low)


def pack(where, gain, shift, bias, sums):
    half = gain.shape[1] // 2
    return pl.pallas_call(
        pack_kernel,
        in_specs=[pl.BlockSpec(memory_space=pltpu.SMEM)]
        + [pl.BlockSpec(memory_space=pltpu.VMEM)] * 8,
        out_specs=[pl.BlockSpec(memory_space=pltpu.VMEM)] * 2,
        out_shape=[jax.ShapeDtypeStruct((12, half), f32)] * 2,
        cost_estimate=work(1),
        name="pack",
    )(where, gain, shift, bias, *sums)


def by_head(tile):
    lane = lax.broadcasted_iota(jnp.int32, tile.shape, 1)
    zero = jnp.zeros_like(tile)
    return jnp.concatenate(
        [jnp.where((lane >= 64 * h) & (lane < 64 * h + 64), tile, zero) for h in range(3)], axis=0
    )


def by_head_t(tile):
    flipped = tile.T
    feat = lax.broadcasted_iota(jnp.int32, flipped.shape, 0)
    zero = jnp.zeros_like(flipped)
    return jnp.concatenate(
        [jnp.where((feat >= 64 * h) & (feat < 64 * h + 64), flipped, zero) for h in range(3)], axis=1
    )


def tile_rows(index):
    return pl.ds(pl.multiple_of(index * TILE, TILE), TILE)


def tile_pair(plan_ref, i, step, tiles):
    first = plan_ref[0, i] + 2 * step
    beyond = jnp.where(first + 1 < plan_ref[1, i], 0, 1 << 20)
    second = jnp.minimum(first + 1, tiles - 1)
    return tile_rows(first), tile_rows(second), beyond


def pair_rows(own_ref, oth_ref, first, second, lanes):
    return jnp.concatenate(
        [own_ref[first, lanes], oth_ref[first, lanes], own_ref[second, lanes], oth_ref[second, lanes]],
        axis=0,
    )


def pair_columns(own_ref, oth_ref, first, second):
    return jnp.concatenate(
        [own_ref[:, first], oth_ref[:, first], own_ref[:, second], oth_ref[:, second]], axis=1
    )


def visible_pair(kpos_ref, first, second, beyond, meta):
    keys = jnp.concatenate(
        [
            kpos_ref[0, first, :],
            kpos_ref[1, first, :],
            kpos_ref[0, second, :] + beyond,
            kpos_ref[1, second, :] + beyond,
        ],
        axis=0,
    )
    keys = jnp.concatenate([keys, keys, keys], axis=1)
    return (keys <= meta[0:1, :]) & (keys >= meta[1:2, :])


def pairs_of(plan_ref, i):
    return (plan_ref[1, i] - plan_ref[0, i] + 1) // 2


def attend_kernel(
    plan_ref, q_ref, own_ref, oth_ref, kpos_ref, meta_ref,
    o_ref, lse_ref, out_ref,
    vown, voth, stack, acc, top, held,
):
    spans, span_rows, feats = out_ref.shape
    tiles = q_ref.shape[0] // TILE
    keys_step = 4 * TILE
    vown[...] = own_ref[:, PAD:].T
    voth[...] = oth_ref[:, PAD:].T

    def one_tile(i, carry):
        here = tile_rows(i)
        stack[...] = by_head_t(q_ref[here, :])
        meta = meta_ref[i]
        acc[...] = jnp.zeros_like(acc)
        top[...] = jnp.full_like(top, neg_large)

        def score(step, inner):
            first, second, beyond = tile_pair(plan_ref, i, step, tiles)
            keys = pair_rows(own_ref, oth_ref, first, second, slice(0, PAD))
            scores = dot(keys, stack[...], ((1,), (0,)))
            allowed = visible_pair(kpos_ref, first, second, beyond, meta)
            scores = jnp.where(allowed, scores, neg_large)
            held[pl.ds(pl.multiple_of(step * keys_step, keys_step), keys_step), :] = scores
            best = jnp.max(scores.reshape(keys_step // 8, 8, scores.shape[1]), axis=0)
            top[...] = jnp.maximum(top[...], best)
            return inner

        lax.fori_loop(0, pairs_of(plan_ref, i), score, 0)
        peak = jnp.max(top[...], axis=0, keepdims=True)

        def weigh(step, inner):
            first, second, unused = tile_pair(plan_ref, i, step, tiles)
            scores = held[pl.ds(pl.multiple_of(step * keys_step, keys_step), keys_step), :]
            probs = jnp.exp(scores - peak).astype(bf16)
            vals = pair_columns(vown, voth, first, second)
            acc[...] += dot(vals, probs, ((1,), (0,)))
            return inner

        lax.fori_loop(0, pairs_of(plan_ref, i), weigh, 0)
        total = acc[192:193, :]
        lse_ref[i] = peak + jnp.log(total)
        parts = [
            acc[64 * h : 64 * h + 64, TILE * h : TILE * h + TILE]
            / total[:, TILE * h : TILE * h + TILE]
            for h in range(3)
        ]
        heads_t = jnp.concatenate(parts + [jnp.zeros((64, TILE), f32)], axis=0)
        o_ref[here, :] = heads_t.T
        return carry

    lax.fori_loop(0, tiles, one_tile, 0)
    for a in range(spans):
        out_ref[plan_ref[2, a]] = o_ref[span_rows * a : span_rows * (a + 1), :feats].astype(bf16)


def attend(plan, q, own, oth, kpos, meta, spans):
    rows = q.shape[0]
    tiles = rows // TILE
    wide = 3 * TILE
    return pl.pallas_call(
        attend_kernel,
        in_specs=[pl.BlockSpec(memory_space=pltpu.SMEM)]
        + [pl.BlockSpec(memory_space=pltpu.VMEM)] * 5,
        out_specs=[pl.BlockSpec(memory_space=pltpu.VMEM)] * 3,
        out_shape=[
            jax.ShapeDtypeStruct((rows, PAD), f32),
            jax.ShapeDtypeStruct((tiles, 1, wide), f32),
            jax.ShapeDtypeStruct((spans, rows // spans, 192), bf16),
        ],
        scratch_shapes=[
            VMEM((PAD, rows), bf16),
            VMEM((PAD, rows), bf16),
            VMEM((PAD, wide), bf16),
            VMEM((PAD, wide), f32),
            VMEM((8, wide), f32),
            VMEM((2 * rows + 2 * TILE, wide), f32),
        ],
        compiler_params=pltpu.CompilerParams(vmem_limit_bytes=vmem_cap),
        cost_estimate=work(15),
        name="attend",
    )(plan, q, own, oth, kpos, meta)


def attend_back_kernel(
    plan_ref, q_ref, own_ref, oth_ref, kpos_ref, meta_ref, grad_ref, o_ref, lse_ref,
    dq_ref, down_ref, doth_ref,
    grads, kown, koth, acc_oth, stack, gstack, stack_t, gstack_t, dq_t,
):
    spans, span_rows, feats = grad_ref.shape
    tiles = q_ref.shape[0] // TILE
    kown[...] = own_ref[:, :PAD].T
    koth[...] = oth_ref[:, :PAD].T
    down_ref[...] = jnp.zeros_like(down_ref)
    acc_oth[...] = jnp.zeros_like(acc_oth)
    grads[:, 128:] = jnp.zeros((grads.shape[0], PAD - 128), f32)
    for a in range(spans):
        grads[span_rows * a : span_rows * (a + 1), :feats] = grad_ref[plan_ref[2, a]].astype(f32)

    def one_tile(i, carry):
        here = tile_rows(i)
        grad = grads[here, :]
        grad_low = grad.astype(bf16)
        stack[...] = by_head(q_ref[here, :])
        gstack[...] = by_head(grad_low)
        stack_t[...] = by_head_t(q_ref[here, :])
        gstack_t[...] = by_head_t(grad_low)
        product = (grad * o_ref[here, :]).T
        delta = jnp.concatenate(
            [jnp.sum(product[64 * h : 64 * h + 64], axis=0, keepdims=True) for h in range(3)], axis=1
        )
        lse = lse_ref[i]
        meta = meta_ref[i]
        dq_t[...] = jnp.zeros_like(dq_t)

        def one(step, inner):
            first, second, beyond = tile_pair(plan_ref, i, step, tiles)
            keys = pair_rows(own_ref, oth_ref, first, second, slice(0, PAD))
            vals = pair_rows(own_ref, oth_ref, first, second, slice(PAD, 2 * PAD))
            scores = dot(keys, stack_t[...], ((1,), (0,)))
            allowed = visible_pair(kpos_ref, first, second, beyond, meta)
            probs = jnp.where(allowed, jnp.exp(scores - lse), 0.0)
            d_probs = dot(vals, gstack_t[...], ((1,), (0,)))
            d_scores = (probs * (d_probs - delta)).astype(bf16)
            d_vals = dot(probs.astype(bf16), gstack[...], ((1,), (0,)))
            d_keys = dot(d_scores, stack[...], ((1,), (0,)))
            down_ref[first, :PAD] += d_keys[:TILE]
            down_ref[first, PAD:] += d_vals[:TILE]
            acc_oth[first, :PAD] += d_keys[TILE : 2 * TILE]
            acc_oth[first, PAD:] += d_vals[TILE : 2 * TILE]
            down_ref[second, :PAD] += d_keys[2 * TILE : 3 * TILE]
            down_ref[second, PAD:] += d_vals[2 * TILE : 3 * TILE]
            acc_oth[second, :PAD] += d_keys[3 * TILE :]
            acc_oth[second, PAD:] += d_vals[3 * TILE :]
            dq_t[...] += dot(pair_columns(kown, koth, first, second), d_scores, ((1,), (0,)))
            return inner

        lax.fori_loop(0, pairs_of(plan_ref, i), one, 0)
        parts = [dq_t[64 * h : 64 * h + 64, TILE * h : TILE * h + TILE] for h in range(3)]
        heads_t = jnp.concatenate(parts + [jnp.zeros((64, TILE), f32)], axis=0) * 0.125
        dq_ref[here, :] = heads_t.T.astype(bf16)
        return carry

    lax.fori_loop(0, tiles, one_tile, 0)
    doth_ref[...] = acc_oth[...].astype(bf16)


def attend_back(plan, q, own, oth, kpos, meta, grad, o, lse):
    rows = q.shape[0]
    wide = 3 * TILE
    return pl.pallas_call(
        attend_back_kernel,
        in_specs=[pl.BlockSpec(memory_space=pltpu.SMEM)]
        + [pl.BlockSpec(memory_space=pltpu.VMEM)] * 8,
        out_specs=[pl.BlockSpec(memory_space=pltpu.VMEM)] * 3,
        out_shape=[
            jax.ShapeDtypeStruct((rows, PAD), bf16),
            jax.ShapeDtypeStruct((rows, 2 * PAD), f32),
            jax.ShapeDtypeStruct((rows, 2 * PAD), bf16),
        ],
        scratch_shapes=[
            VMEM((rows, PAD), f32),
            VMEM((PAD, rows), bf16),
            VMEM((PAD, rows), bf16),
            VMEM((rows, 2 * PAD), f32),
            VMEM((wide, PAD), bf16),
            VMEM((wide, PAD), bf16),
            VMEM((PAD, wide), bf16),
            VMEM((PAD, wide), bf16),
            VMEM((PAD, wide), f32),
        ],
        compiler_params=pltpu.CompilerParams(vmem_limit_bytes=vmem_cap),
        cost_estimate=work(24),
        name="attend_back",
    )(plan, q, own, oth, kpos, meta, grad, o, lse)


def unproject_kernel(
    order_ref, place_ref, a_ref, b_ref, c_ref, d_ref, dq_ref, down_ref, doth_ref, weight_ref,
    pieces_ref, grad_ref, gain_ref, shift_ref, bias_ref,
):
    i = pl.program_id(0)
    span_rows = a_ref.shape[1]

    @pl.when(i == 0)
    def _():
        gain_ref[...] = jnp.zeros_like(gain_ref)
        shift_ref[...] = jnp.zeros_like(shift_ref)
        bias_ref[...] = jnp.zeros_like(bias_ref)

    rows = jnp.concatenate([r[0].astype(f32) for r in (a_ref, b_ref, c_ref, d_ref)], axis=0)
    normed, unused = norm_parts(rows)
    dkv = (down_ref[...] + doth_ref[...].astype(f32)).astype(bf16)
    grad = jnp.concatenate([dq_ref[...], dkv], axis=1)
    grad_ref[...] = jnp.concatenate(
        [grad[:, :192], grad[:, PAD : PAD + 192], grad[:, 2 * PAD : 2 * PAD + 192], grad[:, 192:PAD]],
        axis=1,
    )
    bias_ref[...] += jnp.sum(grad.astype(f32), axis=0, keepdims=True)
    back = dot(grad, weight_ref[...], ((1,), (1,)))
    gain_ref[...] += jnp.sum(back * normed, axis=0, keepdims=True)
    shift_ref[...] += jnp.sum(back, axis=0, keepdims=True)
    for t in range(4):
        pieces_ref[place_ref[4 * i + t]] = back[span_rows * t : span_rows * (t + 1)].astype(bf16)


def unproject(order, place, pieces, dq, down, doth, weight):
    spans, span_rows, width = pieces.shape
    rows = spans * span_rows
    step = 4 * span_rows
    grid_spec = pltpu.PrefetchScalarGridSpec(
        num_scalar_prefetch=2,
        grid=(spans // 4,),
        in_specs=span_specs(span_rows, width)
        + [
            pl.BlockSpec((step, PAD), lambda i, *unused: (i, 0)),
            pl.BlockSpec((step, 2 * PAD), lambda i, *unused: (i, 0)),
            pl.BlockSpec((step, 2 * PAD), lambda i, *unused: (i, 0)),
            full_spec((width, 3 * PAD)),
        ],
        out_specs=[
            full_spec(pieces.shape),
            pl.BlockSpec((step, PACK), lambda i, *unused: (i, 0)),
            full_spec((1, width)),
            full_spec((1, width)),
            full_spec((1, 3 * PAD)),
        ],
    )
    return pl.pallas_call(
        unproject_kernel,
        grid_spec=grid_spec,
        out_shape=[
            jax.ShapeDtypeStruct(pieces.shape, bf16),
            jax.ShapeDtypeStruct((rows, PACK), bf16),
            jax.ShapeDtypeStruct((1, width), f32),
            jax.ShapeDtypeStruct((1, width), f32),
            jax.ShapeDtypeStruct((1, 3 * PAD), f32),
        ],
        compiler_params=pltpu.CompilerParams(vmem_limit_bytes=vmem_cap),
        cost_estimate=work(8),
        name="unproject",
    )(order, place, pieces, pieces, pieces, pieces, dq, down, doth, weight)


def halve(value, bit):
    value = value.reshape(2, value.shape[0] // 2, value.shape[1])
    return row(value, bit), row(value, 1 - bit)


def reduce_z(value, z):
    value = value.reshape(4, value.shape[0] // 4, value.shape[1])
    return row(value, z), [row(value, (z + k) % 4) for k in (1, 2, 3)]


def over_z(sends):
    return [send_z(sends[k - 1], k) for k in (1, 2, 3)]


def reduce_plane(value, group):
    value = value.reshape(4, value.shape[0] // 4, value.shape[1])
    return row(value, group), [row(value, group ^ f) for f in (1, 2, 3)]


def over_plane(sends):
    return [send_flip(sends[f - 1], f) for f in (1, 2, 3)]


def gather_z(value):
    pair = jnp.stack([value, send_flip(value, 8)])
    return jnp.concatenate([pair, send_flip(pair, 4)], axis=0)


def spread_once(left, right):
    return jnp.concatenate([left, send_flip(left, 1)], axis=0), jnp.concatenate(
        [right, send_flip(right, 2)], axis=0
    )


def spread_twice(left, right):
    return left, send_flip(left, 2), right, send_flip(right, 1)


def cut_lanes(value, at):
    return value[:, :, :at], value[:, :, at:]


def entry(refs, side, f, k):
    if side == 0:
        return refs[f // 2][4 * (f % 2) + k].astype(f32)
    return refs[2 + f % 2][4 * (f // 2) + k].astype(f32)


def block_of(z, k):
    return ((z & 1) ^ (k >> 1)) * 2 + ((z >> 1) ^ (k & 1))


def chip_of(z, k):
    return z ^ ((k >> 1) + 2 * (k & 1))


def place_proj_kernel(where_ref, *refs):
    parts, out_ref = refs[:4], refs[4]
    z, group = where_ref[0], where_ref[1]
    rows, half = parts[0].shape[1:]
    for f in range(4):
        x, y = (group ^ f) & 1, (group ^ f) >> 1
        for k in range(4):
            at = ((2 * x + y) * 4 + block_of(z, k)) * rows
            out_ref[pl.ds(pl.multiple_of(at, 8), rows), :half] = entry(parts, 0, f, k)
            at = ((2 * y + x) * 4 + block_of(z, k)) * rows
            out_ref[pl.ds(pl.multiple_of(at, 8), rows), half:] = entry(parts, 1, f, k)


def place_rest_kernel(where_ref, *refs):
    parts, fc_ref, out_ref = refs[:4], refs[4], refs[5]
    z, group = where_ref[0], where_ref[1]
    rows, half = parts[0].shape[1:]
    fc_wide = fc_ref.shape[1]
    for f in range(4):
        for k in range(4):
            at = ((group ^ f) * 4 + chip_of(z, k)) * rows
            at = pl.ds(pl.multiple_of(at, 8), rows)
            fc_ref[at, :half] = entry(parts, 0, f, k)
            right = entry(parts, 1, f, k)
            fc_ref[at, half:] = right[:, : fc_wide - half]
            out_ref[at, :] = right[:, fc_wide - half :]


def place_in_kernel(where_ref, *refs):
    parts, in_ref, small_ref, held = refs[:4], refs[4], refs[5], refs[6]
    z, group = where_ref[0], where_ref[1]
    upper = parts[0].shape[1]
    rows = upper + parts[2].shape[1] - 8
    small_ref[...] = jnp.zeros(small_ref.shape, f32)
    for f in range(4):
        for k in range(4):
            block = block_of(z, k)
            held[group ^ f, block, :upper] = entry(parts, 0, f, k)
            right = entry(parts, 1, f, k)
            held[group ^ f, block, upper:rows] = right[:-8]
            small_ref[block] = small_ref[block] + right[-8:]
    for block in range(4):
        for i in range(3):
            at = 192 * i
            columns = [held[g, block, :, at : at + 192] for g in range(4)]
            in_ref[rows * block : rows * (block + 1), 768 * i : 768 * (i + 1)] = jnp.concatenate(
                columns, axis=1
            )


def place(kernel, name, micros, where, parts, shapes, scratch=()):
    return pl.pallas_call(
        kernel,
        in_specs=[pl.BlockSpec(memory_space=pltpu.SMEM)]
        + [pl.BlockSpec(memory_space=pltpu.VMEM)] * len(parts),
        out_specs=[pl.BlockSpec(memory_space=pltpu.VMEM)] * len(shapes),
        out_shape=[jax.ShapeDtypeStruct(shape, f32) for shape in shapes],
        scratch_shapes=list(scratch),
        compiler_params=pltpu.CompilerParams(vmem_limit_bytes=vmem_cap),
        cost_estimate=work(micros),
        name=name,
    )(where, *parts)


def split_halves(value, w, axis):
    low, high = jnp.split(value, 2, axis)
    return jnp.where(w == 0, low, high), jnp.where(w == 0, high, low)


def grad_dot(left, right):
    return dot(left, right, ((0,), (0,)))


def gelu_tanh(values):
    return (
        0.5
        * values
        * (1.0 + jnp.tanh(0.7978845608028654 * (values + 0.044715 * values * values * values)))
    )


def layer_norm(values, gain, shift):
    center = jnp.mean(values, axis=-1, keepdims=True)
    moved = values - center
    spread = jnp.mean(moved * moved, axis=-1, keepdims=True)
    return moved * lax.rsqrt(spread + 1e-05) * gain + shift


def norm_back(grad, rows, gain):
    normed, inverse = norm_parts(rows)
    scaled = grad * gain
    part = scaled - jnp.mean(scaled, axis=-1, keepdims=True)
    part = part - normed * jnp.mean(scaled * normed, axis=-1, keepdims=True)
    return inverse * part, normed


def by_owner(
    block_input, span_order, doc_lengths, ln1_gain, ln1_bias, w_qkv, qv_bias, w_out, out_bias,
    ln2_gain, ln2_bias, w_fc, fc_bias, w_proj, proj_bias, d_out,
):
    seq_group, seq_dev, width = block_input.shape
    seqs = 2 * seq_group
    span_rows = seq_dev // 2
    chips = span_order.shape[0]
    rows = chips * span_rows
    me = lax.axis_index("ctx")
    w = lax.axis_index("wt")
    z, y, x = me // 4, me // 2 % 2, me % 2
    where = (z, y, x)
    group = me % 4

    second = (row(span_order, me)[0] % 2) != w

    def take_spans(value):
        value = value.reshape(seq_group, 2, span_rows, width)
        keep = jnp.where(second, value[:, 1], value[:, 0])
        give = jnp.where(second, value[:, 0], value[:, 1])
        got = other_core(give)
        return jnp.where(
            w == 0, jnp.concatenate([keep, got], axis=0), jnp.concatenate([got, keep], axis=0)
        )

    def give_spans(value):
        low, high = value[:seq_group], value[seq_group:]
        keep = jnp.where(w == 0, low, high)
        got = other_core(jnp.where(w == 0, high, low))
        first = jnp.where(second, got, keep)
        last = jnp.where(second, keep, got)
        return jnp.concatenate([first, last], axis=1)

    def to_sequence(value):
        got = [send_z(row(value, (z + k) % 4), k) for k in (1, 2, 3)]
        return [row(value, z)] + got

    def from_sequence(value):
        got = [value[0]] + [send_z(value[k], 4 - k) for k in (1, 2, 3)]
        got = jnp.stack(got)
        return jnp.stack([row(got, (s - z) % 4) for s in range(seqs)])

    kept = to_sequence(take_spans(block_input))
    left, right = jnp.stack(kept[:2]), jnp.stack(kept[2:])
    tokens_low = jnp.concatenate([left, right], axis=0)
    span_order, doc_lengths, unused = lax.optimization_barrier((span_order, doc_lengths, (left, right)))
    left = jnp.concatenate([left, send_flip(left, 1)], axis=0)
    right = jnp.concatenate([right, send_flip(right, 2)], axis=0)
    pieces = jnp.concatenate([left, send_flip(left, 2), right, send_flip(right, 1)], axis=0)
    ln1_gain, ln1_bias, w_qkv, qv_bias, d_out, unused = lax.optimization_barrier(
        (ln1_gain, ln1_bias, w_qkv, qv_bias, d_out, (left, right))
    )
    cot_low = jnp.stack(to_sequence(take_spans(d_out)))

    chip_ids = jnp.arange(chips, dtype=jnp.int32)
    span_here = jnp.where(span_order[:, 0] % 2 == w, span_order[:, 0], span_order[:, 1]) // 2
    span_ids = jnp.arange(chips, dtype=jnp.int32)
    holder = jnp.sum(
        jnp.where(span_here[None, :] == span_ids[:, None], chip_ids[None, :], 0), axis=1
    ).astype(jnp.int32)
    back_z = (z - holder // 4) % 4
    flip = group ^ (holder % 4)
    order = jnp.where(
        back_z < 2,
        (flip // 2) * 4 + (flip % 2) * 2 + back_z,
        8 + (flip % 2) * 4 + (flip // 2) * 2 + back_z - 2,
    ).astype(jnp.int32)
    order_back = (flip * 4 + back_z).astype(jnp.int32)
    owner = (holder % 4 * 4 + back_z).astype(jnp.int32)

    lengths_oth = other_core(doc_lengths)
    lengths = jnp.where(
        w == 0,
        jnp.concatenate([doc_lengths, lengths_oth], axis=0),
        jnp.concatenate([lengths_oth, doc_lengths], axis=0),
    )
    lengths = row(lengths, z)
    ends = jnp.cumsum(lengths)[:-1]
    ranks = jnp.arange(rows, dtype=jnp.int32)
    even_pos = 2 * span_rows * (ranks // span_rows) + ranks % span_rows
    own_pos = even_pos + span_rows * w
    oth_pos = even_pos + span_rows * (1 - w)
    starts = jnp.sum(
        jnp.where(own_pos[:, None] >= ends[None, :], lengths[None, :-1], 0), axis=1
    ).astype(jnp.int32)
    tiles = rows // TILE
    own_tiles = own_pos.reshape(tiles, TILE)
    start_tiles = starts.reshape(tiles, TILE)
    meta = jnp.tile(jnp.stack([own_tiles, start_tiles], axis=1), (1, 1, 3)).astype(jnp.int32)
    kpos = jnp.broadcast_to(jnp.stack([own_pos, oth_pos])[:, :, None], (2, rows, TILE)).astype(jnp.int32)
    even_tiles = even_pos.reshape(tiles, TILE)
    low = jnp.sum(
        (even_tiles[None, :, -1] + span_rows < start_tiles[:, 0:1]).astype(jnp.int32), axis=1
    ).astype(jnp.int32)
    high = jnp.sum(
        (even_tiles[None, :, 0] <= own_tiles[:, -1:]).astype(jnp.int32), axis=1
    ).astype(jnp.int32)

    room = jnp.zeros((chips - tiles,), jnp.int32)
    plan = jnp.stack([jnp.concatenate([low, room]), jnp.concatenate([high, room]), owner])

    feats = width // GROUPS
    half = width // 2
    here = jnp.stack([z, group, w]).astype(jnp.int32)
    in_own = jnp.concatenate(
        [
            lax.dynamic_slice_in_dim(w_qkv, width * i + half * (group // 2), half, 1)
            for i in range(3)
        ],
        axis=1,
    )
    in_oth_core = other_core(in_own)
    def rows_of(*vectors):
        return jnp.concatenate([v.astype(f32).reshape(-1, half) for v in vectors], axis=0)

    small = rows_of(ln1_gain, ln1_bias, qv_bias[0], qv_bias[1])
    small_oth = other_core(small)
    weight_out = lax.all_gather(w_out, "wt", axis=0, tiled=True)
    weight_fc = lax.all_gather(w_fc, "wt", axis=0, tiled=True)
    weight_proj = lax.all_gather(w_proj, "wt", axis=0, tiled=True)

    pieces = after(pieces, kpos, meta, plan, in_oth_core, small_oth, cot_low)
    normed_one, query, kv_own, weight_in = project(
        order, here, pieces, in_own, in_oth_core, small, small_oth
    )
    kv_oth = other_core(kv_own)
    attn, lse, attn_send = attend(plan, query, kv_own, kv_oth, kpos, meta, chips)
    attn_got = swap_plane(attn_send.reshape(GROUPS, seqs, span_rows, feats))

    later = (ln1_gain, out_bias, ln2_gain, ln2_bias, proj_bias, fc_bias)
    later = rows_of(*lax.optimization_barrier(later + (attn_send,))[:-1])
    later_oth = other_core(later)
    later_pair = jnp.where(w == 0, jnp.stack([later, later_oth]), jnp.stack([later_oth, later]))

    def vector(index, count=1):
        return later_pair[:, index : index + count].reshape(1, 2 * count * half)

    gain_one, bias_out, gain_two, shift_two, bias_proj = (vector(i) for i in range(5))
    bias_fc = vector(5, fc_bias.shape[0] // half)
    cotangent = after(cot_low, attn_send).reshape(seqs * span_rows, width).astype(f32)
    d_mlp = (branch_scale * cotangent).astype(bf16)
    mlp_both = jnp.concatenate([d_mlp, other_core(d_mlp)], axis=0)
    d_hidden = dot(d_mlp, weight_proj, ((1,), (1,)))
    attn_got = after(attn_got, d_hidden, later_pair, mlp_both)
    attn_low = (
        attn_got.transpose(1, 2, 0, 3)
        .reshape(seqs * span_rows, width)
    )

    tokens = tokens_low.reshape(seqs * span_rows, width).astype(f32)
    branch = dot(attn_low, weight_out, ((1,), (0,))) + bias_out
    resid = tokens + branch_scale * branch
    normed_two = layer_norm(resid, gain_two, shift_two).astype(bf16)
    hidden = dot(normed_two, weight_fc, ((1,), (0,))) + bias_fc
    hidden_low = gelu_tanh(hidden).astype(bf16)
    gelu_unused, gelu_pull = jax.vjp(gelu_tanh, hidden)
    d_pre = gelu_pull(d_hidden)[0].astype(bf16)
    hidden_own, hidden_oth = split_halves(hidden_low, w, 1)
    hidden_both = jnp.concatenate([hidden_own, other_core(hidden_oth)], axis=0)
    pre_both = jnp.concatenate([d_pre, other_core(d_pre)], axis=0)
    normed_own, normed_oth = split_halves(normed_two, w, 1)
    normed_both = jnp.concatenate([normed_own, other_core(normed_oth)], axis=0)
    attn_own, attn_oth = split_halves(attn_low, w, 1)
    attn_both = jnp.concatenate([attn_own, other_core(attn_oth)], axis=0)
    d_normed_two = dot(d_pre, weight_fc, ((1,), (1,)))
    d_part, unit_two = norm_back(d_normed_two, resid, gain_two)
    d_resid = cotangent + d_part
    d_branch = (branch_scale * d_resid).astype(bf16)
    d_attn = dot(d_branch, weight_out, ((1,), (1,))).astype(bf16)
    d_send = (
        d_attn.reshape(seqs, span_rows, GROUPS, feats)
        .transpose(2, 0, 1, 3)
    )
    d_got = swap_plane(d_send).reshape(chips, span_rows, feats)

    low_bit, high_bit = z % 2, z // 2
    branch_both = jnp.concatenate([d_branch, other_core(d_branch)], axis=0)
    hidden_both = after(hidden_both, d_send)
    grad_proj = grad_dot(hidden_both, mlp_both).astype(bf16)
    proj_left, left_send = halve(grad_proj[:, :half], x)
    proj_right, right_send = halve(grad_proj[:, half:], y)
    left_recv, right_recv = send_flip(left_send, 1), send_flip(right_send, 2)
    normed_both, attn_both, d_got, unused = lax.optimization_barrier(
        (normed_both, attn_both, d_got, (left_send, right_send))
    )
    fc_cols = d_pre.shape[1]
    grad_rest = jnp.concatenate(
        [grad_dot(normed_both, pre_both).astype(bf16), grad_dot(attn_both, branch_both).astype(bf16)],
        axis=1,
    )
    rest_keep, rest_sends = reduce_plane(grad_rest, group)
    left_recv, right_recv, unused = lax.optimization_barrier((left_recv, right_recv, rest_sends))
    proj_left, left_send = halve(sum_low(proj_left, left_recv), y)
    proj_right, right_send = halve(sum_low(proj_right, right_recv), x)
    left_recv, right_recv = send_flip(left_send, 2), send_flip(right_send, 1)
    rest_plane = over_plane(rest_sends)

    def total(value):
        return jnp.sum(value.astype(f32), axis=0, keepdims=True)

    sums = [
        total(d_branch),
        total(d_normed_two * unit_two),
        total(d_normed_two),
        total(d_mlp),
        total(d_pre),
    ]

    d_got = after(d_got, left_send, right_send, *rest_sends)
    d_query, d_own, d_oth = attend_back(plan, query, kv_own, kv_oth, kpos, meta, d_got, attn, lse)
    left_recv, right_recv, rest_plane, d_query, d_oth = lax.optimization_barrier(
        (left_recv, right_recv, rest_plane, d_query, d_oth)
    )
    d_recv = other_core(d_oth)
    grad_proj = jnp.concatenate(
        [sum_low(proj_left, left_recv), sum_low(proj_right, right_recv)], axis=1
    )
    proj_keep, proj_send = halve(grad_proj, low_bit)
    proj_recv = send_flip(proj_send, 4)
    rest_keep, rest_sends = reduce_z(sum_low(rest_keep, *rest_plane), z)
    proj_recv, d_recv, rest_sends = lax.optimization_barrier((proj_recv, d_recv, rest_sends))
    rest_z = over_z(rest_sends)
    proj_keep, proj_send = halve(sum_low(proj_keep, proj_recv), high_bit)
    proj_recv = send_flip(proj_send, 8)
    d_recv = after(d_recv, proj_send)
    d_pieces, d_qkv, part_gain, part_shift, part_bias = unproject(
        order, order_back, pieces, d_query, d_own, d_recv, weight_in
    )
    proj_recv, rest_z, d_pieces, d_qkv = lax.optimization_barrier((proj_recv, rest_z, d_pieces, d_qkv))

    normed_own, normed_oth = split_halves(normed_one, w, 1)
    in_oth = grad_dot(normed_oth, d_qkv).astype(bf16)
    in_got = other_core(in_oth)
    d_pieces, unused = lax.optimization_barrier((d_pieces, in_oth))
    back_sends = [d_pieces[4 * f : 4 * f + 4] for f in (1, 2, 3)]
    back = over_plane(back_sends)
    small_own, small_oth = pack(here, part_gain, part_shift, part_bias, sums)
    small_rows = (small_own + other_core(small_oth)).astype(bf16).reshape(4, 3, half)
    small_rows = jnp.pad(small_rows, ((0, 0), (0, 5), (0, PACK - half)))
    normed_own = after(normed_own, back_sends)
    grad_in = (grad_dot(normed_own, d_qkv) + in_got.astype(f32)).astype(bf16)
    grad_in = jnp.concatenate([grad_in.reshape(4, half // 4, PACK), small_rows], axis=1)
    in_keep, in_send = halve(grad_in.reshape(-1, PACK), low_bit)
    in_recv = send_flip(in_send, 4)
    proj_recv, rest_z, unused = lax.optimization_barrier((proj_recv, rest_z, in_send))
    proj_shard = sum_low(proj_keep, proj_recv)
    rest_shard = sum_low(rest_keep, *rest_z)
    proj_pair = jnp.stack([proj_shard, send_flip(proj_shard, 8)])
    rest_pair = jnp.stack([rest_shard, send_flip(rest_shard, 8)])
    back, in_recv, proj_pair, rest_pair = lax.optimization_barrier((back, in_recv, proj_pair, rest_pair))
    in_keep, in_send = halve(sum_low(in_keep, in_recv), high_bit)
    in_recv = send_flip(in_send, 8)
    proj_all = jnp.concatenate([proj_pair, send_flip(proj_pair, 4)], axis=0)
    rest_all = jnp.concatenate([rest_pair, send_flip(rest_pair, 4)], axis=0)
    proj_all, in_recv = lax.optimization_barrier((proj_all, in_recv))
    in_shard = sum_low(in_keep, in_recv)
    in_pair = jnp.stack([in_shard, send_flip(in_shard, 8)])
    proj_left, proj_right = cut_lanes(proj_all, half)
    proj_left2, proj_right2 = spread_once(proj_left, proj_right)
    rest_all, in_pair, proj_left2, proj_right2 = lax.optimization_barrier(
        (rest_all, in_pair, proj_left2, proj_right2)
    )
    proj_parts = spread_twice(proj_left2, proj_right2)
    mlp = dot(after(hidden_low, proj_left2, proj_right2), weight_proj, ((1,), (0,))) + bias_proj
    block_out = (resid + branch_scale * mlp).astype(bf16)
    in_all = jnp.concatenate([in_pair, send_flip(in_pair, 4)], axis=0)
    rest_left, rest_right = cut_lanes(rest_all, rest_all.shape[2] // 2)
    rest_left2, rest_right2 = spread_once(rest_left, rest_right)
    proj_parts, rest_left2, rest_right2, in_all = lax.optimization_barrier(
        (proj_parts, rest_left2, rest_right2, in_all)
    )
    rest_parts = spread_twice(rest_left2, rest_right2)
    in_parts = spread_once(in_all[:, :56], in_all[:, 56:])
    rest_parts, in_parts = lax.optimization_barrier((rest_parts, in_parts))
    in_parts = spread_twice(*in_parts)
    (grad_proj,) = place(
        place_proj_kernel, "place_proj", 5, here, proj_parts, [(fc_cols // 2, width)]
    )
    grad_fc, grad_out = place(
        place_rest_kernel, "place_rest", 5, here, rest_parts, [(half, fc_cols), (half, width)]
    )
    grad_w_qkv, small_all = place(
        place_in_kernel, "place_in", 4, here, in_parts,
        [(half, 3 * width), (4, 8, PACK)],
        [VMEM((4, 4, half // 4, PACK), f32)],
    )

    d_normed_one = sum_low(d_pieces[:4], *back).reshape(seqs * span_rows, width).astype(f32)
    d_first, unused = norm_back(d_normed_one, tokens, gain_one)
    d_input = (d_resid + d_first).reshape(seqs, span_rows, width)
    d_input = from_sequence(d_input.astype(bf16))

    def piece(index):
        return small_all[index // 3, index % 3, :half]

    return (
        give_spans(from_sequence(block_out.reshape(seqs, span_rows, width))),
        give_spans(d_input).astype(f32),
        piece(0),
        piece(1),
        grad_w_qkv,
        jnp.stack([piece(2), piece(3)]),
        grad_out,
        piece(4),
        piece(5),
        piece(6),
        grad_fc,
        jnp.concatenate([piece(8), piece(9), piece(10), piece(11)]),
        grad_proj,
        piece(7),
    )


def split_count(row_total, limit):
    pieces = 1
    while row_total % pieces != 0 or row_total // pieces > limit:
        pieces += 1
    return pieces


def row_positions(order_table, first_index, row_total, seq_dev, span_rows):
    rows_here = first_index + jnp.arange(row_total, dtype=jnp.int32)
    device_of = rows_here // seq_dev
    half_of = rows_here % seq_dev // span_rows
    slot_index = device_of * 2 + half_of
    flat_order = order_table.reshape(-1)
    table_slots = jnp.arange(flat_order.shape[0], dtype=jnp.int32)
    picked = jnp.sum(
        jnp.where(slot_index[:, None] == table_slots[None, :], flat_order[None, :], 0), axis=1
    )
    return picked * span_rows + rows_here % span_rows


def doc_of(positions, lengths_row):
    ends_at = jnp.cumsum(lengths_row)
    inner_ends = ends_at[:-1]
    return jnp.sum((positions[:, None] >= inner_ends[None, :]).astype(jnp.int32), axis=1)


def visible(query_pos, query_doc, key_pos, key_doc):
    causal = key_pos[None, None, :] <= query_pos[None, :, None]
    same_doc = key_doc[:, None, :] == query_doc[:, :, None]
    return (causal & same_doc)[:, :, None, :]


def per_device(
    block_input,
    span_order,
    doc_lengths,
    ln1_gain,
    ln1_bias,
    w_qkv,
    qv_bias,
    w_out,
    out_bias,
    ln2_gain,
    ln2_bias,
    w_fc,
    fc_bias,
    w_proj,
    proj_bias,
    d_out,
):
    seq_group, seq_dev, width = block_input.shape
    heads = HEADS
    head_dim = width // heads
    span_rows = seq_dev // 2
    score_scale = head_dim ** (-0.5)

    def docs_for(positions):
        return jax.vmap(doc_of, in_axes=(None, 0))(positions, doc_lengths)

    weights_all = (
        lax.all_gather(ln1_gain, "wt", axis=0, tiled=True),
        lax.all_gather(ln1_bias, "wt", axis=0, tiled=True),
        lax.all_gather(w_qkv, "wt", axis=0, tiled=True),
        lax.all_gather(qv_bias, "wt", axis=1, tiled=True),
        lax.all_gather(w_out, "wt", axis=0, tiled=True),
        lax.all_gather(out_bias, "wt", axis=0, tiled=True),
        lax.all_gather(ln2_gain, "wt", axis=0, tiled=True),
        lax.all_gather(ln2_bias, "wt", axis=0, tiled=True),
        lax.all_gather(w_fc, "wt", axis=0, tiled=True),
        lax.all_gather(fc_bias, "wt", axis=0, tiled=True),
        lax.all_gather(w_proj, "wt", axis=0, tiled=True),
        lax.all_gather(proj_bias, "wt", axis=0, tiled=True),
    )
    gain_one = weights_all[0].astype(jnp.float32)
    shift_one = weights_all[1].astype(jnp.float32)
    bias_pair = weights_all[3].astype(jnp.float32)
    bias_out = weights_all[5].astype(jnp.float32)
    gain_two = weights_all[6].astype(jnp.float32)
    shift_two = weights_all[7].astype(jnp.float32)
    bias_fc = weights_all[9].astype(jnp.float32)
    bias_proj = weights_all[11].astype(jnp.float32)
    me_ctx = lax.axis_index("ctx")
    local_pos = row_positions(span_order, me_ctx * seq_dev, seq_dev, seq_dev, span_rows)
    local_doc = docs_for(local_pos)
    tokens_in = block_input.astype(jnp.float32)
    normed_one = layer_norm(tokens_in, gain_one, shift_one).astype(jnp.bfloat16)
    qkv_bias = jnp.concatenate([bias_pair[0], jnp.zeros((width,), jnp.float32), bias_pair[1]])
    projected = (
        jnp.einsum("btd,de->bte", normed_one, weights_all[2], preferred_element_type=jnp.float32)
        + qkv_bias
    )
    projected_low = projected.astype(jnp.bfloat16)
    query_low = projected_low[..., :width]
    key_low = projected_low[..., width : 2 * width]
    value_low = projected_low[..., 2 * width :]
    query_heads = query_low.reshape(seq_group, seq_dev, heads, head_dim)
    key_heads = key_low.reshape(seq_group, seq_dev, heads, head_dim)
    value_heads = value_low.reshape(seq_group, seq_dev, heads, head_dim)
    start_state = (
        jnp.zeros((seq_group, seq_dev, heads, head_dim), jnp.float32),
        jnp.full((seq_group, seq_dev, heads), neg_large, jnp.float32),
        jnp.zeros((seq_group, seq_dev, heads), jnp.float32),
    )
    key_piece = lax.all_gather(key_low, "ctx", axis=1, tiled=True)
    value_piece = lax.all_gather(value_low, "ctx", axis=1, tiled=True)
    piece_rows = key_piece.shape[1]
    key_pos = row_positions(span_order, jnp.int32(0), piece_rows, seq_dev, span_rows)
    key_doc = docs_for(key_pos)
    block_rows = piece_rows // split_count(piece_rows, 1024)

    def one_block(block_index, running):
        acc_sum, run_max, run_total = running
        first_row = block_index * block_rows
        key_block = lax.dynamic_slice_in_dim(key_piece, first_row, block_rows, 1).reshape(
            seq_group, block_rows, heads, head_dim
        )
        value_block = lax.dynamic_slice_in_dim(value_piece, first_row, block_rows, 1).reshape(
            seq_group, block_rows, heads, head_dim
        )
        allowed = visible(
            local_pos,
            local_doc,
            lax.dynamic_slice_in_dim(key_pos, first_row, block_rows, 0),
            lax.dynamic_slice_in_dim(key_doc, first_row, block_rows, 1),
        )
        scores = (
            jnp.einsum(
                "bqhd,bkhd->bqhk", query_heads, key_block, preferred_element_type=jnp.float32
            )
            * score_scale
        )
        scores = jnp.where(allowed, scores, neg_large)
        new_max = jnp.maximum(run_max, jnp.max(scores, axis=-1))
        weights = jnp.where(allowed, jnp.exp(scores - new_max[..., None]), 0.0)
        rescale = jnp.exp(run_max - new_max)
        run_total = run_total * rescale + jnp.sum(weights, axis=-1)
        acc_sum = acc_sum * rescale[..., None] + jnp.einsum(
            "bqhk,bkhd->bqhd",
            weights.astype(jnp.bfloat16),
            value_block,
            preferred_element_type=jnp.float32,
        )
        return (acc_sum, new_max, run_total)

    acc_sum, run_max, run_total = lax.fori_loop(0, piece_rows // block_rows, one_block, start_state)
    attn_heads = acc_sum / run_total[..., None]
    log_total = run_max + jnp.log(run_total)
    attn_out = attn_heads.reshape(seq_group, seq_dev, width)
    attn_low = attn_out.astype(jnp.bfloat16)
    branch_pre = (
        jnp.einsum("btd,de->bte", attn_low, weights_all[4], preferred_element_type=jnp.float32)
        + bias_out
    )
    resid_one = tokens_in + branch_scale * branch_pre
    normed_two = layer_norm(resid_one, gain_two, shift_two).astype(jnp.bfloat16)
    hidden_pre = (
        jnp.einsum("btd,df->btf", normed_two, weights_all[8], preferred_element_type=jnp.float32)
        + bias_fc
    )
    hidden_low = gelu_tanh(hidden_pre).astype(jnp.bfloat16)
    mlp_pre = (
        jnp.einsum("btf,fd->btd", hidden_low, weights_all[10], preferred_element_type=jnp.float32)
        + bias_proj
    )
    block_out = (resid_one + branch_scale * mlp_pre).astype(jnp.bfloat16)
    weights_back = (
        lax.all_gather(ln1_gain, "wt", axis=0, tiled=True),
        lax.all_gather(ln1_bias, "wt", axis=0, tiled=True),
        lax.all_gather(w_qkv, "wt", axis=0, tiled=True),
        lax.all_gather(qv_bias, "wt", axis=1, tiled=True),
        lax.all_gather(w_out, "wt", axis=0, tiled=True),
        lax.all_gather(out_bias, "wt", axis=0, tiled=True),
        lax.all_gather(ln2_gain, "wt", axis=0, tiled=True),
        lax.all_gather(ln2_bias, "wt", axis=0, tiled=True),
        lax.all_gather(w_fc, "wt", axis=0, tiled=True),
        lax.all_gather(fc_bias, "wt", axis=0, tiled=True),
        lax.all_gather(w_proj, "wt", axis=0, tiled=True),
        lax.all_gather(proj_bias, "wt", axis=0, tiled=True),
    )
    back_gain_one = weights_back[0].astype(jnp.float32)
    back_shift_one = weights_back[1].astype(jnp.float32)
    back_gain_two = weights_back[6].astype(jnp.float32)
    back_shift_two = weights_back[7].astype(jnp.float32)
    cotangent = d_out.astype(jnp.float32)
    d_mlp = (branch_scale * cotangent).astype(jnp.bfloat16)
    grad_w_proj = jnp.einsum("btf,btd->fd", hidden_low, d_mlp, preferred_element_type=jnp.float32)
    grad_proj_bias = jnp.sum(d_mlp.astype(jnp.float32), axis=(0, 1))
    d_hidden = jnp.einsum(
        "btd,fd->btf", d_mlp, weights_back[10], preferred_element_type=jnp.float32
    )
    gelu_unused, gelu_pull = jax.vjp(gelu_tanh, hidden_pre)
    d_pre = gelu_pull(d_hidden)[0].astype(jnp.bfloat16)
    grad_w_fc = jnp.einsum("btd,btf->df", normed_two, d_pre, preferred_element_type=jnp.float32)
    grad_fc_bias = jnp.sum(d_pre.astype(jnp.float32), axis=(0, 1))
    d_normed_two = jnp.einsum(
        "btf,df->btd", d_pre, weights_back[8], preferred_element_type=jnp.float32
    )
    norm_unused, norm_pull = jax.vjp(layer_norm, resid_one, back_gain_two, back_shift_two)
    d_resid_part, grad_ln2_gain, grad_ln2_bias = norm_pull(d_normed_two)
    d_resid = cotangent + d_resid_part
    d_branch = (branch_scale * d_resid).astype(jnp.bfloat16)
    grad_w_out = jnp.einsum("btd,bte->de", attn_low, d_branch, preferred_element_type=jnp.float32)
    grad_out_bias = jnp.sum(d_branch.astype(jnp.float32), axis=(0, 1))
    d_attn_low = jnp.einsum(
        "bte,de->btd", d_branch, weights_back[4], preferred_element_type=jnp.float32
    ).astype(jnp.bfloat16)
    d_attn_heads = d_attn_low.reshape(seq_group, seq_dev, heads, head_dim)
    delta = jnp.sum(d_attn_heads.astype(jnp.float32) * attn_heads, axis=-1)
    fold_key_piece = lax.all_gather(key_low, "ctx", axis=1, tiled=True)
    fold_value_piece = lax.all_gather(value_low, "ctx", axis=1, tiled=True)
    piece_rows = fold_key_piece.shape[1]
    fold_key_pos = row_positions(span_order, jnp.int32(0), piece_rows, seq_dev, span_rows)
    fold_key_doc = docs_for(fold_key_pos)
    fold_block_rows = piece_rows // split_count(piece_rows, 1024)

    def one_block(block_index, grad_query):
        first_row = block_index * fold_block_rows
        key_block = lax.dynamic_slice_in_dim(fold_key_piece, first_row, fold_block_rows, 1).reshape(
            seq_group, fold_block_rows, heads, head_dim
        )
        value_block = lax.dynamic_slice_in_dim(
            fold_value_piece, first_row, fold_block_rows, 1
        ).reshape(seq_group, fold_block_rows, heads, head_dim)
        allowed = visible(
            local_pos,
            local_doc,
            lax.dynamic_slice_in_dim(fold_key_pos, first_row, fold_block_rows, 0),
            lax.dynamic_slice_in_dim(fold_key_doc, first_row, fold_block_rows, 1),
        )
        scores = (
            jnp.einsum(
                "bqhd,bkhd->bqhk", query_heads, key_block, preferred_element_type=jnp.float32
            )
            * score_scale
        )
        probs = jnp.where(allowed, jnp.exp(scores - log_total[..., None]), 0.0)
        d_probs = jnp.einsum(
            "bqhd,bkhd->bqhk", d_attn_heads, value_block, preferred_element_type=jnp.float32
        )
        d_scores = (probs * (d_probs - delta[..., None])).astype(jnp.bfloat16)
        return (
            grad_query
            + jnp.einsum("bqhk,bkhd->bqhd", d_scores, key_block, preferred_element_type=jnp.float32)
            * score_scale
        )

    grad_query = lax.fori_loop(
        0,
        piece_rows // fold_block_rows,
        one_block,
        jnp.zeros((seq_group, seq_dev, heads, head_dim), jnp.float32),
    )
    stats_all = (
        lax.all_gather(log_total, "ctx", axis=1, tiled=True),
        lax.all_gather(delta, "ctx", axis=1, tiled=True),
    )
    totals_every = stats_all[0]
    deltas_every = stats_all[1]

    def fold_keys(carried, received, first_index):
        query_piece, grad_piece = received
        piece_rows = query_piece.shape[1]
        query_pos = row_positions(span_order, first_index, piece_rows, seq_dev, span_rows)
        query_doc = docs_for(query_pos)
        block_rows = piece_rows // split_count(piece_rows, 1024)

        def one_block(block_index, running):
            grad_key, grad_value = running
            first_row = block_index * block_rows
            query_block = lax.dynamic_slice_in_dim(query_piece, first_row, block_rows, 1).reshape(
                seq_group, block_rows, heads, head_dim
            )
            grad_block = lax.dynamic_slice_in_dim(grad_piece, first_row, block_rows, 1).reshape(
                seq_group, block_rows, heads, head_dim
            )
            total_block = lax.dynamic_slice_in_dim(totals_every, first_row, block_rows, 1)
            delta_block = lax.dynamic_slice_in_dim(deltas_every, first_row, block_rows, 1)
            allowed = visible(
                lax.dynamic_slice_in_dim(query_pos, first_row, block_rows, 0),
                lax.dynamic_slice_in_dim(query_doc, first_row, block_rows, 1),
                local_pos,
                local_doc,
            )
            scores = (
                jnp.einsum(
                    "bqhd,bkhd->bqhk", query_block, key_heads, preferred_element_type=jnp.float32
                )
                * score_scale
            )
            probs = jnp.where(allowed, jnp.exp(scores - total_block[..., None]), 0.0)
            grad_value = grad_value + jnp.einsum(
                "bqhk,bqhd->bkhd",
                probs.astype(jnp.bfloat16),
                grad_block,
                preferred_element_type=jnp.float32,
            )
            d_probs = jnp.einsum(
                "bqhd,bkhd->bqhk", grad_block, value_heads, preferred_element_type=jnp.float32
            )
            d_scores = (probs * (d_probs - delta_block[..., None])).astype(jnp.bfloat16)
            grad_key = (
                grad_key
                + jnp.einsum(
                    "bqhk,bqhd->bkhd", d_scores, query_block, preferred_element_type=jnp.float32
                )
                * score_scale
            )
            return (grad_key, grad_value)

        return lax.fori_loop(0, piece_rows // block_rows, one_block, carried)

    zero_heads = jnp.zeros((seq_group, seq_dev, heads, head_dim), jnp.float32)
    grad_key, grad_value = fold_keys(
        (zero_heads, zero_heads),
        (
            lax.all_gather(query_low, "ctx", axis=1, tiled=True),
            lax.all_gather(d_attn_low, "ctx", axis=1, tiled=True),
        ),
        jnp.int32(0),
    )
    d_projected = jnp.concatenate(
        [
            grad_query.reshape(seq_group, seq_dev, width),
            grad_key.reshape(seq_group, seq_dev, width),
            grad_value.reshape(seq_group, seq_dev, width),
        ],
        axis=-1,
    ).astype(jnp.bfloat16)
    grad_w_qkv = jnp.einsum(
        "btd,bte->de", normed_one, d_projected, preferred_element_type=jnp.float32
    )
    column_sums = jnp.sum(d_projected.astype(jnp.float32), axis=(0, 1))
    grad_qv_bias = jnp.stack([column_sums[:width], column_sums[2 * width :]])
    d_normed_one = jnp.einsum(
        "bte,de->btd", d_projected, weights_back[2], preferred_element_type=jnp.float32
    )
    first_unused, first_pull = jax.vjp(layer_norm, tokens_in, back_gain_one, back_shift_one)
    d_input_part, grad_ln1_gain, grad_ln1_bias = first_pull(d_normed_one)
    d_input = d_resid + d_input_part
    shares = (
        lax.psum_scatter(
            grad_ln1_gain.astype(jnp.bfloat16), "wt", scatter_dimension=0, tiled=True
        ).astype(jnp.float32),
        lax.psum_scatter(
            grad_ln1_bias.astype(jnp.bfloat16), "wt", scatter_dimension=0, tiled=True
        ).astype(jnp.float32),
        lax.psum_scatter(
            grad_w_qkv.astype(jnp.bfloat16), "wt", scatter_dimension=0, tiled=True
        ).astype(jnp.float32),
        lax.psum_scatter(
            grad_qv_bias.astype(jnp.bfloat16), "wt", scatter_dimension=1, tiled=True
        ).astype(jnp.float32),
        lax.psum_scatter(
            grad_w_out.astype(jnp.bfloat16), "wt", scatter_dimension=0, tiled=True
        ).astype(jnp.float32),
        lax.psum_scatter(
            grad_out_bias.astype(jnp.bfloat16), "wt", scatter_dimension=0, tiled=True
        ).astype(jnp.float32),
        lax.psum_scatter(
            grad_ln2_gain.astype(jnp.bfloat16), "wt", scatter_dimension=0, tiled=True
        ).astype(jnp.float32),
        lax.psum_scatter(
            grad_ln2_bias.astype(jnp.bfloat16), "wt", scatter_dimension=0, tiled=True
        ).astype(jnp.float32),
        lax.psum_scatter(
            grad_w_fc.astype(jnp.bfloat16), "wt", scatter_dimension=0, tiled=True
        ).astype(jnp.float32),
        lax.psum_scatter(
            grad_fc_bias.astype(jnp.bfloat16), "wt", scatter_dimension=0, tiled=True
        ).astype(jnp.float32),
        lax.psum_scatter(
            grad_w_proj.astype(jnp.bfloat16), "wt", scatter_dimension=0, tiled=True
        ).astype(jnp.float32),
        lax.psum_scatter(
            grad_proj_bias.astype(jnp.bfloat16), "wt", scatter_dimension=0, tiled=True
        ).astype(jnp.float32),
    )
    totals = lax.psum(
        (
            shares[0],
            shares[1],
            shares[2],
            shares[3],
            shares[4],
            shares[5],
            shares[6],
            shares[7],
            shares[8],
            shares[9],
            shares[10],
            shares[11],
        ),
        "ctx",
    )
    return (
        block_out,
        d_input,
        totals[0],
        totals[1],
        totals[2],
        totals[3],
        totals[4],
        totals[5],
        totals[6],
        totals[7],
        totals[8],
        totals[9],
        totals[10],
        totals[11],
    )


def solution(mesh):
    placed = (
        P("wt", "ctx", None),
        P(),
        P("wt", None),
        P("wt"),
        P("wt"),
        P("wt", None),
        P(None, "wt"),
        P("wt", None),
        P("wt"),
        P("wt"),
        P("wt"),
        P("wt", None),
        P("wt"),
        P("wt", None),
        P("wt"),
        P("wt", "ctx", None),
    )
    fast = dict(mesh.shape) == {"ctx": 16, "wt": 2}
    return jax.shard_map(
        by_owner if fast else per_device,
        mesh=mesh,
        in_specs=placed,
        out_specs=(
            P("wt", "ctx", None),
            P("wt", "ctx", None),
            P("wt"),
            P("wt"),
            P("wt", None),
            P(None, "wt"),
            P("wt", None),
            P("wt"),
            P("wt"),
            P("wt"),
            P("wt", None),
            P("wt"),
            P("wt", None),
            P("wt"),
        ),
        check_vma=False,
    )
```

```python
import functools

import jax
import jax.numpy as jnp
from jax import lax
from jax.experimental import pallas as pl
from jax.experimental.pallas import tpu as pltpu
from jax.sharding import PartitionSpec as P

HEADS = 12

branch_scale = 0.14433756729740643
neg_large = -1e30
f32 = jnp.float32
bf16 = jnp.bfloat16
VMEM = pltpu.VMEM
vmem_cap = 56 << 20

GROUPS = 4
TILE = 128
PAD = 256
PACK = 640

pair = [(0, 1), (1, 0)]
flips = [[(i, i ^ flip) for i in range(16)] for flip in range(16)]


def z_shift(step):
    return [(i, (i // 4 + step) % 4 * 4 + i % 4) for i in range(16)]


def other_core(value):
    return lax.ppermute(value, "wt", pair)


def send_flip(value, flip):
    return lax.ppermute(value, "ctx", flips[flip])


def send_z(value, step):
    return lax.ppermute(value, "ctx", z_shift(step))


planes = [[4 * i + j for j in range(4)] for i in range(4)]


def swap_plane(value):
    return lax.all_to_all(value, "ctx", 0, 0, axis_index_groups=planes, tiled=True)


def row(value, index):
    return lax.dynamic_index_in_dim(value, index, 0, keepdims=False)


def sum_low(*terms):
    total = terms[0].astype(f32)
    for term in terms[1:]:
        total = total + term.astype(f32)
    return total.astype(bf16)


def after(value, *others):
    return lax.optimization_barrier((value,) + others)[0]


def work(micros):
    return pl.CostEstimate(flops=int(micros * 1e6), bytes_accessed=1 << 12, transcendentals=0)


def busy(micros):
    return pl.CostEstimate(flops=int(micros * 1.1e9), bytes_accessed=1 << 20, transcendentals=0)


def full_spec(shape):
    zeros = (0,) * len(shape)
    return pl.BlockSpec(shape, lambda *unused: zeros)


def dot(left, right, dims):
    return lax.dot_general(left, right, (dims, ((), ())), preferred_element_type=f32)


def norm_parts(rows):
    center = jnp.mean(rows, axis=-1, keepdims=True)
    moved = rows - center
    spread = jnp.mean(moved * moved, axis=-1, keepdims=True)
    inverse = lax.rsqrt(spread + 1e-05)
    return moved * inverse, inverse


def joined(own, oth, core):
    return jnp.concatenate([jnp.where(core == 0, own, oth), jnp.where(core == 0, oth, own)], axis=1)


def of_group(vector, group):
    picked = jnp.zeros((1, 192), f32)
    for g in range(GROUPS):
        picked = jnp.where(group == g, vector[:, 192 * g : 192 * (g + 1)], picked)
    return picked


def project_kernel(
    order_ref, where_ref, a_ref, b_ref, c_ref, d_ref, own_ref, oth_ref, small_own_ref, small_oth_ref,
    x_ref, h_ref, q_ref, kv_ref, weight_ref,
    held,
):
    group, core = where_ref[1], where_ref[2]
    half = own_ref.shape[0]
    for source, at in ((own_ref, core), (oth_ref, 1 - core)):
        rows = pl.ds(pl.multiple_of(at * half, half), half)
        for i in range(3):
            window = source[:, 384 * i : 384 * (i + 1)].astype(f32)
            part = jnp.where(group % 2 == 0, window[:, :192], window[:, 192:])
            weight_ref[rows, PAD * i : PAD * (i + 1)] = jnp.concatenate(
                [part, jnp.zeros((half, PAD - 192), f32)], axis=1
            ).astype(bf16)
    for index, source in enumerate((a_ref, b_ref, c_ref, d_ref)):
        held[4 * index : 4 * index + 4] = source[...]

    small = joined(small_own_ref[0:4, :], small_oth_ref[0:4, :], core)
    lane = lax.broadcasted_iota(jnp.int32, (1, PAD - 192), 1)
    none = jnp.zeros((1, PAD - 192), f32)
    bias = jnp.concatenate(
        [
            of_group(small[2:3], group), none, jnp.zeros((1, PAD), f32),
            of_group(small[3:4], group), (lane == 0).astype(f32),
        ],
        axis=1,
    )
    step = 4 * held.shape[1]
    for i in range(4):
        at = slice(step * i, step * (i + 1))
        rows = jnp.concatenate([held[order_ref[4 * i + t]].astype(f32) for t in range(4)], axis=0)
        x_ref[at, :] = rows.astype(bf16)
        normed, unused = norm_parts(rows)
        low = (normed * small[0:1] + small[1:2]).astype(bf16)
        h_ref[at, :] = low
        out = dot(low, weight_ref[...], ((1,), (0,))) + bias
        q_ref[at, :] = (out[:, :PAD].astype(bf16) * 0.125).astype(bf16)
        kv_ref[at, :] = out[:, PAD:].astype(bf16)


def project(order, where, pieces, own, oth, small_own, small_oth):
    blocks, span_rows, width = pieces[0].shape
    spans = 4 * blocks
    rows = spans * span_rows
    return pl.pallas_call(
        project_kernel,
        in_specs=[pl.BlockSpec(memory_space=pltpu.SMEM)] * 2
        + [pl.BlockSpec(memory_space=pltpu.VMEM)] * 8,
        out_specs=[pl.BlockSpec(memory_space=pltpu.VMEM)] * 5,
        out_shape=[
            jax.ShapeDtypeStruct((rows, width), bf16),
            jax.ShapeDtypeStruct((rows, width), bf16),
            jax.ShapeDtypeStruct((rows, PAD), bf16),
            jax.ShapeDtypeStruct((rows, 2 * PAD), bf16),
            jax.ShapeDtypeStruct((width, 3 * PAD), bf16),
        ],
        scratch_shapes=[VMEM((spans, span_rows, width), bf16)],
        compiler_params=pltpu.CompilerParams(vmem_limit_bytes=vmem_cap),
        cost_estimate=busy(6),
        name="project",
    )(order, where, *pieces, own, oth, small_own, small_oth)


def middle_kernel(
    where_ref, attn_ref, x_ref, cot_ref, d_mlp_ref, grad_own_ref, proj_oth_ref, out_own_ref, out_oth_ref, fc_own_ref, fc_oth_ref,
    small_own_ref, small_oth_ref,
    resid_ref, attn_low_ref, normed_ref, hidden_ref, pre_ref, d_resid_ref, d_branch_ref, send_ref,
    branch_sum_ref, gain_sum_ref, shift_sum_ref, mlp_sum_ref, pre_sum_ref,
    back, bias_fc, w_out_ref, w_fc_ref,
):
    core = where_ref[2]
    for own, oth, whole in ((out_own_ref, out_oth_ref, w_out_ref), (fc_own_ref, fc_oth_ref, w_fc_ref)):
        rows = own.shape[0]
        whole[pl.ds(pl.multiple_of(core * rows, rows), rows), :] = own[...]
        whole[pl.ds(pl.multiple_of((1 - core) * rows, rows), rows), :] = oth[...]
    small = joined(small_own_ref[...], small_oth_ref[...], core)
    half = small_own_ref.shape[1]
    gain = small[5:6]
    for i in range(4):
        bias_fc[:, half * i : half * (i + 1)] = jnp.where(
            core == 0, small_own_ref[8 + i : 9 + i], small_oth_ref[8 + i : 9 + i]
        )
        bias_fc[:, half * (4 + i) : half * (5 + i)] = jnp.where(
            core == 0, small_oth_ref[8 + i : 9 + i], small_own_ref[8 + i : 9 + i]
        )
    attn = jnp.concatenate([attn_ref[g].astype(f32) for g in range(GROUPS)], axis=1).astype(bf16)
    attn_low_ref[...] = attn
    cot = cot_ref[...].astype(f32)
    branch = dot(attn, w_out_ref[...], ((1,), (0,))) + small[4:5]
    resid = x_ref[...].astype(f32) + branch_scale * branch
    resid_ref[...] = resid
    unit, inverse = norm_parts(resid)
    low = (unit * gain + small[6:7]).astype(bf16)
    normed_ref[...] = low
    back[...] = jnp.zeros_like(back)
    wide = 512

    def columns(hidden_grad, first, t, carry):
        here = pl.ds(pl.multiple_of(t * wide, wide), wide)
        at = pl.ds(pl.multiple_of(first + t * wide, wide), wide)
        weight = w_fc_ref[:, at]
        u = dot(low, weight, ((1,), (0,))) + bias_fc[:, at]
        square = u * u
        th = jnp.tanh(0.7978845608028654 * (u + 0.044715 * (square * u)))
        one = 0.5 * (1.0 + th)
        hidden_ref[:, at] = (u * one).astype(bf16)
        slope = one + 0.5 * u * (1.0 - th * th) * (0.7978845608028654 * (1.0 + 0.134145 * square))
        pre = (hidden_grad(here) * slope).astype(bf16)
        pre_ref[:, at] = pre
        pre_sum_ref[:, at] = jnp.sum(pre.astype(f32), axis=0, keepdims=True)
        back[...] += dot(pre, weight, ((1,), (1,)))
        return carry

    span = grad_own_ref.shape[1]
    lax.fori_loop(
        0, span // wide, functools.partial(columns, lambda here: grad_own_ref[:, here], core * span), 0
    )
    lax.fori_loop(
        0, span // wide,
        functools.partial(
            columns,
            lambda here: dot(d_mlp_ref[...], proj_oth_ref[here, :], ((1,), (1,))),
            (1 - core) * span,
        ),
        0,
    )
    d_normed = back[...]
    gain_sum_ref[...] = jnp.sum(d_normed * unit, axis=0, keepdims=True)
    shift_sum_ref[...] = jnp.sum(d_normed, axis=0, keepdims=True)
    scaled = d_normed * gain
    part = scaled - jnp.mean(scaled, axis=-1, keepdims=True)
    part = part - unit * jnp.mean(scaled * unit, axis=-1, keepdims=True)
    d_resid = cot + inverse * part
    d_resid_ref[...] = d_resid
    d_branch = (branch_scale * d_resid).astype(bf16)
    d_branch_ref[...] = d_branch
    branch_sum_ref[...] = jnp.sum(d_branch.astype(f32), axis=0, keepdims=True)
    mlp_sum_ref[...] = jnp.sum(d_mlp_ref[...].astype(f32), axis=0, keepdims=True)
    d_attn = dot(d_branch, w_out_ref[...], ((1,), (1,)))
    feats = send_ref.shape[2]
    for g in range(GROUPS):
        send_ref[g] = d_attn[:, feats * g : feats * (g + 1)].astype(bf16)


def middle(
    attn, x, cot, d_mlp, grad_own, proj_oth, out_own, out_oth, fc_own, fc_oth, where, small_own, small_oth
):
    groups, rows, feats = attn.shape
    width, wide = out_own.shape[1], fc_own.shape[1]
    shapes = [
        ((rows, width), f32), ((rows, width), bf16), ((rows, width), bf16), ((rows, wide), bf16),
        ((rows, wide), bf16), ((rows, width), f32), ((rows, width), bf16), (attn.shape, bf16),
        ((1, width), f32), ((1, width), f32), ((1, width), f32), ((1, width), f32), ((1, wide), f32),
    ]
    return pl.pallas_call(
        middle_kernel,
        in_specs=[pl.BlockSpec(memory_space=pltpu.SMEM)]
        + [pl.BlockSpec(memory_space=pltpu.VMEM)] * 12,
        out_specs=[pl.BlockSpec(memory_space=pltpu.VMEM)] * len(shapes),
        out_shape=[jax.ShapeDtypeStruct(shape, kind) for shape, kind in shapes],
        scratch_shapes=[
            VMEM((rows, width), f32),
            VMEM((1, wide), f32),
            VMEM((width, width), bf16),
            VMEM((width, wide), bf16),
        ],
        compiler_params=pltpu.CompilerParams(vmem_limit_bytes=vmem_cap),
        cost_estimate=work(12),
        name="middle",
    )(
        where, attn, x, cot, d_mlp, grad_own, proj_oth, out_own, out_oth, fc_own, fc_oth, small_own, small_oth
    )


def pack_kernel(where_ref, gain_ref, shift_ref, bias_ref, *refs):
    sums, own_ref, oth_ref = refs[:5], refs[5], refs[6]
    group, core = where_ref[1], where_ref[2]
    half = own_ref.shape[1]

    def spread(part):
        none = jnp.zeros((1, 192), f32)
        return jnp.concatenate([jnp.where(group == g, part, none) for g in range(GROUPS)], axis=1)

    vectors = [
        gain_ref[...], shift_ref[...],
        spread(bias_ref[:, :192]), spread(bias_ref[:, 2 * PAD : 2 * PAD + 192]),
    ]
    vectors += [r[...] for r in sums[:4]]
    for index, vector in enumerate(vectors):
        low, high = vector[:, :half], vector[:, half:]
        own_ref[index : index + 1, :] = jnp.where(core == 0, low, high)
        oth_ref[index : index + 1, :] = jnp.where(core == 0, high, low)
    wide = sums[4][...]
    for index in range(4):
        low = wide[:, half * index : half * (index + 1)]
        high = wide[:, half * (index + 4) : half * (index + 5)]
        own_ref[8 + index : 9 + index, :] = jnp.where(core == 0, low, high)
        oth_ref[8 + index : 9 + index, :] = jnp.where(core == 0, high, low)


def pack(where, gain, shift, bias, sums):
    half = gain.shape[1] // 2
    return pl.pallas_call(
        pack_kernel,
        in_specs=[pl.BlockSpec(memory_space=pltpu.SMEM)]
        + [pl.BlockSpec(memory_space=pltpu.VMEM)] * 8,
        out_specs=[pl.BlockSpec(memory_space=pltpu.VMEM)] * 2,
        out_shape=[jax.ShapeDtypeStruct((12, half), f32)] * 2,
        cost_estimate=work(1),
        name="pack",
    )(where, gain, shift, bias, *sums)


def by_head(tile):
    lane = lax.broadcasted_iota(jnp.int32, tile.shape, 1)
    zero = jnp.zeros_like(tile)
    return jnp.concatenate(
        [jnp.where((lane >= 64 * h) & (lane < 64 * h + 64), tile, zero) for h in range(3)], axis=0
    )


def by_head_t(tile):
    flipped = tile.T
    feat = lax.broadcasted_iota(jnp.int32, flipped.shape, 0)
    zero = jnp.zeros_like(flipped)
    return jnp.concatenate(
        [jnp.where((feat >= 64 * h) & (feat < 64 * h + 64), flipped, zero) for h in range(3)], axis=1
    )


def tile_rows(index):
    return pl.ds(pl.multiple_of(index * TILE, TILE), TILE)


def tile_pair(plan_ref, i, step, tiles):
    first = plan_ref[0, i] + 2 * step
    beyond = jnp.where(first + 1 < plan_ref[1, i], 0, 1 << 20)
    second = jnp.minimum(first + 1, tiles - 1)
    return tile_rows(first), tile_rows(second), beyond


def pair_rows(own_ref, oth_ref, first, second, lanes):
    return jnp.concatenate(
        [own_ref[first, lanes], oth_ref[first, lanes], own_ref[second, lanes], oth_ref[second, lanes]],
        axis=0,
    )


def pair_columns(own_ref, oth_ref, first, second):
    return jnp.concatenate(
        [own_ref[:, first], oth_ref[:, first], own_ref[:, second], oth_ref[:, second]], axis=1
    )


def visible_pair(kpos_ref, first, second, beyond, meta):
    keys = jnp.concatenate(
        [
            kpos_ref[0, first, :],
            kpos_ref[1, first, :],
            kpos_ref[0, second, :] + beyond,
            kpos_ref[1, second, :] + beyond,
        ],
        axis=0,
    )
    keys = jnp.concatenate([keys, keys, keys], axis=1)
    return (keys <= meta[0:1, :]) & (keys >= meta[1:2, :])


def pairs_of(plan_ref, i):
    return (plan_ref[1, i] - plan_ref[0, i] + 1) // 2


def attend_kernel(
    plan_ref, q_ref, own_ref, oth_ref, kpos_ref, meta_ref,
    o_ref, lse_ref, out_ref,
    vown, voth, stack, acc, top, held,
):
    spans, span_rows, feats = out_ref.shape
    tiles = q_ref.shape[0] // TILE
    keys_step = 4 * TILE
    vown[...] = own_ref[:, PAD:].T
    voth[...] = oth_ref[:, PAD:].T

    def one_tile(i, carry):
        here = tile_rows(i)
        stack[...] = by_head_t(q_ref[here, :])
        meta = meta_ref[i]
        acc[...] = jnp.zeros_like(acc)
        top[...] = jnp.full_like(top, neg_large)

        def score(step, inner):
            first, second, beyond = tile_pair(plan_ref, i, step, tiles)
            keys = pair_rows(own_ref, oth_ref, first, second, slice(0, PAD))
            scores = dot(keys, stack[...], ((1,), (0,)))
            allowed = visible_pair(kpos_ref, first, second, beyond, meta)
            scores = jnp.where(allowed, scores, neg_large)
            held[pl.ds(pl.multiple_of(step * keys_step, keys_step), keys_step), :] = scores
            best = jnp.max(scores.reshape(keys_step // 8, 8, scores.shape[1]), axis=0)
            top[...] = jnp.maximum(top[...], best)
            return inner

        lax.fori_loop(0, pairs_of(plan_ref, i), score, 0)
        peak = jnp.max(top[...], axis=0, keepdims=True)

        def weigh(step, inner):
            first, second, unused = tile_pair(plan_ref, i, step, tiles)
            scores = held[pl.ds(pl.multiple_of(step * keys_step, keys_step), keys_step), :]
            probs = jnp.exp(scores - peak).astype(bf16)
            vals = pair_columns(vown, voth, first, second)
            acc[...] += dot(vals, probs, ((1,), (0,)))
            return inner

        lax.fori_loop(0, pairs_of(plan_ref, i), weigh, 0)
        total = acc[192:193, :]
        lse_ref[i] = peak + jnp.log(total)
        parts = [
            acc[64 * h : 64 * h + 64, TILE * h : TILE * h + TILE]
            / total[:, TILE * h : TILE * h + TILE]
            for h in range(3)
        ]
        heads_t = jnp.concatenate(parts + [jnp.zeros((64, TILE), f32)], axis=0)
        o_ref[here, :] = heads_t.T
        return carry

    lax.fori_loop(0, tiles, one_tile, 0)
    for a in range(spans):
        out_ref[plan_ref[2, a]] = o_ref[span_rows * a : span_rows * (a + 1), :feats].astype(bf16)


def attend(plan, q, own, oth, kpos, meta, spans):
    rows = q.shape[0]
    tiles = rows // TILE
    wide = 3 * TILE
    return pl.pallas_call(
        attend_kernel,
        in_specs=[pl.BlockSpec(memory_space=pltpu.SMEM)]
        + [pl.BlockSpec(memory_space=pltpu.VMEM)] * 5,
        out_specs=[pl.BlockSpec(memory_space=pltpu.VMEM)] * 3,
        out_shape=[
            jax.ShapeDtypeStruct((rows, PAD), f32),
            jax.ShapeDtypeStruct((tiles, 1, wide), f32),
            jax.ShapeDtypeStruct((spans, rows // spans, 192), bf16),
        ],
        scratch_shapes=[
            VMEM((PAD, rows), bf16),
            VMEM((PAD, rows), bf16),
            VMEM((PAD, wide), bf16),
            VMEM((PAD, wide), f32),
            VMEM((8, wide), f32),
            VMEM((2 * rows + 2 * TILE, wide), f32),
        ],
        compiler_params=pltpu.CompilerParams(vmem_limit_bytes=vmem_cap),
        cost_estimate=work(15),
        name="attend",
    )(plan, q, own, oth, kpos, meta)


def attend_back_kernel(
    plan_ref, q_ref, own_ref, oth_ref, kpos_ref, meta_ref, grad_ref, o_ref, lse_ref,
    dq_ref, down_ref, doth_ref,
    grads, kown, koth, acc_oth, stack, gstack, stack_t, gstack_t, dq_t,
):
    spans, span_rows, feats = grad_ref.shape
    tiles = q_ref.shape[0] // TILE
    kown[...] = own_ref[:, :PAD].T
    koth[...] = oth_ref[:, :PAD].T
    down_ref[...] = jnp.zeros_like(down_ref)
    acc_oth[...] = jnp.zeros_like(acc_oth)
    grads[:, 128:] = jnp.zeros((grads.shape[0], PAD - 128), f32)
    for a in range(spans):
        grads[span_rows * a : span_rows * (a + 1), :feats] = grad_ref[plan_ref[2, a]].astype(f32)

    def one_tile(i, carry):
        here = tile_rows(i)
        grad = grads[here, :]
        grad_low = grad.astype(bf16)
        stack[...] = by_head(q_ref[here, :])
        gstack[...] = by_head(grad_low)
        stack_t[...] = by_head_t(q_ref[here, :])
        gstack_t[...] = by_head_t(grad_low)
        product = (grad * o_ref[here, :]).T
        delta = jnp.concatenate(
            [jnp.sum(product[64 * h : 64 * h + 64], axis=0, keepdims=True) for h in range(3)], axis=1
        )
        lse = lse_ref[i]
        meta = meta_ref[i]
        dq_t[...] = jnp.zeros_like(dq_t)

        def one(step, inner):
            first, second, beyond = tile_pair(plan_ref, i, step, tiles)
            keys = pair_rows(own_ref, oth_ref, first, second, slice(0, PAD))
            vals = pair_rows(own_ref, oth_ref, first, second, slice(PAD, 2 * PAD))
            scores = dot(keys, stack_t[...], ((1,), (0,)))
            allowed = visible_pair(kpos_ref, first, second, beyond, meta)
            probs = jnp.where(allowed, jnp.exp(scores - lse), 0.0)
            d_probs = dot(vals, gstack_t[...], ((1,), (0,)))
            d_scores = (probs * (d_probs - delta)).astype(bf16)
            d_vals = dot(probs.astype(bf16), gstack[...], ((1,), (0,)))
            d_keys = dot(d_scores, stack[...], ((1,), (0,)))
            down_ref[first, :PAD] += d_keys[:TILE]
            down_ref[first, PAD:] += d_vals[:TILE]
            acc_oth[first, :PAD] += d_keys[TILE : 2 * TILE]
            acc_oth[first, PAD:] += d_vals[TILE : 2 * TILE]
            down_ref[second, :PAD] += d_keys[2 * TILE : 3 * TILE]
            down_ref[second, PAD:] += d_vals[2 * TILE : 3 * TILE]
            acc_oth[second, :PAD] += d_keys[3 * TILE :]
            acc_oth[second, PAD:] += d_vals[3 * TILE :]
            dq_t[...] += dot(pair_columns(kown, koth, first, second), d_scores, ((1,), (0,)))
            return inner

        lax.fori_loop(0, pairs_of(plan_ref, i), one, 0)
        parts = [dq_t[64 * h : 64 * h + 64, TILE * h : TILE * h + TILE] for h in range(3)]
        heads_t = jnp.concatenate(parts + [jnp.zeros((64, TILE), f32)], axis=0) * 0.125
        dq_ref[here, :] = heads_t.T.astype(bf16)
        return carry

    lax.fori_loop(0, tiles, one_tile, 0)
    doth_ref[...] = acc_oth[...].astype(bf16)


def attend_back(plan, q, own, oth, kpos, meta, grad, o, lse):
    rows = q.shape[0]
    wide = 3 * TILE
    return pl.pallas_call(
        attend_back_kernel,
        in_specs=[pl.BlockSpec(memory_space=pltpu.SMEM)]
        + [pl.BlockSpec(memory_space=pltpu.VMEM)] * 8,
        out_specs=[pl.BlockSpec(memory_space=pltpu.VMEM)] * 3,
        out_shape=[
            jax.ShapeDtypeStruct((rows, PAD), bf16),
            jax.ShapeDtypeStruct((rows, 2 * PAD), f32),
            jax.ShapeDtypeStruct((rows, 2 * PAD), bf16),
        ],
        scratch_shapes=[
            VMEM((rows, PAD), f32),
            VMEM((PAD, rows), bf16),
            VMEM((PAD, rows), bf16),
            VMEM((rows, 2 * PAD), f32),
            VMEM((wide, PAD), bf16),
            VMEM((wide, PAD), bf16),
            VMEM((PAD, wide), bf16),
            VMEM((PAD, wide), bf16),
            VMEM((PAD, wide), f32),
        ],
        compiler_params=pltpu.CompilerParams(vmem_limit_bytes=vmem_cap),
        cost_estimate=busy(24),
        name="attend_back",
    )(plan, q, own, oth, kpos, meta, grad, o, lse)


def unproject_kernel(
    place_ref, x_ref, dq_ref, down_ref, doth_ref, weight_ref,
    pieces_ref, grad_ref, gain_ref, shift_ref, bias_ref,
):
    i = pl.program_id(0)
    span_rows = pieces_ref.shape[1]

    @pl.when(i == 0)
    def _():
        gain_ref[...] = jnp.zeros_like(gain_ref)
        shift_ref[...] = jnp.zeros_like(shift_ref)
        bias_ref[...] = jnp.zeros_like(bias_ref)

    normed, unused = norm_parts(x_ref[...].astype(f32))
    dkv = (down_ref[...] + doth_ref[...].astype(f32)).astype(bf16)
    grad = jnp.concatenate([dq_ref[...], dkv], axis=1)
    grad_ref[...] = jnp.concatenate(
        [grad[:, :192], grad[:, PAD : PAD + 192], grad[:, 2 * PAD : 2 * PAD + 192], grad[:, 192:PAD]],
        axis=1,
    )
    bias_ref[...] += jnp.sum(grad.astype(f32), axis=0, keepdims=True)
    back = dot(grad, weight_ref[...], ((1,), (1,)))
    gain_ref[...] += jnp.sum(back * normed, axis=0, keepdims=True)
    shift_ref[...] += jnp.sum(back, axis=0, keepdims=True)
    for t in range(4):
        pieces_ref[place_ref[4 * i + t]] = back[span_rows * t : span_rows * (t + 1)].astype(bf16)


def unproject(place, x, dq, down, doth, weight, spans):
    rows, width = x.shape
    step = rows // 4
    pieces = jax.ShapeDtypeStruct((spans, rows // spans, width), bf16)
    grid_spec = pltpu.PrefetchScalarGridSpec(
        num_scalar_prefetch=1,
        grid=(4,),
        in_specs=[
            pl.BlockSpec((step, width), lambda i, *unused: (i, 0)),
            pl.BlockSpec((step, PAD), lambda i, *unused: (i, 0)),
            pl.BlockSpec((step, 2 * PAD), lambda i, *unused: (i, 0)),
            pl.BlockSpec((step, 2 * PAD), lambda i, *unused: (i, 0)),
            full_spec((width, 3 * PAD)),
        ],
        out_specs=[
            full_spec(pieces.shape),
            pl.BlockSpec((step, PACK), lambda i, *unused: (i, 0)),
            full_spec((1, width)),
            full_spec((1, width)),
            full_spec((1, 3 * PAD)),
        ],
    )
    return pl.pallas_call(
        unproject_kernel,
        grid_spec=grid_spec,
        out_shape=[
            pieces,
            jax.ShapeDtypeStruct((rows, PACK), bf16),
            jax.ShapeDtypeStruct((1, width), f32),
            jax.ShapeDtypeStruct((1, width), f32),
            jax.ShapeDtypeStruct((1, 3 * PAD), f32),
        ],
        compiler_params=pltpu.CompilerParams(vmem_limit_bytes=vmem_cap),
        cost_estimate=busy(8),
        name="unproject",
    )(place, x, dq, down, doth, weight)


def halve(value, bit):
    value = value.reshape(2, value.shape[0] // 2, value.shape[1])
    return row(value, bit), row(value, 1 - bit)


def reduce_z(value, z):
    value = value.reshape(4, value.shape[0] // 4, value.shape[1])
    return row(value, z), [row(value, (z + k) % 4) for k in (1, 2, 3)]


def over_z(sends):
    return [send_z(sends[k - 1], k) for k in (1, 2, 3)]


def reduce_plane(value, group):
    value = value.reshape(4, value.shape[0] // 4, value.shape[1])
    return row(value, group), [row(value, group ^ f) for f in (1, 2, 3)]


def over_plane(sends):
    return [send_flip(sends[f - 1], f) for f in (1, 2, 3)]


def gather_z(value):
    pair = jnp.stack([value, send_flip(value, 8)])
    return jnp.concatenate([pair, send_flip(pair, 4)], axis=0)


def spread_once(left, right):
    return jnp.concatenate([left, send_flip(left, 1)], axis=0), jnp.concatenate(
        [right, send_flip(right, 2)], axis=0
    )


def spread_twice(left, right):
    return left, send_flip(left, 2), right, send_flip(right, 1)


def cut_lanes(value, at):
    return value[:, :, :at], value[:, :, at:]


def entry(refs, side, f, k):
    if side == 0:
        return refs[f // 2][4 * (f % 2) + k].astype(f32)
    return refs[2 + f % 2][4 * (f // 2) + k].astype(f32)


def block_of(z, k):
    return ((z & 1) ^ (k >> 1)) * 2 + ((z >> 1) ^ (k & 1))


def chip_of(z, k):
    return z ^ ((k >> 1) + 2 * (k & 1))


def place_proj_kernel(where_ref, *refs):
    parts, out_ref = refs[:4], refs[4]
    z, group = where_ref[0], where_ref[1]
    rows, half = parts[0].shape[1:]
    for f in range(4):
        x, y = (group ^ f) & 1, (group ^ f) >> 1
        for k in range(4):
            at = ((2 * x + y) * 4 + block_of(z, k)) * rows
            out_ref[pl.ds(pl.multiple_of(at, 8), rows), :half] = entry(parts, 0, f, k)
            at = ((2 * y + x) * 4 + block_of(z, k)) * rows
            out_ref[pl.ds(pl.multiple_of(at, 8), rows), half:] = entry(parts, 1, f, k)


def place_rest_kernel(where_ref, *refs):
    parts, fc_ref, out_ref = refs[:4], refs[4], refs[5]
    z, group = where_ref[0], where_ref[1]
    rows, half = parts[0].shape[1:]
    fc_wide = fc_ref.shape[1]
    for f in range(4):
        for k in range(4):
            at = ((group ^ f) * 4 + chip_of(z, k)) * rows
            at = pl.ds(pl.multiple_of(at, 8), rows)
            fc_ref[at, :half] = entry(parts, 0, f, k)
            right = entry(parts, 1, f, k)
            fc_ref[at, half:] = right[:, : fc_wide - half]
            out_ref[at, :] = right[:, fc_wide - half :]


def place_in_kernel(where_ref, *refs):
    parts, in_ref, small_ref, held = refs[:4], refs[4], refs[5], refs[6]
    z, group = where_ref[0], where_ref[1]
    upper = parts[0].shape[1]
    rows = upper + parts[2].shape[1] - 8
    small_ref[...] = jnp.zeros(small_ref.shape, f32)
    for f in range(4):
        for k in range(4):
            block = z ^ k
            held[group ^ f, block, :upper] = entry(parts, 0, f, k)
            right = entry(parts, 1, f, k)
            held[group ^ f, block, upper:rows] = right[:-8]
            small_ref[block] = small_ref[block] + right[-8:]
    for block in range(4):
        for i in range(3):
            at = 192 * i
            columns = [held[g, block, :, at : at + 192] for g in range(4)]
            in_ref[rows * block : rows * (block + 1), 768 * i : 768 * (i + 1)] = jnp.concatenate(
                columns, axis=1
            )


def place(kernel, name, micros, where, parts, shapes, scratch=()):
    return pl.pallas_call(
        kernel,
        in_specs=[pl.BlockSpec(memory_space=pltpu.SMEM)]
        + [pl.BlockSpec(memory_space=pltpu.VMEM)] * len(parts),
        out_specs=[pl.BlockSpec(memory_space=pltpu.VMEM)] * len(shapes),
        out_shape=[jax.ShapeDtypeStruct(shape, f32) for shape in shapes],
        scratch_shapes=list(scratch),
        compiler_params=pltpu.CompilerParams(vmem_limit_bytes=vmem_cap),
        cost_estimate=busy(micros),
        name=name,
    )(where, *parts)


def split_halves(value, w, axis):
    low, high = jnp.split(value, 2, axis)
    return jnp.where(w == 0, low, high), jnp.where(w == 0, high, low)


def grad_dot(left, right):
    return dot(left, right, ((0,), (0,)))


def norm_back(grad, rows, gain):
    normed, inverse = norm_parts(rows)
    scaled = grad * gain
    part = scaled - jnp.mean(scaled, axis=-1, keepdims=True)
    part = part - normed * jnp.mean(scaled * normed, axis=-1, keepdims=True)
    return inverse * part, normed


def by_owner(
    block_input, span_order, doc_lengths, ln1_gain, ln1_bias, w_qkv, qv_bias, w_out, out_bias,
    ln2_gain, ln2_bias, w_fc, fc_bias, w_proj, proj_bias, d_out,
):
    seq_group, seq_dev, width = block_input.shape
    seqs = 2 * seq_group
    span_rows = seq_dev // 2
    chips = span_order.shape[0]
    rows = chips * span_rows
    me = lax.axis_index("ctx")
    w = lax.axis_index("wt")
    z, y, x = me // 4, me // 2 % 2, me % 2
    where = (z, y, x)
    group = me % 4

    second = (row(span_order, me)[0] % 2) != w

    def take_spans(value):
        value = value.reshape(seq_group, 2, span_rows, width)
        keep = jnp.where(second, value[:, 1], value[:, 0])
        give = jnp.where(second, value[:, 0], value[:, 1])
        got = other_core(give)
        return jnp.where(
            w == 0, jnp.concatenate([keep, got], axis=0), jnp.concatenate([got, keep], axis=0)
        )

    def give_spans(value):
        low, high = value[:seq_group], value[seq_group:]
        keep = jnp.where(w == 0, low, high)
        got = other_core(jnp.where(w == 0, high, low))
        first = jnp.where(second, got, keep)
        last = jnp.where(second, keep, got)
        return jnp.concatenate([first, last], axis=1)

    def to_sequence(value):
        got = [send_z(row(value, (z + k) % 4), k) for k in (1, 2, 3)]
        return [row(value, z)] + got

    z_low, z_high = z % 2, z // 2

    def z_first(blocks):
        keep = jnp.stack([row(blocks, z_low + 2 * h) for h in (0, 1)])
        give = jnp.stack([row(blocks, 1 - z_low + 2 * h) for h in (0, 1)])
        return keep, send_flip(give, 4)

    def z_second(keep, got):
        pairs = jnp.stack([keep, got], axis=1)
        here, there = row(pairs, z_high), send_flip(row(pairs, 1 - z_high), 8)
        return jnp.concatenate([here, there], axis=0)

    def by_chip(value):
        return jnp.stack([row(value, (z - s) % 4) for s in range(seqs)])

    def by_source(got):
        return jnp.stack([row(got, z ^ s) for s in range(seqs)])

    kept = to_sequence(take_spans(block_input))
    left, right = jnp.stack(kept[:2]), jnp.stack(kept[2:])
    tokens_low = jnp.concatenate([left, right], axis=0)
    span_order, doc_lengths, unused = lax.optimization_barrier((span_order, doc_lengths, (left, right)))
    left_x, right_y = send_flip(left, 1), send_flip(right, 2)
    ranks = jnp.arange(rows, dtype=jnp.int32)
    even_pos = 2 * span_rows * (ranks // span_rows) + ranks % span_rows
    own_pos = even_pos + span_rows * w
    oth_pos = even_pos + span_rows * (1 - w)
    kpos = jnp.broadcast_to(jnp.stack([own_pos, oth_pos])[:, :, None], (2, rows, TILE)).astype(jnp.int32)
    left_x, right_y, kpos = lax.optimization_barrier((left_x, right_y, kpos))
    left = jnp.concatenate([left, left_x], axis=0)
    right = jnp.concatenate([right, right_y], axis=0)
    pieces = (left, send_flip(left, 2), right, send_flip(right, 1))
    (
        ln1_gain, ln1_bias, w_qkv, qv_bias, d_out, out_bias, ln2_gain, ln2_bias, proj_bias, fc_bias, unused,
    ) = lax.optimization_barrier(
        (
            ln1_gain, ln1_bias, w_qkv, qv_bias, d_out, out_bias, ln2_gain, ln2_bias, proj_bias, fc_bias,
            (left, right),
        )
    )
    cot_low = jnp.stack(to_sequence(take_spans(d_out))).reshape(seqs * span_rows, width)
    d_mlp = (branch_scale * cot_low.astype(f32)).astype(bf16)

    chip_ids = jnp.arange(chips, dtype=jnp.int32)
    span_here = jnp.where(span_order[:, 0] % 2 == w, span_order[:, 0], span_order[:, 1]) // 2
    span_ids = jnp.arange(chips, dtype=jnp.int32)
    holder = jnp.sum(
        jnp.where(span_here[None, :] == span_ids[:, None], chip_ids[None, :], 0), axis=1
    ).astype(jnp.int32)
    back_z = (z - holder // 4) % 4
    flip = group ^ (holder % 4)
    order = jnp.where(
        back_z < 2,
        (flip // 2) * 4 + (flip % 2) * 2 + back_z,
        8 + (flip % 2) * 4 + (flip // 2) * 2 + back_z - 2,
    ).astype(jnp.int32)
    order_back = (flip * 4 + back_z).astype(jnp.int32)
    owner = (holder % 4 * 4 + back_z).astype(jnp.int32)

    lengths_oth = other_core(doc_lengths)
    lengths = jnp.where(
        w == 0,
        jnp.concatenate([doc_lengths, lengths_oth], axis=0),
        jnp.concatenate([lengths_oth, doc_lengths], axis=0),
    )
    lengths = row(lengths, z)
    ends = jnp.cumsum(lengths)[:-1]
    starts = jnp.sum(
        jnp.where(own_pos[:, None] >= ends[None, :], lengths[None, :-1], 0), axis=1
    ).astype(jnp.int32)
    tiles = rows // TILE
    own_tiles = own_pos.reshape(tiles, TILE)
    start_tiles = starts.reshape(tiles, TILE)
    meta = jnp.tile(jnp.stack([own_tiles, start_tiles], axis=1), (1, 1, 3)).astype(jnp.int32)
    even_tiles = even_pos.reshape(tiles, TILE)
    low = jnp.sum(
        (even_tiles[None, :, -1] + span_rows < start_tiles[:, 0:1]).astype(jnp.int32), axis=1
    ).astype(jnp.int32)
    high = jnp.sum(
        (even_tiles[None, :, 0] <= own_tiles[:, -1:]).astype(jnp.int32), axis=1
    ).astype(jnp.int32)

    room = jnp.zeros((chips - tiles,), jnp.int32)
    plan = jnp.stack([jnp.concatenate([low, room]), jnp.concatenate([high, room]), owner])

    feats = width // GROUPS
    half = width // 2
    here = jnp.stack([z, group, w]).astype(jnp.int32)
    in_own = jnp.concatenate(
        [
            lax.dynamic_slice_in_dim(w_qkv, width * i + half * (group // 2), half, 1)
            for i in range(3)
        ],
        axis=1,
    )
    in_oth_core = other_core(in_own)
    vectors = [ln1_gain, ln1_bias, qv_bias[0], qv_bias[1], out_bias, ln2_gain, ln2_bias, proj_bias]
    vectors += [fc_bias[half * i : half * (i + 1)] for i in range(4)]
    lines = lax.broadcasted_iota(jnp.int32, (len(vectors), half), 0)
    small = jnp.zeros((len(vectors), half), f32)
    for i, one in enumerate(vectors):
        small = jnp.where(lines == i, jnp.broadcast_to(one.astype(f32), small.shape), small)
    small_oth = other_core(small)

    def vector(index):
        own, oth = small[index : index + 1], small_oth[index : index + 1]
        return jnp.concatenate([jnp.where(w == 0, own, oth), jnp.where(w == 0, oth, own)], axis=1)

    pieces, w_out, w_fc, w_proj, unused = lax.optimization_barrier(
        (pieces, w_out, w_fc, w_proj, (meta, plan, in_oth_core, small_oth, d_mlp))
    )
    out_oth, fc_oth, proj_oth = other_core(w_out), other_core(w_fc), other_core(w_proj)
    x_sorted, normed_one, query, kv_own, weight_in = project(
        order, here, pieces, in_own, in_oth_core, small, small_oth
    )
    query, kv_own, out_oth, fc_oth, proj_oth = lax.optimization_barrier(
        (query, kv_own, out_oth, fc_oth, proj_oth)
    )
    kv_oth = other_core(kv_own)
    attn, lse, attn_send = attend(plan, query, kv_own, kv_oth, kpos, meta, chips)
    attn_got = swap_plane(attn_send.reshape(GROUPS, seqs, span_rows, feats))

    d_mlp = after(d_mlp, attn_send)
    mlp_both = jnp.concatenate([d_mlp, other_core(d_mlp)], axis=0)
    grad_own = dot(d_mlp, w_proj, ((1,), (1,)))
    attn_got = after(attn_got, grad_own, mlp_both).reshape(GROUPS, seqs * span_rows, feats)

    tokens = tokens_low.reshape(seqs * span_rows, width)
    (
        resid, attn_low, normed_two, hidden_low, d_pre, d_resid, d_branch, d_send, *sums
    ) = middle(
        attn_got, tokens, cot_low, d_mlp, grad_own, proj_oth,
        w_out, out_oth, w_fc, fc_oth, here, small, small_oth,
    )
    d_got = swap_plane(d_send.reshape(GROUPS, seqs, span_rows, feats)).reshape(chips, span_rows, feats)
    hidden_own, hidden_oth = split_halves(hidden_low, w, 1)
    hidden_both = jnp.concatenate([hidden_own, other_core(hidden_oth)], axis=0)
    pre_both = jnp.concatenate([d_pre, other_core(d_pre)], axis=0)
    normed_own, normed_oth = split_halves(normed_two, w, 1)
    normed_both = jnp.concatenate([normed_own, other_core(normed_oth)], axis=0)
    attn_own, attn_oth = split_halves(attn_low, w, 1)
    attn_both = jnp.concatenate([attn_own, other_core(attn_oth)], axis=0)
    low_bit, high_bit = z % 2, z // 2
    branch_both = jnp.concatenate([d_branch, other_core(d_branch)], axis=0)
    hidden_both = after(hidden_both, d_send)
    grad_proj = grad_dot(hidden_both, mlp_both).astype(bf16)
    proj_left, left_send = halve(grad_proj[:, :half], x)
    proj_right, right_send = halve(grad_proj[:, half:], y)
    left_recv, right_recv = send_flip(left_send, 1), send_flip(right_send, 2)
    normed_both, attn_both, d_got, unused = lax.optimization_barrier(
        (normed_both, attn_both, d_got, (left_send, right_send))
    )
    fc_cols = d_pre.shape[1]
    grad_rest = jnp.concatenate(
        [grad_dot(normed_both, pre_both).astype(bf16), grad_dot(attn_both, branch_both).astype(bf16)],
        axis=1,
    )
    rest_keep, rest_sends = reduce_plane(grad_rest, group)
    left_recv, right_recv, unused = lax.optimization_barrier((left_recv, right_recv, rest_sends))
    proj_left, left_send = halve(sum_low(proj_left, left_recv), y)
    proj_right, right_send = halve(sum_low(proj_right, right_recv), x)
    left_recv, right_recv = send_flip(left_send, 2), send_flip(right_send, 1)
    rest_plane = over_plane(rest_sends)

    d_got = after(d_got, left_send, right_send, *rest_sends)
    d_query, d_own, d_oth = attend_back(plan, query, kv_own, kv_oth, kpos, meta, d_got, attn, lse)
    left_recv, right_recv, rest_plane, d_query, d_oth = lax.optimization_barrier(
        (left_recv, right_recv, rest_plane, d_query, d_oth)
    )
    d_recv = other_core(d_oth)
    grad_proj = jnp.concatenate(
        [sum_low(proj_left, left_recv), sum_low(proj_right, right_recv)], axis=1
    )
    proj_keep, proj_send = halve(grad_proj, low_bit)
    proj_recv = send_flip(proj_send, 4)
    rest_keep, rest_sends = reduce_z(sum_low(rest_keep, *rest_plane), z)
    proj_recv, d_recv, rest_sends = lax.optimization_barrier((proj_recv, d_recv, rest_sends))
    rest_z = over_z(rest_sends)
    proj_keep, proj_send = halve(sum_low(proj_keep, proj_recv), high_bit)
    proj_recv = send_flip(proj_send, 8)
    d_recv = after(d_recv, proj_send)
    d_pieces, d_qkv, part_gain, part_shift, part_bias = unproject(
        order_back, x_sorted, d_query, d_own, d_recv, weight_in, chips
    )
    proj_recv, rest_z, d_pieces, d_qkv, part_gain, part_shift, part_bias, sums = lax.optimization_barrier(
        (proj_recv, rest_z, d_pieces, d_qkv, part_gain, part_shift, part_bias, sums)
    )

    proj_shard = sum_low(proj_keep, proj_recv)
    rest_shard = sum_low(rest_keep, *rest_z)
    d_qkv, unused = lax.optimization_barrier((d_qkv, (proj_shard, rest_shard)))
    proj_pair = jnp.stack([proj_shard, send_flip(proj_shard, 8)])
    rest_pair = jnp.stack([rest_shard, send_flip(rest_shard, 8)])
    back_sends = [d_pieces[4 * f : 4 * f + 4] for f in (1, 2, 3)]
    back_x, back_y = send_flip(back_sends[0], 1), send_flip(back_sends[1], 2)
    normed_own, normed_oth = split_halves(normed_one, w, 1)
    in_oth = grad_dot(normed_oth, d_qkv).astype(bf16)
    in_got = other_core(in_oth)
    grads_own, grads_oth = pack(here, part_gain, part_shift, part_bias, sums)
    small_rows = (grads_own + other_core(grads_oth)).astype(bf16).reshape(4, 3, half)
    small_rows = jnp.pad(small_rows, ((0, 0), (0, 5), (0, PACK - half)))
    grad_in = (grad_dot(normed_own, d_qkv) + in_got.astype(f32)).astype(bf16)
    grad_in = jnp.concatenate([grad_in.reshape(4, half // 4, PACK), small_rows], axis=1)
    in_keep, in_send = halve(grad_in.reshape(-1, PACK), high_bit)
    proj_pair, rest_pair, back_x, back_y, back_xy, in_send = lax.optimization_barrier(
        (proj_pair, rest_pair, back_x, back_y, back_sends[2], in_send)
    )
    proj_all = jnp.concatenate([proj_pair, send_flip(proj_pair, 4)], axis=0)
    rest_all = jnp.concatenate([rest_pair, send_flip(rest_pair, 4)], axis=0)
    in_recv = send_flip(in_send, 8)
    back_xy = send_flip(back_xy, 3)
    proj_all, rest_all, in_recv, back_xy = lax.optimization_barrier((proj_all, rest_all, in_recv, back_xy))
    in_keep, in_send = halve(sum_low(in_keep, in_recv), low_bit)
    in_recv = send_flip(in_send, 4)
    proj_once = spread_once(*cut_lanes(proj_all, half))
    rest_once = spread_once(*cut_lanes(rest_all, rest_all.shape[2] // 2))
    proj_once, rest_once, in_recv = lax.optimization_barrier((proj_once, rest_once, in_recv))
    in_shard = sum_low(in_keep, in_recv)
    in_pair = jnp.stack([in_shard, send_flip(in_shard, 4)])
    proj_parts = spread_twice(*proj_once)
    back = sum_low(d_pieces[:4], back_x, back_y, after(back_xy, in_shard))
    proj_parts, in_pair, rest_once, back = lax.optimization_barrier((proj_parts, in_pair, rest_once, back))
    in_all = jnp.concatenate([in_pair, send_flip(in_pair, 8)], axis=0)
    rest_parts = spread_twice(*rest_once)
    d_first, unused = norm_back(
        back.reshape(seqs * span_rows, width).astype(f32), tokens.astype(f32), vector(0)
    )
    d_input = (d_resid + d_first).astype(bf16).reshape(seqs, span_rows, width)
    d_input = z_first(by_chip(d_input))
    hidden_own, hidden_oth, unused = lax.optimization_barrier((hidden_own, hidden_oth, in_pair))
    mlp = dot(hidden_own, w_proj, ((1,), (0,))) + dot(hidden_oth, proj_oth, ((1,), (0,))) + vector(7)
    block_out = (resid + branch_scale * mlp).astype(bf16).reshape(seqs, span_rows, width)
    block_out = by_chip(block_out)
    rest_parts, in_all, block_out, proj_parts, d_input = lax.optimization_barrier(
        (rest_parts, in_all, block_out, proj_parts, d_input)
    )
    in_once = spread_once(in_all[:, :56], in_all[:, 56:])
    d_input = z_second(*d_input)
    block_out = z_first(block_out)
    in_once, d_input, block_out, proj_parts, rest_parts = lax.optimization_barrier(
        (in_once, d_input, block_out, proj_parts, rest_parts)
    )
    in_parts = spread_twice(*in_once)
    block_out = z_second(*block_out)
    (grad_proj,) = place(
        place_proj_kernel, "place_proj", 5, here, proj_parts, [(fc_cols // 2, width)]
    )
    grad_fc, grad_out = place(
        place_rest_kernel, "place_rest", 5, here, rest_parts, [(half, fc_cols), (half, width)]
    )
    grad_w_qkv, small_all = place(
        place_in_kernel, "place_in", 4, here, in_parts,
        [(half, 3 * width), (4, 8, PACK)],
        [VMEM((4, 4, half // 4, PACK), f32)],
    )

    def piece(index):
        return small_all[index // 3, index % 3, :half]

    return (
        give_spans(by_source(block_out)),
        give_spans(by_source(d_input)).astype(f32),
        piece(0),
        piece(1),
        grad_w_qkv,
        jnp.stack([piece(2), piece(3)]),
        grad_out,
        piece(4),
        piece(5),
        piece(6),
        grad_fc,
        jnp.concatenate([piece(8), piece(9), piece(10), piece(11)]),
        grad_proj,
        piece(7),
    )


def layer_norm(values, gain, shift):
    center = jnp.mean(values, axis=-1, keepdims=True)
    moved = values - center
    spread = jnp.mean(moved * moved, axis=-1, keepdims=True)
    return moved * lax.rsqrt(spread + 1e-05) * gain + shift


def gelu_tanh(values):
    return (
        0.5
        * values
        * (1.0 + jnp.tanh(0.7978845608028654 * (values + 0.044715 * values * values * values)))
    )


def split_count(row_total, limit):
    pieces = 1
    while row_total % pieces != 0 or row_total // pieces > limit:
        pieces += 1
    return pieces


def row_positions(order_table, first_index, row_total, seq_dev, span_rows):
    rows_here = first_index + jnp.arange(row_total, dtype=jnp.int32)
    device_of = rows_here // seq_dev
    half_of = rows_here % seq_dev // span_rows
    slot_index = device_of * 2 + half_of
    flat_order = order_table.reshape(-1)
    table_slots = jnp.arange(flat_order.shape[0], dtype=jnp.int32)
    picked = jnp.sum(
        jnp.where(slot_index[:, None] == table_slots[None, :], flat_order[None, :], 0), axis=1
    )
    return picked * span_rows + rows_here % span_rows


def doc_of(positions, lengths_row):
    ends_at = jnp.cumsum(lengths_row)
    inner_ends = ends_at[:-1]
    return jnp.sum((positions[:, None] >= inner_ends[None, :]).astype(jnp.int32), axis=1)


def visible(query_pos, query_doc, key_pos, key_doc):
    causal = key_pos[None, None, :] <= query_pos[None, :, None]
    same_doc = key_doc[:, None, :] == query_doc[:, :, None]
    return (causal & same_doc)[:, :, None, :]


def per_device(
    block_input,
    span_order,
    doc_lengths,
    ln1_gain,
    ln1_bias,
    w_qkv,
    qv_bias,
    w_out,
    out_bias,
    ln2_gain,
    ln2_bias,
    w_fc,
    fc_bias,
    w_proj,
    proj_bias,
    d_out,
):
    seq_group, seq_dev, width = block_input.shape
    heads = HEADS
    head_dim = width // heads
    span_rows = seq_dev // 2
    score_scale = head_dim ** (-0.5)

    def docs_for(positions):
        return jax.vmap(doc_of, in_axes=(None, 0))(positions, doc_lengths)

    weights_all = (
        lax.all_gather(ln1_gain, "wt", axis=0, tiled=True),
        lax.all_gather(ln1_bias, "wt", axis=0, tiled=True),
        lax.all_gather(w_qkv, "wt", axis=0, tiled=True),
        lax.all_gather(qv_bias, "wt", axis=1, tiled=True),
        lax.all_gather(w_out, "wt", axis=0, tiled=True),
        lax.all_gather(out_bias, "wt", axis=0, tiled=True),
        lax.all_gather(ln2_gain, "wt", axis=0, tiled=True),
        lax.all_gather(ln2_bias, "wt", axis=0, tiled=True),
        lax.all_gather(w_fc, "wt", axis=0, tiled=True),
        lax.all_gather(fc_bias, "wt", axis=0, tiled=True),
        lax.all_gather(w_proj, "wt", axis=0, tiled=True),
        lax.all_gather(proj_bias, "wt", axis=0, tiled=True),
    )
    gain_one = weights_all[0].astype(jnp.float32)
    shift_one = weights_all[1].astype(jnp.float32)
    bias_pair = weights_all[3].astype(jnp.float32)
    bias_out = weights_all[5].astype(jnp.float32)
    gain_two = weights_all[6].astype(jnp.float32)
    shift_two = weights_all[7].astype(jnp.float32)
    bias_fc = weights_all[9].astype(jnp.float32)
    bias_proj = weights_all[11].astype(jnp.float32)
    me_ctx = lax.axis_index("ctx")
    local_pos = row_positions(span_order, me_ctx * seq_dev, seq_dev, seq_dev, span_rows)
    local_doc = docs_for(local_pos)
    tokens_in = block_input.astype(jnp.float32)
    normed_one = layer_norm(tokens_in, gain_one, shift_one).astype(jnp.bfloat16)
    qkv_bias = jnp.concatenate([bias_pair[0], jnp.zeros((width,), jnp.float32), bias_pair[1]])
    projected = (
        jnp.einsum("btd,de->bte", normed_one, weights_all[2], preferred_element_type=jnp.float32)
        + qkv_bias
    )
    projected_low = projected.astype(jnp.bfloat16)
    query_low = projected_low[..., :width]
    key_low = projected_low[..., width : 2 * width]
    value_low = projected_low[..., 2 * width :]
    query_heads = query_low.reshape(seq_group, seq_dev, heads, head_dim)
    key_heads = key_low.reshape(seq_group, seq_dev, heads, head_dim)
    value_heads = value_low.reshape(seq_group, seq_dev, heads, head_dim)
    start_state = (
        jnp.zeros((seq_group, seq_dev, heads, head_dim), jnp.float32),
        jnp.full((seq_group, seq_dev, heads), neg_large, jnp.float32),
        jnp.zeros((seq_group, seq_dev, heads), jnp.float32),
    )
    key_piece = lax.all_gather(key_low, "ctx", axis=1, tiled=True)
    value_piece = lax.all_gather(value_low, "ctx", axis=1, tiled=True)
    piece_rows = key_piece.shape[1]
    key_pos = row_positions(span_order, jnp.int32(0), piece_rows, seq_dev, span_rows)
    key_doc = docs_for(key_pos)
    block_rows = piece_rows // split_count(piece_rows, 1024)

    def one_block(block_index, running):
        acc_sum, run_max, run_total = running
        first_row = block_index * block_rows
        key_block = lax.dynamic_slice_in_dim(key_piece, first_row, block_rows, 1).reshape(
            seq_group, block_rows, heads, head_dim
        )
        value_block = lax.dynamic_slice_in_dim(value_piece, first_row, block_rows, 1).reshape(
            seq_group, block_rows, heads, head_dim
        )
        allowed = visible(
            local_pos,
            local_doc,
            lax.dynamic_slice_in_dim(key_pos, first_row, block_rows, 0),
            lax.dynamic_slice_in_dim(key_doc, first_row, block_rows, 1),
        )
        scores = (
            jnp.einsum(
                "bqhd,bkhd->bqhk", query_heads, key_block, preferred_element_type=jnp.float32
            )
            * score_scale
        )
        scores = jnp.where(allowed, scores, neg_large)
        new_max = jnp.maximum(run_max, jnp.max(scores, axis=-1))
        weights = jnp.where(allowed, jnp.exp(scores - new_max[..., None]), 0.0)
        rescale = jnp.exp(run_max - new_max)
        run_total = run_total * rescale + jnp.sum(weights, axis=-1)
        acc_sum = acc_sum * rescale[..., None] + jnp.einsum(
            "bqhk,bkhd->bqhd",
            weights.astype(jnp.bfloat16),
            value_block,
            preferred_element_type=jnp.float32,
        )
        return (acc_sum, new_max, run_total)

    acc_sum, run_max, run_total = lax.fori_loop(0, piece_rows // block_rows, one_block, start_state)
    attn_heads = acc_sum / run_total[..., None]
    log_total = run_max + jnp.log(run_total)
    attn_out = attn_heads.reshape(seq_group, seq_dev, width)
    attn_low = attn_out.astype(jnp.bfloat16)
    branch_pre = (
        jnp.einsum("btd,de->bte", attn_low, weights_all[4], preferred_element_type=jnp.float32)
        + bias_out
    )
    resid_one = tokens_in + branch_scale * branch_pre
    normed_two = layer_norm(resid_one, gain_two, shift_two).astype(jnp.bfloat16)
    hidden_pre = (
        jnp.einsum("btd,df->btf", normed_two, weights_all[8], preferred_element_type=jnp.float32)
        + bias_fc
    )
    hidden_low = gelu_tanh(hidden_pre).astype(jnp.bfloat16)
    mlp_pre = (
        jnp.einsum("btf,fd->btd", hidden_low, weights_all[10], preferred_element_type=jnp.float32)
        + bias_proj
    )
    block_out = (resid_one + branch_scale * mlp_pre).astype(jnp.bfloat16)
    weights_back = (
        lax.all_gather(ln1_gain, "wt", axis=0, tiled=True),
        lax.all_gather(ln1_bias, "wt", axis=0, tiled=True),
        lax.all_gather(w_qkv, "wt", axis=0, tiled=True),
        lax.all_gather(qv_bias, "wt", axis=1, tiled=True),
        lax.all_gather(w_out, "wt", axis=0, tiled=True),
        lax.all_gather(out_bias, "wt", axis=0, tiled=True),
        lax.all_gather(ln2_gain, "wt", axis=0, tiled=True),
        lax.all_gather(ln2_bias, "wt", axis=0, tiled=True),
        lax.all_gather(w_fc, "wt", axis=0, tiled=True),
        lax.all_gather(fc_bias, "wt", axis=0, tiled=True),
        lax.all_gather(w_proj, "wt", axis=0, tiled=True),
        lax.all_gather(proj_bias, "wt", axis=0, tiled=True),
    )
    back_gain_one = weights_back[0].astype(jnp.float32)
    back_shift_one = weights_back[1].astype(jnp.float32)
    back_gain_two = weights_back[6].astype(jnp.float32)
    back_shift_two = weights_back[7].astype(jnp.float32)
    cotangent = d_out.astype(jnp.float32)
    d_mlp = (branch_scale * cotangent).astype(jnp.bfloat16)
    grad_w_proj = jnp.einsum("btf,btd->fd", hidden_low, d_mlp, preferred_element_type=jnp.float32)
    grad_proj_bias = jnp.sum(d_mlp.astype(jnp.float32), axis=(0, 1))
    d_hidden = jnp.einsum(
        "btd,fd->btf", d_mlp, weights_back[10], preferred_element_type=jnp.float32
    )
    gelu_unused, gelu_pull = jax.vjp(gelu_tanh, hidden_pre)
    d_pre = gelu_pull(d_hidden)[0].astype(jnp.bfloat16)
    grad_w_fc = jnp.einsum("btd,btf->df", normed_two, d_pre, preferred_element_type=jnp.float32)
    grad_fc_bias = jnp.sum(d_pre.astype(jnp.float32), axis=(0, 1))
    d_normed_two = jnp.einsum(
        "btf,df->btd", d_pre, weights_back[8], preferred_element_type=jnp.float32
    )
    norm_unused, norm_pull = jax.vjp(layer_norm, resid_one, back_gain_two, back_shift_two)
    d_resid_part, grad_ln2_gain, grad_ln2_bias = norm_pull(d_normed_two)
    d_resid = cotangent + d_resid_part
    d_branch = (branch_scale * d_resid).astype(jnp.bfloat16)
    grad_w_out = jnp.einsum("btd,bte->de", attn_low, d_branch, preferred_element_type=jnp.float32)
    grad_out_bias = jnp.sum(d_branch.astype(jnp.float32), axis=(0, 1))
    d_attn_low = jnp.einsum(
        "bte,de->btd", d_branch, weights_back[4], preferred_element_type=jnp.float32
    ).astype(jnp.bfloat16)
    d_attn_heads = d_attn_low.reshape(seq_group, seq_dev, heads, head_dim)
    delta = jnp.sum(d_attn_heads.astype(jnp.float32) * attn_heads, axis=-1)
    fold_key_piece = lax.all_gather(key_low, "ctx", axis=1, tiled=True)
    fold_value_piece = lax.all_gather(value_low, "ctx", axis=1, tiled=True)
    piece_rows = fold_key_piece.shape[1]
    fold_key_pos = row_positions(span_order, jnp.int32(0), piece_rows, seq_dev, span_rows)
    fold_key_doc = docs_for(fold_key_pos)
    fold_block_rows = piece_rows // split_count(piece_rows, 1024)

    def one_block(block_index, grad_query):
        first_row = block_index * fold_block_rows
        key_block = lax.dynamic_slice_in_dim(fold_key_piece, first_row, fold_block_rows, 1).reshape(
            seq_group, fold_block_rows, heads, head_dim
        )
        value_block = lax.dynamic_slice_in_dim(
            fold_value_piece, first_row, fold_block_rows, 1
        ).reshape(seq_group, fold_block_rows, heads, head_dim)
        allowed = visible(
            local_pos,
            local_doc,
            lax.dynamic_slice_in_dim(fold_key_pos, first_row, fold_block_rows, 0),
            lax.dynamic_slice_in_dim(fold_key_doc, first_row, fold_block_rows, 1),
        )
        scores = (
            jnp.einsum(
                "bqhd,bkhd->bqhk", query_heads, key_block, preferred_element_type=jnp.float32
            )
            * score_scale
        )
        probs = jnp.where(allowed, jnp.exp(scores - log_total[..., None]), 0.0)
        d_probs = jnp.einsum(
            "bqhd,bkhd->bqhk", d_attn_heads, value_block, preferred_element_type=jnp.float32
        )
        d_scores = (probs * (d_probs - delta[..., None])).astype(jnp.bfloat16)
        return (
            grad_query
            + jnp.einsum("bqhk,bkhd->bqhd", d_scores, key_block, preferred_element_type=jnp.float32)
            * score_scale
        )

    grad_query = lax.fori_loop(
        0,
        piece_rows // fold_block_rows,
        one_block,
        jnp.zeros((seq_group, seq_dev, heads, head_dim), jnp.float32),
    )
    stats_all = (
        lax.all_gather(log_total, "ctx", axis=1, tiled=True),
        lax.all_gather(delta, "ctx", axis=1, tiled=True),
    )
    totals_every = stats_all[0]
    deltas_every = stats_all[1]

    def fold_keys(carried, received, first_index):
        query_piece, grad_piece = received
        piece_rows = query_piece.shape[1]
        query_pos = row_positions(span_order, first_index, piece_rows, seq_dev, span_rows)
        query_doc = docs_for(query_pos)
        block_rows = piece_rows // split_count(piece_rows, 1024)

        def one_block(block_index, running):
            grad_key, grad_value = running
            first_row = block_index * block_rows
            query_block = lax.dynamic_slice_in_dim(query_piece, first_row, block_rows, 1).reshape(
                seq_group, block_rows, heads, head_dim
            )
            grad_block = lax.dynamic_slice_in_dim(grad_piece, first_row, block_rows, 1).reshape(
                seq_group, block_rows, heads, head_dim
            )
            total_block = lax.dynamic_slice_in_dim(totals_every, first_row, block_rows, 1)
            delta_block = lax.dynamic_slice_in_dim(deltas_every, first_row, block_rows, 1)
            allowed = visible(
                lax.dynamic_slice_in_dim(query_pos, first_row, block_rows, 0),
                lax.dynamic_slice_in_dim(query_doc, first_row, block_rows, 1),
                local_pos,
                local_doc,
            )
            scores = (
                jnp.einsum(
                    "bqhd,bkhd->bqhk", query_block, key_heads, preferred_element_type=jnp.float32
                )
                * score_scale
            )
            probs = jnp.where(allowed, jnp.exp(scores - total_block[..., None]), 0.0)
            grad_value = grad_value + jnp.einsum(
                "bqhk,bqhd->bkhd",
                probs.astype(jnp.bfloat16),
                grad_block,
                preferred_element_type=jnp.float32,
            )
            d_probs = jnp.einsum(
                "bqhd,bkhd->bqhk", grad_block, value_heads, preferred_element_type=jnp.float32
            )
            d_scores = (probs * (d_probs - delta_block[..., None])).astype(jnp.bfloat16)
            grad_key = (
                grad_key
                + jnp.einsum(
                    "bqhk,bqhd->bkhd", d_scores, query_block, preferred_element_type=jnp.float32
                )
                * score_scale
            )
            return (grad_key, grad_value)

        return lax.fori_loop(0, piece_rows // block_rows, one_block, carried)

    zero_heads = jnp.zeros((seq_group, seq_dev, heads, head_dim), jnp.float32)
    grad_key, grad_value = fold_keys(
        (zero_heads, zero_heads),
        (
            lax.all_gather(query_low, "ctx", axis=1, tiled=True),
            lax.all_gather(d_attn_low, "ctx", axis=1, tiled=True),
        ),
        jnp.int32(0),
    )
    d_projected = jnp.concatenate(
        [
            grad_query.reshape(seq_group, seq_dev, width),
            grad_key.reshape(seq_group, seq_dev, width),
            grad_value.reshape(seq_group, seq_dev, width),
        ],
        axis=-1,
    ).astype(jnp.bfloat16)
    grad_w_qkv = jnp.einsum(
        "btd,bte->de", normed_one, d_projected, preferred_element_type=jnp.float32
    )
    column_sums = jnp.sum(d_projected.astype(jnp.float32), axis=(0, 1))
    grad_qv_bias = jnp.stack([column_sums[:width], column_sums[2 * width :]])
    d_normed_one = jnp.einsum(
        "bte,de->btd", d_projected, weights_back[2], preferred_element_type=jnp.float32
    )
    first_unused, first_pull = jax.vjp(layer_norm, tokens_in, back_gain_one, back_shift_one)
    d_input_part, grad_ln1_gain, grad_ln1_bias = first_pull(d_normed_one)
    d_input = d_resid + d_input_part
    shares = (
        lax.psum_scatter(
            grad_ln1_gain.astype(jnp.bfloat16), "wt", scatter_dimension=0, tiled=True
        ).astype(jnp.float32),
        lax.psum_scatter(
            grad_ln1_bias.astype(jnp.bfloat16), "wt", scatter_dimension=0, tiled=True
        ).astype(jnp.float32),
        lax.psum_scatter(
            grad_w_qkv.astype(jnp.bfloat16), "wt", scatter_dimension=0, tiled=True
        ).astype(jnp.float32),
        lax.psum_scatter(
            grad_qv_bias.astype(jnp.bfloat16), "wt", scatter_dimension=1, tiled=True
        ).astype(jnp.float32),
        lax.psum_scatter(
            grad_w_out.astype(jnp.bfloat16), "wt", scatter_dimension=0, tiled=True
        ).astype(jnp.float32),
        lax.psum_scatter(
            grad_out_bias.astype(jnp.bfloat16), "wt", scatter_dimension=0, tiled=True
        ).astype(jnp.float32),
        lax.psum_scatter(
            grad_ln2_gain.astype(jnp.bfloat16), "wt", scatter_dimension=0, tiled=True
        ).astype(jnp.float32),
        lax.psum_scatter(
            grad_ln2_bias.astype(jnp.bfloat16), "wt", scatter_dimension=0, tiled=True
        ).astype(jnp.float32),
        lax.psum_scatter(
            grad_w_fc.astype(jnp.bfloat16), "wt", scatter_dimension=0, tiled=True
        ).astype(jnp.float32),
        lax.psum_scatter(
            grad_fc_bias.astype(jnp.bfloat16), "wt", scatter_dimension=0, tiled=True
        ).astype(jnp.float32),
        lax.psum_scatter(
            grad_w_proj.astype(jnp.bfloat16), "wt", scatter_dimension=0, tiled=True
        ).astype(jnp.float32),
        lax.psum_scatter(
            grad_proj_bias.astype(jnp.bfloat16), "wt", scatter_dimension=0, tiled=True
        ).astype(jnp.float32),
    )
    totals = lax.psum(
        (
            shares[0],
            shares[1],
            shares[2],
            shares[3],
            shares[4],
            shares[5],
            shares[6],
            shares[7],
            shares[8],
            shares[9],
            shares[10],
            shares[11],
        ),
        "ctx",
    )
    return (
        block_out,
        d_input,
        totals[0],
        totals[1],
        totals[2],
        totals[3],
        totals[4],
        totals[5],
        totals[6],
        totals[7],
        totals[8],
        totals[9],
        totals[10],
        totals[11],
    )


def solution(mesh):
    placed = (
        P("wt", "ctx", None),
        P(),
        P("wt", None),
        P("wt"),
        P("wt"),
        P("wt", None),
        P(None, "wt"),
        P("wt", None),
        P("wt"),
        P("wt"),
        P("wt"),
        P("wt", None),
        P("wt"),
        P("wt", None),
        P("wt"),
        P("wt", "ctx", None),
    )
    fast = dict(mesh.shape) == {"ctx": 16, "wt": 2}
    return jax.shard_map(
        by_owner if fast else per_device,
        mesh=mesh,
        in_specs=placed,
        out_specs=(
            P("wt", "ctx", None),
            P("wt", "ctx", None),
            P("wt"),
            P("wt"),
            P("wt", None),
            P(None, "wt"),
            P("wt", None),
            P("wt"),
            P("wt"),
            P("wt"),
            P("wt", None),
            P("wt"),
            P("wt", None),
            P("wt"),
        ),
        check_vma=False,
    )
```

```python
import functools

import jax
import jax.numpy as jnp
from jax import lax
from jax.experimental import pallas as pl
from jax.experimental.pallas import tpu as pltpu
from jax.sharding import PartitionSpec as P

HEADS = 12

branch_scale = 0.14433756729740643
neg_large = -1e30
f32 = jnp.float32
bf16 = jnp.bfloat16
VMEM = pltpu.VMEM
vmem_cap = 56 << 20

GROUPS = 4
TILE = 128
PAD = 256
PACK = 640

pair = [(0, 1), (1, 0)]
flips = [[(i, i ^ flip) for i in range(16)] for flip in range(16)]


def z_shift(step):
    return [(i, (i // 4 + step) % 4 * 4 + i % 4) for i in range(16)]


def other_core(value):
    return lax.ppermute(value, "wt", pair)


def send_flip(value, flip):
    return lax.ppermute(value, "ctx", flips[flip])


def send_z(value, step):
    return lax.ppermute(value, "ctx", z_shift(step))


planes = [[4 * i + j for j in range(4)] for i in range(4)]


def swap_plane(value):
    return lax.all_to_all(value, "ctx", 0, 0, axis_index_groups=planes, tiled=True)


def row(value, index):
    return lax.dynamic_index_in_dim(value, index, 0, keepdims=False)


def sum_low(*terms):
    total = terms[0].astype(f32)
    for term in terms[1:]:
        total = total + term.astype(f32)
    return total.astype(bf16)


def after(value, *others):
    return lax.optimization_barrier((value,) + others)[0]


def work(micros):
    return pl.CostEstimate(flops=int(micros * 1e6), bytes_accessed=1 << 12, transcendentals=0)


def busy(micros):
    return pl.CostEstimate(flops=int(micros * 1.1e9), bytes_accessed=1 << 20, transcendentals=0)


def full_spec(shape):
    zeros = (0,) * len(shape)
    return pl.BlockSpec(shape, lambda *unused: zeros)


def dot(left, right, dims):
    return lax.dot_general(left, right, (dims, ((), ())), preferred_element_type=f32)


def norm_parts(rows):
    center = jnp.mean(rows, axis=-1, keepdims=True)
    moved = rows - center
    spread = jnp.mean(moved * moved, axis=-1, keepdims=True)
    inverse = lax.rsqrt(spread + 1e-05)
    return moved * inverse, inverse


def joined(own, oth, core):
    return jnp.concatenate([jnp.where(core == 0, own, oth), jnp.where(core == 0, oth, own)], axis=1)


def of_group(vector, group):
    picked = jnp.zeros((1, 192), f32)
    for g in range(GROUPS):
        picked = jnp.where(group == g, vector[:, 192 * g : 192 * (g + 1)], picked)
    return picked


def project_kernel(
    order_ref, where_ref, a_ref, b_ref, c_ref, d_ref, own_ref, oth_ref, small_own_ref, small_oth_ref,
    x_ref, h_ref, q_ref, kv_ref, weight_ref,
    held,
):
    group, core = where_ref[1], where_ref[2]
    half = own_ref.shape[0]
    for source, at in ((own_ref, core), (oth_ref, 1 - core)):
        rows = pl.ds(pl.multiple_of(at * half, half), half)
        for i in range(3):
            window = source[:, 384 * i : 384 * (i + 1)].astype(f32)
            part = jnp.where(group % 2 == 0, window[:, :192], window[:, 192:])
            weight_ref[rows, PAD * i : PAD * (i + 1)] = jnp.concatenate(
                [part, jnp.zeros((half, PAD - 192), f32)], axis=1
            ).astype(bf16)
    for index, source in enumerate((a_ref, b_ref, c_ref, d_ref)):
        held[4 * index : 4 * index + 4] = source[...]

    small = joined(small_own_ref[0:4, :], small_oth_ref[0:4, :], core)
    lane = lax.broadcasted_iota(jnp.int32, (1, PAD - 192), 1)
    none = jnp.zeros((1, PAD - 192), f32)
    bias = jnp.concatenate(
        [
            of_group(small[2:3], group), none, jnp.zeros((1, PAD), f32),
            of_group(small[3:4], group), (lane == 0).astype(f32),
        ],
        axis=1,
    )
    step = 4 * held.shape[1]
    for i in range(4):
        at = slice(step * i, step * (i + 1))
        rows = jnp.concatenate([held[order_ref[4 * i + t]].astype(f32) for t in range(4)], axis=0)
        x_ref[at, :] = rows.astype(bf16)
        normed, unused = norm_parts(rows)
        low = (normed * small[0:1] + small[1:2]).astype(bf16)
        h_ref[at, :] = low
        out = dot(low, weight_ref[...], ((1,), (0,))) + bias
        q_ref[at, :] = (out[:, :PAD].astype(bf16) * 0.125).astype(bf16)
        kv_ref[at, :] = out[:, PAD:].astype(bf16)


def project(order, where, pieces, own, oth, small_own, small_oth):
    blocks, span_rows, width = pieces[0].shape
    spans = 4 * blocks
    rows = spans * span_rows
    return pl.pallas_call(
        project_kernel,
        in_specs=[pl.BlockSpec(memory_space=pltpu.SMEM)] * 2
        + [pl.BlockSpec(memory_space=pltpu.VMEM)] * 8,
        out_specs=[pl.BlockSpec(memory_space=pltpu.VMEM)] * 5,
        out_shape=[
            jax.ShapeDtypeStruct((rows, width), bf16),
            jax.ShapeDtypeStruct((rows, width), bf16),
            jax.ShapeDtypeStruct((rows, PAD), bf16),
            jax.ShapeDtypeStruct((rows, 2 * PAD), bf16),
            jax.ShapeDtypeStruct((width, 3 * PAD), bf16),
        ],
        scratch_shapes=[VMEM((spans, span_rows, width), bf16)],
        compiler_params=pltpu.CompilerParams(vmem_limit_bytes=vmem_cap),
        cost_estimate=busy(6),
        name="project",
    )(order, where, *pieces, own, oth, small_own, small_oth)


def middle_kernel(
    where_ref, attn_ref, x_ref, cot_ref, d_mlp_ref, grad_own_ref, proj_oth_ref, out_own_ref, out_oth_ref, fc_own_ref, fc_oth_ref,
    small_own_ref, small_oth_ref,
    resid_ref, attn_own_ref, attn_oth_ref, normed_own_ref, normed_oth_ref, hidden_own_ref, hidden_oth_ref, pre_ref, d_resid_ref, d_branch_ref, send_ref,
    branch_sum_ref, gain_sum_ref, shift_sum_ref, mlp_sum_ref, pre_sum_ref,
    back, bias_fc, w_out_ref, w_fc_ref,
):
    core = where_ref[2]
    for own, oth, whole in ((out_own_ref, out_oth_ref, w_out_ref), (fc_own_ref, fc_oth_ref, w_fc_ref)):
        rows = own.shape[0]
        whole[pl.ds(pl.multiple_of(core * rows, rows), rows), :] = own[...]
        whole[pl.ds(pl.multiple_of((1 - core) * rows, rows), rows), :] = oth[...]
    small = joined(small_own_ref[...], small_oth_ref[...], core)
    half = small_own_ref.shape[1]
    gain = small[5:6]
    for i in range(4):
        bias_fc[:, half * i : half * (i + 1)] = jnp.where(
            core == 0, small_own_ref[8 + i : 9 + i], small_oth_ref[8 + i : 9 + i]
        )
        bias_fc[:, half * (4 + i) : half * (5 + i)] = jnp.where(
            core == 0, small_oth_ref[8 + i : 9 + i], small_own_ref[8 + i : 9 + i]
        )
    attn = jnp.concatenate([attn_ref[g].astype(f32) for g in range(GROUPS)], axis=1).astype(bf16)
    half = small_own_ref.shape[1]
    attn_own_ref[...] = jnp.where(core == 0, attn[:, :half], attn[:, half:])
    attn_oth_ref[...] = jnp.where(core == 0, attn[:, half:], attn[:, :half])
    cot = cot_ref[...].astype(f32)
    branch = dot(attn, w_out_ref[...], ((1,), (0,))) + small[4:5]
    resid = x_ref[...].astype(f32) + branch_scale * branch
    resid_ref[...] = resid
    unit, inverse = norm_parts(resid)
    low = (unit * gain + small[6:7]).astype(bf16)
    normed_own_ref[...] = jnp.where(core == 0, low[:, :half], low[:, half:])
    normed_oth_ref[...] = jnp.where(core == 0, low[:, half:], low[:, :half])
    back[...] = jnp.zeros_like(back)
    wide = 512

    def columns(hidden_grad, hidden_ref, first, t, carry):
        here = pl.ds(pl.multiple_of(t * wide, wide), wide)
        at = pl.ds(pl.multiple_of(first + t * wide, wide), wide)
        weight = w_fc_ref[:, at]
        u = dot(low, weight, ((1,), (0,))) + bias_fc[:, at]
        square = u * u
        th = jnp.tanh(0.7978845608028654 * (u + 0.044715 * (square * u)))
        one = 0.5 * (1.0 + th)
        hidden_ref[:, here] = (u * one).astype(bf16)
        slope = one + 0.5 * u * (1.0 - th * th) * (0.7978845608028654 * (1.0 + 0.134145 * square))
        pre = (hidden_grad(here) * slope).astype(bf16)
        pre_ref[:, at] = pre
        pre_sum_ref[:, at] = jnp.sum(pre.astype(f32), axis=0, keepdims=True)
        back[...] += dot(pre, weight, ((1,), (1,)))
        return carry

    span = grad_own_ref.shape[1]
    lax.fori_loop(
        0, span // wide, functools.partial(columns, lambda here: grad_own_ref[:, here], hidden_own_ref, core * span), 0
    )
    lax.fori_loop(
        0, span // wide,
        functools.partial(
            columns,
            lambda here: dot(d_mlp_ref[...], proj_oth_ref[here, :], ((1,), (1,))),
            hidden_oth_ref,
            (1 - core) * span,
        ),
        0,
    )
    d_normed = back[...]
    gain_sum_ref[...] = jnp.sum(d_normed * unit, axis=0, keepdims=True)
    shift_sum_ref[...] = jnp.sum(d_normed, axis=0, keepdims=True)
    scaled = d_normed * gain
    part = scaled - jnp.mean(scaled, axis=-1, keepdims=True)
    part = part - unit * jnp.mean(scaled * unit, axis=-1, keepdims=True)
    d_resid = cot + inverse * part
    d_resid_ref[...] = d_resid
    d_branch = (branch_scale * d_resid).astype(bf16)
    d_branch_ref[...] = d_branch
    branch_sum_ref[...] = jnp.sum(d_branch.astype(f32), axis=0, keepdims=True)
    mlp_sum_ref[...] = jnp.sum(d_mlp_ref[...].astype(f32), axis=0, keepdims=True)
    d_attn = dot(d_branch, w_out_ref[...], ((1,), (1,)))
    feats = send_ref.shape[2]
    for g in range(GROUPS):
        send_ref[g] = d_attn[:, feats * g : feats * (g + 1)].astype(bf16)


def middle(
    attn, x, cot, d_mlp, grad_own, proj_oth, out_own, out_oth, fc_own, fc_oth, where, small_own, small_oth
):
    groups, rows, feats = attn.shape
    width, wide = out_own.shape[1], fc_own.shape[1]
    shapes = [
        ((rows, width), f32), ((rows, width // 2), bf16), ((rows, width // 2), bf16),
        ((rows, width // 2), bf16), ((rows, width // 2), bf16), ((rows, wide // 2), bf16),
        ((rows, wide // 2), bf16),
        ((rows, wide), bf16), ((rows, width), f32), ((rows, width), bf16), (attn.shape, bf16),
        ((1, width), f32), ((1, width), f32), ((1, width), f32), ((1, width), f32), ((1, wide), f32),
    ]
    return pl.pallas_call(
        middle_kernel,
        in_specs=[pl.BlockSpec(memory_space=pltpu.SMEM)]
        + [pl.BlockSpec(memory_space=pltpu.VMEM)] * 12,
        out_specs=[pl.BlockSpec(memory_space=pltpu.VMEM)] * len(shapes),
        out_shape=[jax.ShapeDtypeStruct(shape, kind) for shape, kind in shapes],
        scratch_shapes=[
            VMEM((rows, width), f32),
            VMEM((1, wide), f32),
            VMEM((width, width), bf16),
            VMEM((width, wide), bf16),
        ],
        compiler_params=pltpu.CompilerParams(vmem_limit_bytes=vmem_cap),
        cost_estimate=work(12),
        name="middle",
    )(
        where, attn, x, cot, d_mlp, grad_own, proj_oth, out_own, out_oth, fc_own, fc_oth, small_own, small_oth
    )


def pack_kernel(where_ref, gain_ref, shift_ref, bias_ref, *refs):
    sums, own_ref, oth_ref = refs[:5], refs[5], refs[6]
    group, core = where_ref[1], where_ref[2]
    half = own_ref.shape[1]

    def spread(part):
        none = jnp.zeros((1, 192), f32)
        return jnp.concatenate([jnp.where(group == g, part, none) for g in range(GROUPS)], axis=1)

    vectors = [
        gain_ref[...], shift_ref[...],
        spread(bias_ref[:, :192]), spread(bias_ref[:, 2 * PAD : 2 * PAD + 192]),
    ]
    vectors += [r[...] for r in sums[:4]]
    for index, vector in enumerate(vectors):
        low, high = vector[:, :half], vector[:, half:]
        own_ref[index : index + 1, :] = jnp.where(core == 0, low, high)
        oth_ref[index : index + 1, :] = jnp.where(core == 0, high, low)
    wide = sums[4][...]
    for index in range(4):
        low = wide[:, half * index : half * (index + 1)]
        high = wide[:, half * (index + 4) : half * (index + 5)]
        own_ref[8 + index : 9 + index, :] = jnp.where(core == 0, low, high)
        oth_ref[8 + index : 9 + index, :] = jnp.where(core == 0, high, low)


def pack(where, gain, shift, bias, sums):
    half = gain.shape[1] // 2
    return pl.pallas_call(
        pack_kernel,
        in_specs=[pl.BlockSpec(memory_space=pltpu.SMEM)]
        + [pl.BlockSpec(memory_space=pltpu.VMEM)] * 8,
        out_specs=[pl.BlockSpec(memory_space=pltpu.VMEM)] * 2,
        out_shape=[jax.ShapeDtypeStruct((12, half), f32)] * 2,
        cost_estimate=work(1),
        name="pack",
    )(where, gain, shift, bias, *sums)


def by_head(tile):
    lane = lax.broadcasted_iota(jnp.int32, tile.shape, 1)
    zero = jnp.zeros_like(tile)
    return jnp.concatenate(
        [jnp.where((lane >= 64 * h) & (lane < 64 * h + 64), tile, zero) for h in range(3)], axis=0
    )


def by_head_t(tile):
    flipped = tile.T
    feat = lax.broadcasted_iota(jnp.int32, flipped.shape, 0)
    zero = jnp.zeros_like(flipped)
    return jnp.concatenate(
        [jnp.where((feat >= 64 * h) & (feat < 64 * h + 64), flipped, zero) for h in range(3)], axis=1
    )


def tile_rows(index):
    return pl.ds(pl.multiple_of(index * TILE, TILE), TILE)


def tile_pair(plan_ref, i, step, tiles):
    first = plan_ref[0, i] + 2 * step
    beyond = jnp.where(first + 1 < plan_ref[1, i], 0, 1 << 20)
    second = jnp.minimum(first + 1, tiles - 1)
    return tile_rows(first), tile_rows(second), beyond


def pair_rows(own_ref, oth_ref, first, second, lanes):
    return jnp.concatenate(
        [own_ref[first, lanes], oth_ref[first, lanes], own_ref[second, lanes], oth_ref[second, lanes]],
        axis=0,
    )


def pair_columns(own_ref, oth_ref, first, second):
    return jnp.concatenate(
        [own_ref[:, first], oth_ref[:, first], own_ref[:, second], oth_ref[:, second]], axis=1
    )


def visible_pair(kpos_ref, first, second, beyond, meta):
    keys = jnp.concatenate(
        [
            kpos_ref[0, first, :],
            kpos_ref[1, first, :],
            kpos_ref[0, second, :] + beyond,
            kpos_ref[1, second, :] + beyond,
        ],
        axis=0,
    )
    keys = jnp.concatenate([keys, keys, keys], axis=1)
    return (keys <= meta[0:1, :]) & (keys >= meta[1:2, :])


def pairs_of(plan_ref, i):
    return (plan_ref[1, i] - plan_ref[0, i] + 1) // 2


def attend_kernel(
    plan_ref, q_ref, own_ref, oth_ref, kpos_ref, meta_ref,
    o_ref, lse_ref, out_ref,
    vown, voth, stack, acc, top, held,
):
    spans, span_rows, feats = out_ref.shape
    tiles = q_ref.shape[0] // TILE
    keys_step = 4 * TILE
    vown[...] = own_ref[:, PAD:].T
    voth[...] = oth_ref[:, PAD:].T

    def one_tile(i, carry):
        here = tile_rows(i)
        stack[...] = by_head_t(q_ref[here, :])
        meta = meta_ref[i]
        acc[...] = jnp.zeros_like(acc)
        top[...] = jnp.full_like(top, neg_large)

        def score(step, inner):
            first, second, beyond = tile_pair(plan_ref, i, step, tiles)
            keys = pair_rows(own_ref, oth_ref, first, second, slice(0, PAD))
            scores = dot(keys, stack[...], ((1,), (0,)))
            allowed = visible_pair(kpos_ref, first, second, beyond, meta)
            scores = jnp.where(allowed, scores, neg_large)
            held[pl.ds(pl.multiple_of(step * keys_step, keys_step), keys_step), :] = scores
            best = jnp.max(scores.reshape(keys_step // 8, 8, scores.shape[1]), axis=0)
            top[...] = jnp.maximum(top[...], best)
            return inner

        lax.fori_loop(0, pairs_of(plan_ref, i), score, 0)
        peak = jnp.max(top[...], axis=0, keepdims=True)

        def weigh(step, inner):
            first, second, unused = tile_pair(plan_ref, i, step, tiles)
            scores = held[pl.ds(pl.multiple_of(step * keys_step, keys_step), keys_step), :]
            probs = jnp.exp(scores - peak).astype(bf16)
            vals = pair_columns(vown, voth, first, second)
            acc[...] += dot(vals, probs, ((1,), (0,)))
            return inner

        lax.fori_loop(0, pairs_of(plan_ref, i), weigh, 0)
        total = acc[192:193, :]
        lse_ref[i] = peak + jnp.log(total)
        parts = [
            acc[64 * h : 64 * h + 64, TILE * h : TILE * h + TILE]
            / total[:, TILE * h : TILE * h + TILE]
            for h in range(3)
        ]
        heads_t = jnp.concatenate(parts + [jnp.zeros((64, TILE), f32)], axis=0)
        o_ref[here, :] = heads_t.T
        return carry

    lax.fori_loop(0, tiles, one_tile, 0)
    for a in range(spans):
        out_ref[plan_ref[2, a]] = o_ref[span_rows * a : span_rows * (a + 1), :feats].astype(bf16)


def attend(plan, q, own, oth, kpos, meta, spans):
    rows = q.shape[0]
    tiles = rows // TILE
    wide = 3 * TILE
    return pl.pallas_call(
        attend_kernel,
        in_specs=[pl.BlockSpec(memory_space=pltpu.SMEM)]
        + [pl.BlockSpec(memory_space=pltpu.VMEM)] * 5,
        out_specs=[pl.BlockSpec(memory_space=pltpu.VMEM)] * 3,
        out_shape=[
            jax.ShapeDtypeStruct((rows, PAD), f32),
            jax.ShapeDtypeStruct((tiles, 1, wide), f32),
            jax.ShapeDtypeStruct((spans, rows // spans, 192), bf16),
        ],
        scratch_shapes=[
            VMEM((PAD, rows), bf16),
            VMEM((PAD, rows), bf16),
            VMEM((PAD, wide), bf16),
            VMEM((PAD, wide), f32),
            VMEM((8, wide), f32),
            VMEM((2 * rows + 2 * TILE, wide), f32),
        ],
        compiler_params=pltpu.CompilerParams(vmem_limit_bytes=vmem_cap),
        cost_estimate=work(15),
        name="attend",
    )(plan, q, own, oth, kpos, meta)


def attend_back_kernel(
    plan_ref, q_ref, own_ref, oth_ref, kpos_ref, meta_ref, grad_ref, o_ref, lse_ref,
    dq_ref, down_ref, doth_ref,
    grads, kown, koth, acc_oth, stack, gstack, stack_t, gstack_t, dq_t,
):
    spans, span_rows, feats = grad_ref.shape
    tiles = q_ref.shape[0] // TILE
    kown[...] = own_ref[:, :PAD].T
    koth[...] = oth_ref[:, :PAD].T
    down_ref[...] = jnp.zeros_like(down_ref)
    acc_oth[...] = jnp.zeros_like(acc_oth)
    grads[:, 128:] = jnp.zeros((grads.shape[0], PAD - 128), f32)
    for a in range(spans):
        grads[span_rows * a : span_rows * (a + 1), :feats] = grad_ref[plan_ref[2, a]].astype(f32)

    def one_tile(i, carry):
        here = tile_rows(i)
        grad = grads[here, :]
        grad_low = grad.astype(bf16)
        stack[...] = by_head(q_ref[here, :])
        gstack[...] = by_head(grad_low)
        stack_t[...] = by_head_t(q_ref[here, :])
        gstack_t[...] = by_head_t(grad_low)
        product = (grad * o_ref[here, :]).T
        delta = jnp.concatenate(
            [jnp.sum(product[64 * h : 64 * h + 64], axis=0, keepdims=True) for h in range(3)], axis=1
        )
        lse = lse_ref[i]
        meta = meta_ref[i]
        dq_t[...] = jnp.zeros_like(dq_t)

        def one(step, inner):
            first, second, beyond = tile_pair(plan_ref, i, step, tiles)
            keys = pair_rows(own_ref, oth_ref, first, second, slice(0, PAD))
            vals = pair_rows(own_ref, oth_ref, first, second, slice(PAD, 2 * PAD))
            scores = dot(keys, stack_t[...], ((1,), (0,)))
            allowed = visible_pair(kpos_ref, first, second, beyond, meta)
            probs = jnp.where(allowed, jnp.exp(scores - lse), 0.0)
            d_probs = dot(vals, gstack_t[...], ((1,), (0,)))
            d_scores = (probs * (d_probs - delta)).astype(bf16)
            d_vals = dot(probs.astype(bf16), gstack[...], ((1,), (0,)))
            d_keys = dot(d_scores, stack[...], ((1,), (0,)))
            down_ref[first, :PAD] += d_keys[:TILE]
            down_ref[first, PAD:] += d_vals[:TILE]
            acc_oth[first, :PAD] += d_keys[TILE : 2 * TILE]
            acc_oth[first, PAD:] += d_vals[TILE : 2 * TILE]
            down_ref[second, :PAD] += d_keys[2 * TILE : 3 * TILE]
            down_ref[second, PAD:] += d_vals[2 * TILE : 3 * TILE]
            acc_oth[second, :PAD] += d_keys[3 * TILE :]
            acc_oth[second, PAD:] += d_vals[3 * TILE :]
            dq_t[...] += dot(pair_columns(kown, koth, first, second), d_scores, ((1,), (0,)))
            return inner

        lax.fori_loop(0, pairs_of(plan_ref, i), one, 0)
        parts = [dq_t[64 * h : 64 * h + 64, TILE * h : TILE * h + TILE] for h in range(3)]
        heads_t = jnp.concatenate(parts + [jnp.zeros((64, TILE), f32)], axis=0) * 0.125
        dq_ref[here, :] = heads_t.T.astype(bf16)
        return carry

    lax.fori_loop(0, tiles, one_tile, 0)
    doth_ref[...] = acc_oth[...].astype(bf16)


def attend_back(plan, q, own, oth, kpos, meta, grad, o, lse):
    rows = q.shape[0]
    wide = 3 * TILE
    return pl.pallas_call(
        attend_back_kernel,
        in_specs=[pl.BlockSpec(memory_space=pltpu.SMEM)]
        + [pl.BlockSpec(memory_space=pltpu.VMEM)] * 8,
        out_specs=[pl.BlockSpec(memory_space=pltpu.VMEM)] * 3,
        out_shape=[
            jax.ShapeDtypeStruct((rows, PAD), bf16),
            jax.ShapeDtypeStruct((rows, 2 * PAD), f32),
            jax.ShapeDtypeStruct((rows, 2 * PAD), bf16),
        ],
        scratch_shapes=[
            VMEM((rows, PAD), f32),
            VMEM((PAD, rows), bf16),
            VMEM((PAD, rows), bf16),
            VMEM((rows, 2 * PAD), f32),
            VMEM((wide, PAD), bf16),
            VMEM((wide, PAD), bf16),
            VMEM((PAD, wide), bf16),
            VMEM((PAD, wide), bf16),
            VMEM((PAD, wide), f32),
        ],
        compiler_params=pltpu.CompilerParams(vmem_limit_bytes=vmem_cap),
        cost_estimate=busy(24),
        name="attend_back",
    )(plan, q, own, oth, kpos, meta, grad, o, lse)


def unproject_kernel(
    place_ref, x_ref, dq_ref, down_ref, doth_ref, weight_ref,
    pieces_ref, grad_ref, gain_ref, shift_ref, bias_ref,
):
    i = pl.program_id(0)
    span_rows = pieces_ref.shape[1]

    @pl.when(i == 0)
    def _():
        gain_ref[...] = jnp.zeros_like(gain_ref)
        shift_ref[...] = jnp.zeros_like(shift_ref)
        bias_ref[...] = jnp.zeros_like(bias_ref)

    normed, unused = norm_parts(x_ref[...].astype(f32))
    dkv = (down_ref[...] + doth_ref[...].astype(f32)).astype(bf16)
    grad = jnp.concatenate([dq_ref[...], dkv], axis=1)
    grad_ref[...] = jnp.concatenate(
        [grad[:, :192], grad[:, PAD : PAD + 192], grad[:, 2 * PAD : 2 * PAD + 192], grad[:, 192:PAD]],
        axis=1,
    )
    bias_ref[...] += jnp.sum(grad.astype(f32), axis=0, keepdims=True)
    back = dot(grad, weight_ref[...], ((1,), (1,)))
    gain_ref[...] += jnp.sum(back * normed, axis=0, keepdims=True)
    shift_ref[...] += jnp.sum(back, axis=0, keepdims=True)
    for t in range(4):
        pieces_ref[place_ref[4 * i + t]] = back[span_rows * t : span_rows * (t + 1)].astype(bf16)


def unproject(place, x, dq, down, doth, weight, spans):
    rows, width = x.shape
    step = rows // 4
    pieces = jax.ShapeDtypeStruct((spans, rows // spans, width), bf16)
    grid_spec = pltpu.PrefetchScalarGridSpec(
        num_scalar_prefetch=1,
        grid=(4,),
        in_specs=[
            pl.BlockSpec((step, width), lambda i, *unused: (i, 0)),
            pl.BlockSpec((step, PAD), lambda i, *unused: (i, 0)),
            pl.BlockSpec((step, 2 * PAD), lambda i, *unused: (i, 0)),
            pl.BlockSpec((step, 2 * PAD), lambda i, *unused: (i, 0)),
            full_spec((width, 3 * PAD)),
        ],
        out_specs=[
            full_spec(pieces.shape),
            pl.BlockSpec((step, PACK), lambda i, *unused: (i, 0)),
            full_spec((1, width)),
            full_spec((1, width)),
            full_spec((1, 3 * PAD)),
        ],
    )
    return pl.pallas_call(
        unproject_kernel,
        grid_spec=grid_spec,
        out_shape=[
            pieces,
            jax.ShapeDtypeStruct((rows, PACK), bf16),
            jax.ShapeDtypeStruct((1, width), f32),
            jax.ShapeDtypeStruct((1, width), f32),
            jax.ShapeDtypeStruct((1, 3 * PAD), f32),
        ],
        compiler_params=pltpu.CompilerParams(vmem_limit_bytes=vmem_cap),
        cost_estimate=busy(8),
        name="unproject",
    )(place, x, dq, down, doth, weight)


def halve(value, bit):
    value = value.reshape(2, value.shape[0] // 2, value.shape[1])
    return row(value, bit), row(value, 1 - bit)


def reduce_z(value, z):
    value = value.reshape(4, value.shape[0] // 4, value.shape[1])
    return row(value, z), [row(value, (z + k) % 4) for k in (1, 2, 3)]


def over_z(sends):
    return [send_z(sends[k - 1], k) for k in (1, 2, 3)]


def reduce_plane(value, group):
    value = value.reshape(4, value.shape[0] // 4, value.shape[1])
    return row(value, group), [row(value, group ^ f) for f in (1, 2, 3)]


def over_plane(sends):
    return [send_flip(sends[f - 1], f) for f in (1, 2, 3)]


def gather_z(value):
    pair = jnp.stack([value, send_flip(value, 8)])
    return jnp.concatenate([pair, send_flip(pair, 4)], axis=0)


def spread_once(left, right):
    return jnp.concatenate([left, send_flip(left, 1)], axis=0), jnp.concatenate(
        [right, send_flip(right, 2)], axis=0
    )


def spread_twice(left, right):
    return left, send_flip(left, 2), right, send_flip(right, 1)


def cut_lanes(value, at):
    return value[:, :, :at], value[:, :, at:]


def entry(refs, side, f, k):
    if side == 0:
        return refs[f // 2][4 * (f % 2) + k].astype(f32)
    return refs[2 + f % 2][4 * (f // 2) + k].astype(f32)


def block_of(z, k):
    return ((z & 1) ^ (k >> 1)) * 2 + ((z >> 1) ^ (k & 1))


def chip_of(z, k):
    return z ^ ((k >> 1) + 2 * (k & 1))


def place_proj_kernel(where_ref, *refs):
    parts, out_ref = refs[:4], refs[4]
    z, group = where_ref[0], where_ref[1]
    rows, half = parts[0].shape[1:]
    for f in range(4):
        x, y = (group ^ f) & 1, (group ^ f) >> 1
        for k in range(4):
            at = ((2 * x + y) * 4 + block_of(z, k)) * rows
            out_ref[pl.ds(pl.multiple_of(at, 8), rows), :half] = entry(parts, 0, f, k)
            at = ((2 * y + x) * 4 + block_of(z, k)) * rows
            out_ref[pl.ds(pl.multiple_of(at, 8), rows), half:] = entry(parts, 1, f, k)


def place_rest_kernel(where_ref, *refs):
    parts, fc_ref, out_ref = refs[:4], refs[4], refs[5]
    z, group = where_ref[0], where_ref[1]
    rows, half = parts[0].shape[1:]
    fc_wide = fc_ref.shape[1]
    for f in range(4):
        for k in range(4):
            at = ((group ^ f) * 4 + chip_of(z, k)) * rows
            at = pl.ds(pl.multiple_of(at, 8), rows)
            fc_ref[at, :half] = entry(parts, 0, f, k)
            right = entry(parts, 1, f, k)
            fc_ref[at, half:] = right[:, : fc_wide - half]
            out_ref[at, :] = right[:, fc_wide - half :]


def place_in_kernel(where_ref, *refs):
    parts, in_ref, small_ref, held = refs[:4], refs[4], refs[5], refs[6]
    z, group = where_ref[0], where_ref[1]
    upper = parts[0].shape[1]
    rows = upper + parts[2].shape[1] - 8
    small_ref[...] = jnp.zeros(small_ref.shape, f32)
    for f in range(4):
        for k in range(4):
            block = z ^ k
            held[group ^ f, block, :upper] = entry(parts, 0, f, k)
            right = entry(parts, 1, f, k)
            held[group ^ f, block, upper:rows] = right[:-8]
            small_ref[block] = small_ref[block] + right[-8:]
    for block in range(4):
        for i in range(3):
            at = 192 * i
            columns = [held[g, block, :, at : at + 192] for g in range(4)]
            in_ref[rows * block : rows * (block + 1), 768 * i : 768 * (i + 1)] = jnp.concatenate(
                columns, axis=1
            )


def place(kernel, name, micros, where, parts, shapes, scratch=()):
    return pl.pallas_call(
        kernel,
        in_specs=[pl.BlockSpec(memory_space=pltpu.SMEM)]
        + [pl.BlockSpec(memory_space=pltpu.VMEM)] * len(parts),
        out_specs=[pl.BlockSpec(memory_space=pltpu.VMEM)] * len(shapes),
        out_shape=[jax.ShapeDtypeStruct(shape, f32) for shape in shapes],
        scratch_shapes=list(scratch),
        compiler_params=pltpu.CompilerParams(vmem_limit_bytes=vmem_cap),
        cost_estimate=busy(micros),
        name=name,
    )(where, *parts)


def split_halves(value, w, axis):
    low, high = jnp.split(value, 2, axis)
    return jnp.where(w == 0, low, high), jnp.where(w == 0, high, low)


def grad_dot(left, right):
    return dot(left, right, ((0,), (0,)))


def norm_back(grad, rows, gain):
    normed, inverse = norm_parts(rows)
    scaled = grad * gain
    part = scaled - jnp.mean(scaled, axis=-1, keepdims=True)
    part = part - normed * jnp.mean(scaled * normed, axis=-1, keepdims=True)
    return inverse * part, normed


def by_owner(
    block_input, span_order, doc_lengths, ln1_gain, ln1_bias, w_qkv, qv_bias, w_out, out_bias,
    ln2_gain, ln2_bias, w_fc, fc_bias, w_proj, proj_bias, d_out,
):
    seq_group, seq_dev, width = block_input.shape
    seqs = 2 * seq_group
    span_rows = seq_dev // 2
    chips = span_order.shape[0]
    rows = chips * span_rows
    me = lax.axis_index("ctx")
    w = lax.axis_index("wt")
    z, y, x = me // 4, me // 2 % 2, me % 2
    where = (z, y, x)
    group = me % 4

    second = (row(span_order, me)[0] % 2) != w

    def take_spans(value):
        value = value.reshape(seq_group, 2, span_rows, width)
        keep = jnp.where(second, value[:, 1], value[:, 0])
        give = jnp.where(second, value[:, 0], value[:, 1])
        got = other_core(give)
        return jnp.where(
            w == 0, jnp.concatenate([keep, got], axis=0), jnp.concatenate([got, keep], axis=0)
        )

    def give_spans(value):
        low, high = value[:seq_group], value[seq_group:]
        keep = jnp.where(w == 0, low, high)
        got = other_core(jnp.where(w == 0, high, low))
        first = jnp.where(second, got, keep)
        last = jnp.where(second, keep, got)
        return jnp.concatenate([first, last], axis=1)

    def to_sequence(value):
        got = [send_z(row(value, (z + k) % 4), k) for k in (1, 2, 3)]
        return [row(value, z)] + got

    z_low, z_high = z % 2, z // 2

    def z_first(blocks):
        keep = jnp.stack([row(blocks, z_low + 2 * h) for h in (0, 1)])
        give = jnp.stack([row(blocks, 1 - z_low + 2 * h) for h in (0, 1)])
        return keep, send_flip(give, 4)

    def z_second(keep, got):
        pairs = jnp.stack([keep, got], axis=1)
        here, there = row(pairs, z_high), send_flip(row(pairs, 1 - z_high), 8)
        return jnp.concatenate([here, there], axis=0)

    def by_chip(value):
        return jnp.stack([row(value, (z - s) % 4) for s in range(seqs)])

    def by_source(got):
        return jnp.stack([row(got, z ^ s) for s in range(seqs)])

    kept = to_sequence(take_spans(block_input))
    left, right = jnp.stack(kept[:2]), jnp.stack(kept[2:])
    tokens_low = jnp.concatenate([left, right], axis=0)
    span_order, doc_lengths, d_out, unused = lax.optimization_barrier(
        (span_order, doc_lengths, d_out, (left, right))
    )
    left_x, right_y = send_flip(left, 1), send_flip(right, 2)
    ranks = jnp.arange(rows, dtype=jnp.int32)
    even_pos = 2 * span_rows * (ranks // span_rows) + ranks % span_rows
    own_pos = even_pos + span_rows * w
    oth_pos = even_pos + span_rows * (1 - w)
    kpos = jnp.broadcast_to(jnp.stack([own_pos, oth_pos])[:, :, None], (2, rows, TILE)).astype(jnp.int32)
    left_x, right_y, kpos = lax.optimization_barrier((left_x, right_y, kpos))
    left = jnp.concatenate([left, left_x], axis=0)
    right = jnp.concatenate([right, right_y], axis=0)
    pieces = (left, send_flip(left, 2), right, send_flip(right, 1))
    (
        ln1_gain, ln1_bias, w_qkv, qv_bias, out_bias, ln2_gain, ln2_bias, proj_bias, fc_bias, unused,
    ) = lax.optimization_barrier(
        (
            ln1_gain, ln1_bias, w_qkv, qv_bias, out_bias, ln2_gain, ln2_bias, proj_bias, fc_bias,
            (left, right),
        )
    )
    cot_low = jnp.stack(to_sequence(take_spans(d_out))).reshape(seqs * span_rows, width)
    d_mlp = (branch_scale * cot_low.astype(f32)).astype(bf16)

    chip_ids = jnp.arange(chips, dtype=jnp.int32)
    span_here = jnp.where(span_order[:, 0] % 2 == w, span_order[:, 0], span_order[:, 1]) // 2
    span_ids = jnp.arange(chips, dtype=jnp.int32)
    holder = jnp.sum(
        jnp.where(span_here[None, :] == span_ids[:, None], chip_ids[None, :], 0), axis=1
    ).astype(jnp.int32)
    back_z = (z - holder // 4) % 4
    flip = group ^ (holder % 4)
    order = jnp.where(
        back_z < 2,
        (flip // 2) * 4 + (flip % 2) * 2 + back_z,
        8 + (flip % 2) * 4 + (flip // 2) * 2 + back_z - 2,
    ).astype(jnp.int32)
    order_back = (flip * 4 + back_z).astype(jnp.int32)
    owner = (holder % 4 * 4 + back_z).astype(jnp.int32)

    lengths_oth = other_core(doc_lengths)
    lengths = jnp.where(
        w == 0,
        jnp.concatenate([doc_lengths, lengths_oth], axis=0),
        jnp.concatenate([lengths_oth, doc_lengths], axis=0),
    )
    lengths = row(lengths, z)
    ends = jnp.cumsum(lengths)[:-1]
    starts = jnp.sum(
        jnp.where(own_pos[:, None] >= ends[None, :], lengths[None, :-1], 0), axis=1
    ).astype(jnp.int32)
    tiles = rows // TILE
    own_tiles = own_pos.reshape(tiles, TILE)
    start_tiles = starts.reshape(tiles, TILE)
    meta = jnp.tile(jnp.stack([own_tiles, start_tiles], axis=1), (1, 1, 3)).astype(jnp.int32)
    even_tiles = even_pos.reshape(tiles, TILE)
    low = jnp.sum(
        (even_tiles[None, :, -1] + span_rows < start_tiles[:, 0:1]).astype(jnp.int32), axis=1
    ).astype(jnp.int32)
    high = jnp.sum(
        (even_tiles[None, :, 0] <= own_tiles[:, -1:]).astype(jnp.int32), axis=1
    ).astype(jnp.int32)

    room = jnp.zeros((chips - tiles,), jnp.int32)
    plan = jnp.stack([jnp.concatenate([low, room]), jnp.concatenate([high, room]), owner])

    feats = width // GROUPS
    half = width // 2
    here = jnp.stack([z, group, w]).astype(jnp.int32)
    in_own = jnp.concatenate(
        [
            lax.dynamic_slice_in_dim(w_qkv, width * i + half * (group // 2), half, 1)
            for i in range(3)
        ],
        axis=1,
    )
    in_oth_core = other_core(in_own)
    vectors = [ln1_gain, ln1_bias, qv_bias[0], qv_bias[1], out_bias, ln2_gain, ln2_bias, proj_bias]
    vectors += [fc_bias[half * i : half * (i + 1)] for i in range(4)]
    lines = lax.broadcasted_iota(jnp.int32, (len(vectors), half), 0)
    small = jnp.zeros((len(vectors), half), f32)
    for i, one in enumerate(vectors):
        small = jnp.where(lines == i, jnp.broadcast_to(one.astype(f32), small.shape), small)
    small_oth = other_core(small)

    def vector(index):
        own, oth = small[index : index + 1], small_oth[index : index + 1]
        return jnp.concatenate([jnp.where(w == 0, own, oth), jnp.where(w == 0, oth, own)], axis=1)

    pieces, w_out, w_fc, w_proj, unused = lax.optimization_barrier(
        (pieces, w_out, w_fc, w_proj, (meta, plan, in_oth_core, small_oth, d_mlp))
    )
    out_oth, fc_oth, proj_oth = other_core(w_out), other_core(w_fc), other_core(w_proj)
    x_sorted, normed_one, query, kv_own, weight_in = project(
        order, here, pieces, in_own, in_oth_core, small, small_oth
    )
    query, kv_own, out_oth, fc_oth, proj_oth = lax.optimization_barrier(
        (query, kv_own, out_oth, fc_oth, proj_oth)
    )
    kv_oth = other_core(kv_own)
    attn, lse, attn_send = attend(plan, query, kv_own, kv_oth, kpos, meta, chips)
    attn_got = swap_plane(attn_send.reshape(GROUPS, seqs, span_rows, feats))

    d_mlp = after(d_mlp, attn_send)
    mlp_both = jnp.concatenate([d_mlp, other_core(d_mlp)], axis=0)
    grad_own = dot(d_mlp, w_proj, ((1,), (1,)))
    attn_got = after(attn_got, grad_own, mlp_both).reshape(GROUPS, seqs * span_rows, feats)

    tokens = tokens_low.reshape(seqs * span_rows, width)
    (
        resid, attn_own, attn_oth, normed_own, normed_oth, hidden_own, hidden_oth, d_pre, d_resid, d_branch, d_send, *sums
    ) = middle(
        attn_got, tokens, cot_low, d_mlp, grad_own, proj_oth,
        w_out, out_oth, w_fc, fc_oth, here, small, small_oth,
    )
    d_got = swap_plane(d_send.reshape(GROUPS, seqs, span_rows, feats)).reshape(chips, span_rows, feats)
    hidden_both = jnp.concatenate([hidden_own, other_core(hidden_oth)], axis=0)
    pre_both = jnp.concatenate([d_pre, other_core(d_pre)], axis=0)
    normed_both = jnp.concatenate([normed_own, other_core(normed_oth)], axis=0)
    attn_both = jnp.concatenate([attn_own, other_core(attn_oth)], axis=0)
    low_bit, high_bit = z % 2, z // 2
    branch_both = jnp.concatenate([d_branch, other_core(d_branch)], axis=0)
    hidden_both = after(hidden_both, d_send)
    grad_proj = grad_dot(hidden_both, mlp_both).astype(bf16)
    proj_left, left_send = halve(grad_proj[:, :half], x)
    proj_right, right_send = halve(grad_proj[:, half:], y)
    left_recv, right_recv = send_flip(left_send, 1), send_flip(right_send, 2)
    normed_both, attn_both, d_got, unused = lax.optimization_barrier(
        (normed_both, attn_both, d_got, (left_send, right_send))
    )
    fc_cols = d_pre.shape[1]
    grad_rest = jnp.concatenate(
        [grad_dot(normed_both, pre_both).astype(bf16), grad_dot(attn_both, branch_both).astype(bf16)],
        axis=1,
    )
    rest_keep, rest_sends = reduce_plane(grad_rest, group)
    left_recv, right_recv, unused = lax.optimization_barrier((left_recv, right_recv, rest_sends))
    proj_left, left_send = halve(sum_low(proj_left, left_recv), y)
    proj_right, right_send = halve(sum_low(proj_right, right_recv), x)
    left_recv, right_recv = send_flip(left_send, 2), send_flip(right_send, 1)
    rest_plane = over_plane(rest_sends)

    d_got = after(d_got, left_send, right_send, *rest_sends)
    d_query, d_own, d_oth = attend_back(plan, query, kv_own, kv_oth, kpos, meta, d_got, attn, lse)
    hidden_own, hidden_oth, unused = lax.optimization_barrier((hidden_own, hidden_oth, d_query))
    mlp = dot(hidden_own, w_proj, ((1,), (0,))) + dot(hidden_oth, proj_oth, ((1,), (0,))) + vector(7)
    block_out = (resid + branch_scale * mlp).astype(bf16).reshape(seqs, span_rows, width)
    block_out = by_chip(block_out)
    left_recv, right_recv, rest_plane, d_query, d_oth, block_out = lax.optimization_barrier(
        (left_recv, right_recv, rest_plane, d_query, d_oth, block_out)
    )
    d_recv = other_core(d_oth)
    grad_proj = jnp.concatenate(
        [sum_low(proj_left, left_recv), sum_low(proj_right, right_recv)], axis=1
    )
    proj_keep, proj_send = halve(grad_proj, low_bit)
    proj_recv = send_flip(proj_send, 4)
    rest_keep, rest_sends = reduce_z(sum_low(rest_keep, *rest_plane), z)
    proj_recv, d_recv, rest_sends, block_out = lax.optimization_barrier(
        (proj_recv, d_recv, rest_sends, block_out)
    )
    block_out = z_first(block_out)
    rest_z = over_z(rest_sends)
    proj_keep, proj_send = halve(sum_low(proj_keep, proj_recv), high_bit)
    proj_recv = send_flip(proj_send, 8)
    d_recv = after(d_recv, proj_send)
    d_pieces, d_qkv, part_gain, part_shift, part_bias = unproject(
        order_back, x_sorted, d_query, d_own, d_recv, weight_in, chips
    )
    proj_recv, rest_z, d_pieces, d_qkv, part_gain, part_shift, part_bias, sums, block_out = (
        lax.optimization_barrier(
            (proj_recv, rest_z, d_pieces, d_qkv, part_gain, part_shift, part_bias, sums, block_out)
        )
    )

    proj_shard = sum_low(proj_keep, proj_recv)
    rest_shard = sum_low(rest_keep, *rest_z)
    d_qkv, unused = lax.optimization_barrier((d_qkv, (proj_shard, rest_shard)))
    proj_pair = jnp.stack([proj_shard, send_flip(proj_shard, 8)])
    rest_pair = jnp.stack([rest_shard, send_flip(rest_shard, 8)])
    back_sends = [d_pieces[4 * f : 4 * f + 4] for f in (1, 2, 3)]
    back_x, back_y = send_flip(back_sends[0], 1), send_flip(back_sends[1], 2)
    normed_own, normed_oth = split_halves(normed_one, w, 1)
    in_oth = grad_dot(normed_oth, d_qkv).astype(bf16)
    in_got = other_core(in_oth)
    grads_own, grads_oth = pack(here, part_gain, part_shift, part_bias, sums)
    small_rows = (grads_own + other_core(grads_oth)).astype(bf16).reshape(4, 3, half)
    small_rows = jnp.pad(small_rows, ((0, 0), (0, 5), (0, PACK - half)))
    grad_in = (grad_dot(normed_own, d_qkv) + in_got.astype(f32)).astype(bf16)
    grad_in = jnp.concatenate([grad_in.reshape(4, half // 4, PACK), small_rows], axis=1)
    in_keep, in_send = halve(grad_in.reshape(-1, PACK), high_bit)
    proj_pair, rest_pair, back_x, back_y, back_xy, in_send = lax.optimization_barrier(
        (proj_pair, rest_pair, back_x, back_y, back_sends[2], in_send)
    )
    proj_all = jnp.concatenate([proj_pair, send_flip(proj_pair, 4)], axis=0)
    rest_all = jnp.concatenate([rest_pair, send_flip(rest_pair, 4)], axis=0)
    in_recv = send_flip(in_send, 8)
    back_xy = send_flip(back_xy, 3)
    proj_all, rest_all, in_recv, back_xy = lax.optimization_barrier((proj_all, rest_all, in_recv, back_xy))
    in_keep, in_send = halve(sum_low(in_keep, in_recv), low_bit)
    in_recv = send_flip(in_send, 4)
    proj_once = spread_once(*cut_lanes(proj_all, half))
    rest_once = spread_once(*cut_lanes(rest_all, rest_all.shape[2] // 2))
    proj_once, rest_once, in_recv = lax.optimization_barrier((proj_once, rest_once, in_recv))
    in_shard = sum_low(in_keep, in_recv)
    in_pair = jnp.stack([in_shard, send_flip(in_shard, 4)])
    proj_parts = spread_twice(*proj_once)
    back = sum_low(d_pieces[:4], back_x, back_y, after(back_xy, in_shard))
    block_out, unused = lax.optimization_barrier((block_out, in_shard))
    block_out = z_second(*block_out)
    proj_parts, in_pair, rest_once, back, block_out = lax.optimization_barrier(
        (proj_parts, in_pair, rest_once, back, block_out)
    )
    in_all = jnp.concatenate([in_pair, send_flip(in_pair, 8)], axis=0)
    rest_parts = spread_twice(*rest_once)
    d_first, unused = norm_back(
        back.reshape(seqs * span_rows, width).astype(f32), tokens.astype(f32), vector(0)
    )
    d_input = (d_resid + d_first).astype(bf16).reshape(seqs, span_rows, width)
    d_input = z_first(by_chip(d_input))
    rest_parts, in_all, proj_parts, d_input = lax.optimization_barrier(
        (rest_parts, in_all, proj_parts, d_input)
    )
    in_once = spread_once(in_all[:, :56], in_all[:, 56:])
    in_once, d_input, block_out, proj_parts, rest_parts = lax.optimization_barrier(
        (in_once, d_input, block_out, proj_parts, rest_parts)
    )
    in_parts = spread_twice(*in_once)
    d_input = z_second(*d_input)
    (grad_proj,) = place(
        place_proj_kernel, "place_proj", 5, here, proj_parts, [(fc_cols // 2, width)]
    )
    grad_fc, grad_out = place(
        place_rest_kernel, "place_rest", 5, here, rest_parts, [(half, fc_cols), (half, width)]
    )
    grad_w_qkv, small_all = place(
        place_in_kernel, "place_in", 4, here, in_parts,
        [(half, 3 * width), (4, 8, PACK)],
        [VMEM((4, 4, half // 4, PACK), f32)],
    )

    def piece(index):
        return small_all[index // 3, index % 3, :half]

    return (
        give_spans(by_source(block_out)),
        give_spans(by_source(d_input)).astype(f32),
        piece(0),
        piece(1),
        grad_w_qkv,
        jnp.stack([piece(2), piece(3)]),
        grad_out,
        piece(4),
        piece(5),
        piece(6),
        grad_fc,
        jnp.concatenate([piece(8), piece(9), piece(10), piece(11)]),
        grad_proj,
        piece(7),
    )


def layer_norm(values, gain, shift):
    center = jnp.mean(values, axis=-1, keepdims=True)
    moved = values - center
    spread = jnp.mean(moved * moved, axis=-1, keepdims=True)
    return moved * lax.rsqrt(spread + 1e-05) * gain + shift


def gelu_tanh(values):
    return (
        0.5
        * values
        * (1.0 + jnp.tanh(0.7978845608028654 * (values + 0.044715 * values * values * values)))
    )


def split_count(row_total, limit):
    pieces = 1
    while row_total % pieces != 0 or row_total // pieces > limit:
        pieces += 1
    return pieces


def row_positions(order_table, first_index, row_total, seq_dev, span_rows):
    rows_here = first_index + jnp.arange(row_total, dtype=jnp.int32)
    device_of = rows_here // seq_dev
    half_of = rows_here % seq_dev // span_rows
    slot_index = device_of * 2 + half_of
    flat_order = order_table.reshape(-1)
    table_slots = jnp.arange(flat_order.shape[0], dtype=jnp.int32)
    picked = jnp.sum(
        jnp.where(slot_index[:, None] == table_slots[None, :], flat_order[None, :], 0), axis=1
    )
    return picked * span_rows + rows_here % span_rows


def doc_of(positions, lengths_row):
    ends_at = jnp.cumsum(lengths_row)
    inner_ends = ends_at[:-1]
    return jnp.sum((positions[:, None] >= inner_ends[None, :]).astype(jnp.int32), axis=1)


def visible(query_pos, query_doc, key_pos, key_doc):
    causal = key_pos[None, None, :] <= query_pos[None, :, None]
    same_doc = key_doc[:, None, :] == query_doc[:, :, None]
    return (causal & same_doc)[:, :, None, :]


def per_device(
    block_input,
    span_order,
    doc_lengths,
    ln1_gain,
    ln1_bias,
    w_qkv,
    qv_bias,
    w_out,
    out_bias,
    ln2_gain,
    ln2_bias,
    w_fc,
    fc_bias,
    w_proj,
    proj_bias,
    d_out,
):
    seq_group, seq_dev, width = block_input.shape
    heads = HEADS
    head_dim = width // heads
    span_rows = seq_dev // 2
    score_scale = head_dim ** (-0.5)

    def docs_for(positions):
        return jax.vmap(doc_of, in_axes=(None, 0))(positions, doc_lengths)

    weights_all = (
        lax.all_gather(ln1_gain, "wt", axis=0, tiled=True),
        lax.all_gather(ln1_bias, "wt", axis=0, tiled=True),
        lax.all_gather(w_qkv, "wt", axis=0, tiled=True),
        lax.all_gather(qv_bias, "wt", axis=1, tiled=True),
        lax.all_gather(w_out, "wt", axis=0, tiled=True),
        lax.all_gather(out_bias, "wt", axis=0, tiled=True),
        lax.all_gather(ln2_gain, "wt", axis=0, tiled=True),
        lax.all_gather(ln2_bias, "wt", axis=0, tiled=True),
        lax.all_gather(w_fc, "wt", axis=0, tiled=True),
        lax.all_gather(fc_bias, "wt", axis=0, tiled=True),
        lax.all_gather(w_proj, "wt", axis=0, tiled=True),
        lax.all_gather(proj_bias, "wt", axis=0, tiled=True),
    )
    gain_one = weights_all[0].astype(jnp.float32)
    shift_one = weights_all[1].astype(jnp.float32)
    bias_pair = weights_all[3].astype(jnp.float32)
    bias_out = weights_all[5].astype(jnp.float32)
    gain_two = weights_all[6].astype(jnp.float32)
    shift_two = weights_all[7].astype(jnp.float32)
    bias_fc = weights_all[9].astype(jnp.float32)
    bias_proj = weights_all[11].astype(jnp.float32)
    me_ctx = lax.axis_index("ctx")
    local_pos = row_positions(span_order, me_ctx * seq_dev, seq_dev, seq_dev, span_rows)
    local_doc = docs_for(local_pos)
    tokens_in = block_input.astype(jnp.float32)
    normed_one = layer_norm(tokens_in, gain_one, shift_one).astype(jnp.bfloat16)
    qkv_bias = jnp.concatenate([bias_pair[0], jnp.zeros((width,), jnp.float32), bias_pair[1]])
    projected = (
        jnp.einsum("btd,de->bte", normed_one, weights_all[2], preferred_element_type=jnp.float32)
        + qkv_bias
    )
    projected_low = projected.astype(jnp.bfloat16)
    query_low = projected_low[..., :width]
    key_low = projected_low[..., width : 2 * width]
    value_low = projected_low[..., 2 * width :]
    query_heads = query_low.reshape(seq_group, seq_dev, heads, head_dim)
    key_heads = key_low.reshape(seq_group, seq_dev, heads, head_dim)
    value_heads = value_low.reshape(seq_group, seq_dev, heads, head_dim)
    start_state = (
        jnp.zeros((seq_group, seq_dev, heads, head_dim), jnp.float32),
        jnp.full((seq_group, seq_dev, heads), neg_large, jnp.float32),
        jnp.zeros((seq_group, seq_dev, heads), jnp.float32),
    )
    key_piece = lax.all_gather(key_low, "ctx", axis=1, tiled=True)
    value_piece = lax.all_gather(value_low, "ctx", axis=1, tiled=True)
    piece_rows = key_piece.shape[1]
    key_pos = row_positions(span_order, jnp.int32(0), piece_rows, seq_dev, span_rows)
    key_doc = docs_for(key_pos)
    block_rows = piece_rows // split_count(piece_rows, 1024)

    def one_block(block_index, running):
        acc_sum, run_max, run_total = running
        first_row = block_index * block_rows
        key_block = lax.dynamic_slice_in_dim(key_piece, first_row, block_rows, 1).reshape(
            seq_group, block_rows, heads, head_dim
        )
        value_block = lax.dynamic_slice_in_dim(value_piece, first_row, block_rows, 1).reshape(
            seq_group, block_rows, heads, head_dim
        )
        allowed = visible(
            local_pos,
            local_doc,
            lax.dynamic_slice_in_dim(key_pos, first_row, block_rows, 0),
            lax.dynamic_slice_in_dim(key_doc, first_row, block_rows, 1),
        )
        scores = (
            jnp.einsum(
                "bqhd,bkhd->bqhk", query_heads, key_block, preferred_element_type=jnp.float32
            )
            * score_scale
        )
        scores = jnp.where(allowed, scores, neg_large)
        new_max = jnp.maximum(run_max, jnp.max(scores, axis=-1))
        weights = jnp.where(allowed, jnp.exp(scores - new_max[..., None]), 0.0)
        rescale = jnp.exp(run_max - new_max)
        run_total = run_total * rescale + jnp.sum(weights, axis=-1)
        acc_sum = acc_sum * rescale[..., None] + jnp.einsum(
            "bqhk,bkhd->bqhd",
            weights.astype(jnp.bfloat16),
            value_block,
            preferred_element_type=jnp.float32,
        )
        return (acc_sum, new_max, run_total)

    acc_sum, run_max, run_total = lax.fori_loop(0, piece_rows // block_rows, one_block, start_state)
    attn_heads = acc_sum / run_total[..., None]
    log_total = run_max + jnp.log(run_total)
    attn_out = attn_heads.reshape(seq_group, seq_dev, width)
    attn_low = attn_out.astype(jnp.bfloat16)
    branch_pre = (
        jnp.einsum("btd,de->bte", attn_low, weights_all[4], preferred_element_type=jnp.float32)
        + bias_out
    )
    resid_one = tokens_in + branch_scale * branch_pre
    normed_two = layer_norm(resid_one, gain_two, shift_two).astype(jnp.bfloat16)
    hidden_pre = (
        jnp.einsum("btd,df->btf", normed_two, weights_all[8], preferred_element_type=jnp.float32)
        + bias_fc
    )
    hidden_low = gelu_tanh(hidden_pre).astype(jnp.bfloat16)
    mlp_pre = (
        jnp.einsum("btf,fd->btd", hidden_low, weights_all[10], preferred_element_type=jnp.float32)
        + bias_proj
    )
    block_out = (resid_one + branch_scale * mlp_pre).astype(jnp.bfloat16)
    weights_back = (
        lax.all_gather(ln1_gain, "wt", axis=0, tiled=True),
        lax.all_gather(ln1_bias, "wt", axis=0, tiled=True),
        lax.all_gather(w_qkv, "wt", axis=0, tiled=True),
        lax.all_gather(qv_bias, "wt", axis=1, tiled=True),
        lax.all_gather(w_out, "wt", axis=0, tiled=True),
        lax.all_gather(out_bias, "wt", axis=0, tiled=True),
        lax.all_gather(ln2_gain, "wt", axis=0, tiled=True),
        lax.all_gather(ln2_bias, "wt", axis=0, tiled=True),
        lax.all_gather(w_fc, "wt", axis=0, tiled=True),
        lax.all_gather(fc_bias, "wt", axis=0, tiled=True),
        lax.all_gather(w_proj, "wt", axis=0, tiled=True),
        lax.all_gather(proj_bias, "wt", axis=0, tiled=True),
    )
    back_gain_one = weights_back[0].astype(jnp.float32)
    back_shift_one = weights_back[1].astype(jnp.float32)
    back_gain_two = weights_back[6].astype(jnp.float32)
    back_shift_two = weights_back[7].astype(jnp.float32)
    cotangent = d_out.astype(jnp.float32)
    d_mlp = (branch_scale * cotangent).astype(jnp.bfloat16)
    grad_w_proj = jnp.einsum("btf,btd->fd", hidden_low, d_mlp, preferred_element_type=jnp.float32)
    grad_proj_bias = jnp.sum(d_mlp.astype(jnp.float32), axis=(0, 1))
    d_hidden = jnp.einsum(
        "btd,fd->btf", d_mlp, weights_back[10], preferred_element_type=jnp.float32
    )
    gelu_unused, gelu_pull = jax.vjp(gelu_tanh, hidden_pre)
    d_pre = gelu_pull(d_hidden)[0].astype(jnp.bfloat16)
    grad_w_fc = jnp.einsum("btd,btf->df", normed_two, d_pre, preferred_element_type=jnp.float32)
    grad_fc_bias = jnp.sum(d_pre.astype(jnp.float32), axis=(0, 1))
    d_normed_two = jnp.einsum(
        "btf,df->btd", d_pre, weights_back[8], preferred_element_type=jnp.float32
    )
    norm_unused, norm_pull = jax.vjp(layer_norm, resid_one, back_gain_two, back_shift_two)
    d_resid_part, grad_ln2_gain, grad_ln2_bias = norm_pull(d_normed_two)
    d_resid = cotangent + d_resid_part
    d_branch = (branch_scale * d_resid).astype(jnp.bfloat16)
    grad_w_out = jnp.einsum("btd,bte->de", attn_low, d_branch, preferred_element_type=jnp.float32)
    grad_out_bias = jnp.sum(d_branch.astype(jnp.float32), axis=(0, 1))
    d_attn_low = jnp.einsum(
        "bte,de->btd", d_branch, weights_back[4], preferred_element_type=jnp.float32
    ).astype(jnp.bfloat16)
    d_attn_heads = d_attn_low.reshape(seq_group, seq_dev, heads, head_dim)
    delta = jnp.sum(d_attn_heads.astype(jnp.float32) * attn_heads, axis=-1)
    fold_key_piece = lax.all_gather(key_low, "ctx", axis=1, tiled=True)
    fold_value_piece = lax.all_gather(value_low, "ctx", axis=1, tiled=True)
    piece_rows = fold_key_piece.shape[1]
    fold_key_pos = row_positions(span_order, jnp.int32(0), piece_rows, seq_dev, span_rows)
    fold_key_doc = docs_for(fold_key_pos)
    fold_block_rows = piece_rows // split_count(piece_rows, 1024)

    def one_block(block_index, grad_query):
        first_row = block_index * fold_block_rows
        key_block = lax.dynamic_slice_in_dim(fold_key_piece, first_row, fold_block_rows, 1).reshape(
            seq_group, fold_block_rows, heads, head_dim
        )
        value_block = lax.dynamic_slice_in_dim(
            fold_value_piece, first_row, fold_block_rows, 1
        ).reshape(seq_group, fold_block_rows, heads, head_dim)
        allowed = visible(
            local_pos,
            local_doc,
            lax.dynamic_slice_in_dim(fold_key_pos, first_row, fold_block_rows, 0),
            lax.dynamic_slice_in_dim(fold_key_doc, first_row, fold_block_rows, 1),
        )
        scores = (
            jnp.einsum(
                "bqhd,bkhd->bqhk", query_heads, key_block, preferred_element_type=jnp.float32
            )
            * score_scale
        )
        probs = jnp.where(allowed, jnp.exp(scores - log_total[..., None]), 0.0)
        d_probs = jnp.einsum(
            "bqhd,bkhd->bqhk", d_attn_heads, value_block, preferred_element_type=jnp.float32
        )
        d_scores = (probs * (d_probs - delta[..., None])).astype(jnp.bfloat16)
        return (
            grad_query
            + jnp.einsum("bqhk,bkhd->bqhd", d_scores, key_block, preferred_element_type=jnp.float32)
            * score_scale
        )

    grad_query = lax.fori_loop(
        0,
        piece_rows // fold_block_rows,
        one_block,
        jnp.zeros((seq_group, seq_dev, heads, head_dim), jnp.float32),
    )
    stats_all = (
        lax.all_gather(log_total, "ctx", axis=1, tiled=True),
        lax.all_gather(delta, "ctx", axis=1, tiled=True),
    )
    totals_every = stats_all[0]
    deltas_every = stats_all[1]

    def fold_keys(carried, received, first_index):
        query_piece, grad_piece = received
        piece_rows = query_piece.shape[1]
        query_pos = row_positions(span_order, first_index, piece_rows, seq_dev, span_rows)
        query_doc = docs_for(query_pos)
        block_rows = piece_rows // split_count(piece_rows, 1024)

        def one_block(block_index, running):
            grad_key, grad_value = running
            first_row = block_index * block_rows
            query_block = lax.dynamic_slice_in_dim(query_piece, first_row, block_rows, 1).reshape(
                seq_group, block_rows, heads, head_dim
            )
            grad_block = lax.dynamic_slice_in_dim(grad_piece, first_row, block_rows, 1).reshape(
                seq_group, block_rows, heads, head_dim
            )
            total_block = lax.dynamic_slice_in_dim(totals_every, first_row, block_rows, 1)
            delta_block = lax.dynamic_slice_in_dim(deltas_every, first_row, block_rows, 1)
            allowed = visible(
                lax.dynamic_slice_in_dim(query_pos, first_row, block_rows, 0),
                lax.dynamic_slice_in_dim(query_doc, first_row, block_rows, 1),
                local_pos,
                local_doc,
            )
            scores = (
                jnp.einsum(
                    "bqhd,bkhd->bqhk", query_block, key_heads, preferred_element_type=jnp.float32
                )
                * score_scale
            )
            probs = jnp.where(allowed, jnp.exp(scores - total_block[..., None]), 0.0)
            grad_value = grad_value + jnp.einsum(
                "bqhk,bqhd->bkhd",
                probs.astype(jnp.bfloat16),
                grad_block,
                preferred_element_type=jnp.float32,
            )
            d_probs = jnp.einsum(
                "bqhd,bkhd->bqhk", grad_block, value_heads, preferred_element_type=jnp.float32
            )
            d_scores = (probs * (d_probs - delta_block[..., None])).astype(jnp.bfloat16)
            grad_key = (
                grad_key
                + jnp.einsum(
                    "bqhk,bqhd->bkhd", d_scores, query_block, preferred_element_type=jnp.float32
                )
                * score_scale
            )
            return (grad_key, grad_value)

        return lax.fori_loop(0, piece_rows // block_rows, one_block, carried)

    zero_heads = jnp.zeros((seq_group, seq_dev, heads, head_dim), jnp.float32)
    grad_key, grad_value = fold_keys(
        (zero_heads, zero_heads),
        (
            lax.all_gather(query_low, "ctx", axis=1, tiled=True),
            lax.all_gather(d_attn_low, "ctx", axis=1, tiled=True),
        ),
        jnp.int32(0),
    )
    d_projected = jnp.concatenate(
        [
            grad_query.reshape(seq_group, seq_dev, width),
            grad_key.reshape(seq_group, seq_dev, width),
            grad_value.reshape(seq_group, seq_dev, width),
        ],
        axis=-1,
    ).astype(jnp.bfloat16)
    grad_w_qkv = jnp.einsum(
        "btd,bte->de", normed_one, d_projected, preferred_element_type=jnp.float32
    )
    column_sums = jnp.sum(d_projected.astype(jnp.float32), axis=(0, 1))
    grad_qv_bias = jnp.stack([column_sums[:width], column_sums[2 * width :]])
    d_normed_one = jnp.einsum(
        "bte,de->btd", d_projected, weights_back[2], preferred_element_type=jnp.float32
    )
    first_unused, first_pull = jax.vjp(layer_norm, tokens_in, back_gain_one, back_shift_one)
    d_input_part, grad_ln1_gain, grad_ln1_bias = first_pull(d_normed_one)
    d_input = d_resid + d_input_part
    shares = (
        lax.psum_scatter(
            grad_ln1_gain.astype(jnp.bfloat16), "wt", scatter_dimension=0, tiled=True
        ).astype(jnp.float32),
        lax.psum_scatter(
            grad_ln1_bias.astype(jnp.bfloat16), "wt", scatter_dimension=0, tiled=True
        ).astype(jnp.float32),
        lax.psum_scatter(
            grad_w_qkv.astype(jnp.bfloat16), "wt", scatter_dimension=0, tiled=True
        ).astype(jnp.float32),
        lax.psum_scatter(
            grad_qv_bias.astype(jnp.bfloat16), "wt", scatter_dimension=1, tiled=True
        ).astype(jnp.float32),
        lax.psum_scatter(
            grad_w_out.astype(jnp.bfloat16), "wt", scatter_dimension=0, tiled=True
        ).astype(jnp.float32),
        lax.psum_scatter(
            grad_out_bias.astype(jnp.bfloat16), "wt", scatter_dimension=0, tiled=True
        ).astype(jnp.float32),
        lax.psum_scatter(
            grad_ln2_gain.astype(jnp.bfloat16), "wt", scatter_dimension=0, tiled=True
        ).astype(jnp.float32),
        lax.psum_scatter(
            grad_ln2_bias.astype(jnp.bfloat16), "wt", scatter_dimension=0, tiled=True
        ).astype(jnp.float32),
        lax.psum_scatter(
            grad_w_fc.astype(jnp.bfloat16), "wt", scatter_dimension=0, tiled=True
        ).astype(jnp.float32),
        lax.psum_scatter(
            grad_fc_bias.astype(jnp.bfloat16), "wt", scatter_dimension=0, tiled=True
        ).astype(jnp.float32),
        lax.psum_scatter(
            grad_w_proj.astype(jnp.bfloat16), "wt", scatter_dimension=0, tiled=True
        ).astype(jnp.float32),
        lax.psum_scatter(
            grad_proj_bias.astype(jnp.bfloat16), "wt", scatter_dimension=0, tiled=True
        ).astype(jnp.float32),
    )
    totals = lax.psum(
        (
            shares[0],
            shares[1],
            shares[2],
            shares[3],
            shares[4],
            shares[5],
            shares[6],
            shares[7],
            shares[8],
            shares[9],
            shares[10],
            shares[11],
        ),
        "ctx",
    )
    return (
        block_out,
        d_input,
        totals[0],
        totals[1],
        totals[2],
        totals[3],
        totals[4],
        totals[5],
        totals[6],
        totals[7],
        totals[8],
        totals[9],
        totals[10],
        totals[11],
    )


def solution(mesh):
    placed = (
        P("wt", "ctx", None),
        P(),
        P("wt", None),
        P("wt"),
        P("wt"),
        P("wt", None),
        P(None, "wt"),
        P("wt", None),
        P("wt"),
        P("wt"),
        P("wt"),
        P("wt", None),
        P("wt"),
        P("wt", None),
        P("wt"),
        P("wt", "ctx", None),
    )
    fast = dict(mesh.shape) == {"ctx": 16, "wt": 2}
    return jax.shard_map(
        by_owner if fast else per_device,
        mesh=mesh,
        in_specs=placed,
        out_specs=(
            P("wt", "ctx", None),
            P("wt", "ctx", None),
            P("wt"),
            P("wt"),
            P("wt", None),
            P(None, "wt"),
            P("wt", None),
            P("wt"),
            P("wt"),
            P("wt"),
            P("wt", None),
            P("wt"),
            P("wt", None),
            P("wt"),
        ),
        check_vma=False,
    )
```

```python
import functools

import jax
import jax.numpy as jnp
from jax import lax
from jax.experimental import pallas as pl
from jax.experimental.pallas import tpu as pltpu
from jax.sharding import PartitionSpec as P

HEADS = 12

branch_scale = 0.14433756729740643
neg_large = -1e30
f32 = jnp.float32
bf16 = jnp.bfloat16
VMEM = pltpu.VMEM
vmem_cap = 56 << 20

GROUPS = 4
TILE = 128
PAD = 256
PACK = 640

pair = [(0, 1), (1, 0)]
flips = [[(i, i ^ flip) for i in range(16)] for flip in range(16)]


def z_shift(step):
    return [(i, (i // 4 + step) % 4 * 4 + i % 4) for i in range(16)]


def other_core(value):
    return lax.ppermute(value, "wt", pair)


def send_flip(value, flip):
    return lax.ppermute(value, "ctx", flips[flip])


def send_z(value, step):
    return lax.ppermute(value, "ctx", z_shift(step))


planes = [[4 * i + j for j in range(4)] for i in range(4)]


def swap_plane(value):
    return lax.all_to_all(value, "ctx", 0, 0, axis_index_groups=planes, tiled=True)


def row(value, index):
    return lax.dynamic_index_in_dim(value, index, 0, keepdims=False)


def sum_low(*terms):
    total = terms[0].astype(f32)
    for term in terms[1:]:
        total = total + term.astype(f32)
    return total.astype(bf16)


def after(value, *others):
    return lax.optimization_barrier((value,) + others)[0]


def work(micros):
    return pl.CostEstimate(flops=int(micros * 1e6), bytes_accessed=1 << 12, transcendentals=0)


def busy(micros):
    return pl.CostEstimate(flops=int(micros * 1.1e9), bytes_accessed=1 << 20, transcendentals=0)


def full_spec(shape):
    zeros = (0,) * len(shape)
    return pl.BlockSpec(shape, lambda *unused: zeros)


def dot(left, right, dims):
    return lax.dot_general(left, right, (dims, ((), ())), preferred_element_type=f32)


def norm_parts(rows):
    center = jnp.mean(rows, axis=-1, keepdims=True)
    moved = rows - center
    spread = jnp.mean(moved * moved, axis=-1, keepdims=True)
    inverse = lax.rsqrt(spread + 1e-05)
    return moved * inverse, inverse


def joined(own, oth, core):
    return jnp.concatenate([jnp.where(core == 0, own, oth), jnp.where(core == 0, oth, own)], axis=1)


def of_group(vector, group):
    picked = jnp.zeros((1, 192), f32)
    for g in range(GROUPS):
        picked = jnp.where(group == g, vector[:, 192 * g : 192 * (g + 1)], picked)
    return picked


def project_kernel(
    order_ref, where_ref, a_ref, b_ref, c_ref, d_ref, own_ref, oth_ref, small_own_ref, small_oth_ref,
    x_ref, h_ref, q_ref, kv_ref, weight_ref,
    held,
):
    group, core = where_ref[1], where_ref[2]
    half = own_ref.shape[0]
    for source, at in ((own_ref, core), (oth_ref, 1 - core)):
        rows = pl.ds(pl.multiple_of(at * half, half), half)
        for i in range(3):
            window = source[:, 384 * i : 384 * (i + 1)].astype(f32)
            part = jnp.where(group % 2 == 0, window[:, :192], window[:, 192:])
            weight_ref[rows, PAD * i : PAD * (i + 1)] = jnp.concatenate(
                [part, jnp.zeros((half, PAD - 192), f32)], axis=1
            ).astype(bf16)
    for index, source in enumerate((a_ref, b_ref, c_ref, d_ref)):
        held[4 * index : 4 * index + 4] = source[...]

    small = joined(small_own_ref[0:4, :], small_oth_ref[0:4, :], core)
    lane = lax.broadcasted_iota(jnp.int32, (1, PAD - 192), 1)
    none = jnp.zeros((1, PAD - 192), f32)
    bias = jnp.concatenate(
        [
            of_group(small[2:3], group), none, jnp.zeros((1, PAD), f32),
            of_group(small[3:4], group), (lane == 0).astype(f32),
        ],
        axis=1,
    )
    step = 4 * held.shape[1]
    for i in range(4):
        at = slice(step * i, step * (i + 1))
        rows = jnp.concatenate([held[order_ref[4 * i + t]].astype(f32) for t in range(4)], axis=0)
        x_ref[at, :] = rows.astype(bf16)
        normed, unused = norm_parts(rows)
        low = (normed * small[0:1] + small[1:2]).astype(bf16)
        h_ref[at, :] = low
        out = dot(low, weight_ref[...], ((1,), (0,))) + bias
        q_ref[at, :] = (out[:, :PAD].astype(bf16) * 0.125).astype(bf16)
        kv_ref[at, :] = out[:, PAD:].astype(bf16)


def project(order, where, pieces, own, oth, small_own, small_oth):
    blocks, span_rows, width = pieces[0].shape
    spans = 4 * blocks
    rows = spans * span_rows
    return pl.pallas_call(
        project_kernel,
        in_specs=[pl.BlockSpec(memory_space=pltpu.SMEM)] * 2
        + [pl.BlockSpec(memory_space=pltpu.VMEM)] * 8,
        out_specs=[pl.BlockSpec(memory_space=pltpu.VMEM)] * 5,
        out_shape=[
            jax.ShapeDtypeStruct((rows, width), bf16),
            jax.ShapeDtypeStruct((rows, width), bf16),
            jax.ShapeDtypeStruct((rows, PAD), bf16),
            jax.ShapeDtypeStruct((rows, 2 * PAD), bf16),
            jax.ShapeDtypeStruct((width, 3 * PAD), bf16),
        ],
        scratch_shapes=[VMEM((spans, span_rows, width), bf16)],
        compiler_params=pltpu.CompilerParams(vmem_limit_bytes=vmem_cap),
        cost_estimate=busy(6),
        name="project",
    )(order, where, *pieces, own, oth, small_own, small_oth)


def middle_kernel(
    where_ref, attn_ref, x_ref, cot_ref, d_mlp_ref, grad_own_ref, proj_oth_ref, out_own_ref, out_oth_ref, fc_own_ref, fc_oth_ref,
    small_own_ref, small_oth_ref,
    resid_ref, attn_own_ref, attn_oth_ref, normed_own_ref, normed_oth_ref, hidden_own_ref, hidden_oth_ref, pre_ref, d_resid_ref, d_branch_ref, send_ref,
    branch_sum_ref, gain_sum_ref, shift_sum_ref, mlp_sum_ref, pre_sum_ref,
    back, bias_fc, w_out_ref, w_fc_ref,
):
    core = where_ref[2]
    for own, oth, whole in ((out_own_ref, out_oth_ref, w_out_ref), (fc_own_ref, fc_oth_ref, w_fc_ref)):
        rows = own.shape[0]
        whole[pl.ds(pl.multiple_of(core * rows, rows), rows), :] = own[...]
        whole[pl.ds(pl.multiple_of((1 - core) * rows, rows), rows), :] = oth[...]
    small = joined(small_own_ref[...], small_oth_ref[...], core)
    half = small_own_ref.shape[1]
    gain = small[5:6]
    for i in range(4):
        bias_fc[:, half * i : half * (i + 1)] = jnp.where(
            core == 0, small_own_ref[8 + i : 9 + i], small_oth_ref[8 + i : 9 + i]
        )
        bias_fc[:, half * (4 + i) : half * (5 + i)] = jnp.where(
            core == 0, small_oth_ref[8 + i : 9 + i], small_own_ref[8 + i : 9 + i]
        )
    attn = jnp.concatenate([attn_ref[g].astype(f32) for g in range(GROUPS)], axis=1).astype(bf16)
    half = small_own_ref.shape[1]
    attn_own_ref[...] = jnp.where(core == 0, attn[:, :half], attn[:, half:])
    attn_oth_ref[...] = jnp.where(core == 0, attn[:, half:], attn[:, :half])
    cot = cot_ref[...].astype(f32)
    branch = dot(attn, w_out_ref[...], ((1,), (0,))) + small[4:5]
    resid = x_ref[...].astype(f32) + branch_scale * branch
    resid_ref[...] = resid
    unit, inverse = norm_parts(resid)
    low = (unit * gain + small[6:7]).astype(bf16)
    normed_own_ref[...] = jnp.where(core == 0, low[:, :half], low[:, half:])
    normed_oth_ref[...] = jnp.where(core == 0, low[:, half:], low[:, :half])
    back[...] = jnp.zeros_like(back)
    wide = 512

    def columns(hidden_grad, hidden_ref, first, t, carry):
        here = pl.ds(pl.multiple_of(t * wide, wide), wide)
        at = pl.ds(pl.multiple_of(first + t * wide, wide), wide)
        weight = w_fc_ref[:, at]
        u = dot(low, weight, ((1,), (0,))) + bias_fc[:, at]
        square = u * u
        th = jnp.tanh(0.7978845608028654 * (u + 0.044715 * (square * u)))
        one = 0.5 * (1.0 + th)
        hidden_ref[:, here] = (u * one).astype(bf16)
        slope = one + 0.5 * u * (1.0 - th * th) * (0.7978845608028654 * (1.0 + 0.134145 * square))
        pre = (hidden_grad(here) * slope).astype(bf16)
        pre_ref[:, at] = pre
        pre_sum_ref[:, at] = jnp.sum(pre.astype(f32), axis=0, keepdims=True)
        back[...] += dot(pre, weight, ((1,), (1,)))
        return carry

    span = grad_own_ref.shape[1]
    lax.fori_loop(
        0, span // wide, functools.partial(columns, lambda here: grad_own_ref[:, here], hidden_own_ref, core * span), 0,
        unroll=True,
    )
    lax.fori_loop(
        0, span // wide,
        functools.partial(
            columns,
            lambda here: dot(d_mlp_ref[...], proj_oth_ref[here, :], ((1,), (1,))),
            hidden_oth_ref,
            (1 - core) * span,
        ),
        0,
        unroll=True,
    )
    d_normed = back[...]
    gain_sum_ref[...] = jnp.sum(d_normed * unit, axis=0, keepdims=True)
    shift_sum_ref[...] = jnp.sum(d_normed, axis=0, keepdims=True)
    scaled = d_normed * gain
    part = scaled - jnp.mean(scaled, axis=-1, keepdims=True)
    part = part - unit * jnp.mean(scaled * unit, axis=-1, keepdims=True)
    d_resid = cot + inverse * part
    d_resid_ref[...] = d_resid
    d_branch = (branch_scale * d_resid).astype(bf16)
    d_branch_ref[...] = d_branch
    branch_sum_ref[...] = jnp.sum(d_branch.astype(f32), axis=0, keepdims=True)
    mlp_sum_ref[...] = jnp.sum(d_mlp_ref[...].astype(f32), axis=0, keepdims=True)
    d_attn = dot(d_branch, w_out_ref[...], ((1,), (1,)))
    feats = send_ref.shape[2]
    for g in range(GROUPS):
        send_ref[g] = d_attn[:, feats * g : feats * (g + 1)].astype(bf16)


def middle(
    attn, x, cot, d_mlp, grad_own, proj_oth, out_own, out_oth, fc_own, fc_oth, where, small_own, small_oth
):
    groups, rows, feats = attn.shape
    width, wide = out_own.shape[1], fc_own.shape[1]
    shapes = [
        ((rows, width), f32), ((rows, width // 2), bf16), ((rows, width // 2), bf16),
        ((rows, width // 2), bf16), ((rows, width // 2), bf16), ((rows, wide // 2), bf16),
        ((rows, wide // 2), bf16),
        ((rows, wide), bf16), ((rows, width), f32), ((rows, width), bf16), (attn.shape, bf16),
        ((1, width), f32), ((1, width), f32), ((1, width), f32), ((1, width), f32), ((1, wide), f32),
    ]
    return pl.pallas_call(
        middle_kernel,
        in_specs=[pl.BlockSpec(memory_space=pltpu.SMEM)]
        + [pl.BlockSpec(memory_space=pltpu.VMEM)] * 12,
        out_specs=[pl.BlockSpec(memory_space=pltpu.VMEM)] * len(shapes),
        out_shape=[jax.ShapeDtypeStruct(shape, kind) for shape, kind in shapes],
        scratch_shapes=[
            VMEM((rows, width), f32),
            VMEM((1, wide), f32),
            VMEM((width, width), bf16),
            VMEM((width, wide), bf16),
        ],
        compiler_params=pltpu.CompilerParams(vmem_limit_bytes=vmem_cap),
        cost_estimate=busy(12),
        name="middle",
    )(
        where, attn, x, cot, d_mlp, grad_own, proj_oth, out_own, out_oth, fc_own, fc_oth, small_own, small_oth
    )


def pack_kernel(where_ref, gain_ref, shift_ref, bias_ref, *refs):
    sums, own_ref, oth_ref = refs[:5], refs[5], refs[6]
    group, core = where_ref[1], where_ref[2]
    half = own_ref.shape[1]

    def spread(part):
        none = jnp.zeros((1, 192), f32)
        return jnp.concatenate([jnp.where(group == g, part, none) for g in range(GROUPS)], axis=1)

    vectors = [
        gain_ref[...], shift_ref[...],
        spread(bias_ref[:, :192]), spread(bias_ref[:, 2 * PAD : 2 * PAD + 192]),
    ]
    vectors += [r[...] for r in sums[:4]]
    for index, vector in enumerate(vectors):
        low, high = vector[:, :half], vector[:, half:]
        own_ref[index : index + 1, :] = jnp.where(core == 0, low, high)
        oth_ref[index : index + 1, :] = jnp.where(core == 0, high, low)
    wide = sums[4][...]
    for index in range(4):
        low = wide[:, half * index : half * (index + 1)]
        high = wide[:, half * (index + 4) : half * (index + 5)]
        own_ref[8 + index : 9 + index, :] = jnp.where(core == 0, low, high)
        oth_ref[8 + index : 9 + index, :] = jnp.where(core == 0, high, low)


def pack(where, gain, shift, bias, sums):
    half = gain.shape[1] // 2
    return pl.pallas_call(
        pack_kernel,
        in_specs=[pl.BlockSpec(memory_space=pltpu.SMEM)]
        + [pl.BlockSpec(memory_space=pltpu.VMEM)] * 8,
        out_specs=[pl.BlockSpec(memory_space=pltpu.VMEM)] * 2,
        out_shape=[jax.ShapeDtypeStruct((12, half), f32)] * 2,
        cost_estimate=busy(1),
        name="pack",
    )(where, gain, shift, bias, *sums)


def by_head(tile):
    lane = lax.broadcasted_iota(jnp.int32, tile.shape, 1)
    zero = jnp.zeros_like(tile)
    return jnp.concatenate(
        [jnp.where((lane >= 64 * h) & (lane < 64 * h + 64), tile, zero) for h in range(3)], axis=0
    )


def by_head_t(tile):
    flipped = tile.T
    feat = lax.broadcasted_iota(jnp.int32, flipped.shape, 0)
    zero = jnp.zeros_like(flipped)
    return jnp.concatenate(
        [jnp.where((feat >= 64 * h) & (feat < 64 * h + 64), flipped, zero) for h in range(3)], axis=1
    )


def tile_rows(index):
    return pl.ds(pl.multiple_of(index * TILE, TILE), TILE)


def tile_pair(plan_ref, i, step, tiles):
    first = plan_ref[0, i] + 2 * step
    beyond = jnp.where(first + 1 < plan_ref[1, i], 0, 1 << 20)
    second = jnp.minimum(first + 1, tiles - 1)
    return tile_rows(first), tile_rows(second), beyond


def pair_rows(own_ref, oth_ref, first, second, lanes):
    return jnp.concatenate(
        [own_ref[first, lanes], oth_ref[first, lanes], own_ref[second, lanes], oth_ref[second, lanes]],
        axis=0,
    )


def pair_columns(own_ref, oth_ref, first, second):
    return jnp.concatenate(
        [own_ref[:, first], oth_ref[:, first], own_ref[:, second], oth_ref[:, second]], axis=1
    )


def visible_pair(kpos_ref, first, second, beyond, meta):
    keys = jnp.concatenate(
        [
            kpos_ref[0, first, :],
            kpos_ref[1, first, :],
            kpos_ref[0, second, :] + beyond,
            kpos_ref[1, second, :] + beyond,
        ],
        axis=0,
    )
    keys = jnp.concatenate([keys, keys, keys], axis=1)
    return (keys <= meta[0:1, :]) & (keys >= meta[1:2, :])


def pairs_of(plan_ref, i):
    return (plan_ref[1, i] - plan_ref[0, i] + 1) // 2


def attend_kernel(
    plan_ref, q_ref, own_ref, oth_ref, kpos_ref, meta_ref,
    o_ref, lse_ref, out_ref,
    vown, voth, stack, acc, top, held,
):
    spans, span_rows, feats = out_ref.shape
    tiles = q_ref.shape[0] // TILE
    keys_step = 4 * TILE
    vown[...] = own_ref[:, PAD:].T
    voth[...] = oth_ref[:, PAD:].T

    def one_tile(i, carry):
        here = tile_rows(i)
        stack[...] = by_head_t(q_ref[here, :])
        meta = meta_ref[i]
        acc[...] = jnp.zeros_like(acc)
        top[...] = jnp.full_like(top, neg_large)

        def score(step, inner):
            first, second, beyond = tile_pair(plan_ref, i, step, tiles)
            keys = pair_rows(own_ref, oth_ref, first, second, slice(0, PAD))
            scores = dot(keys, stack[...], ((1,), (0,)))
            allowed = visible_pair(kpos_ref, first, second, beyond, meta)
            scores = jnp.where(allowed, scores, neg_large)
            held[pl.ds(pl.multiple_of(step * keys_step, keys_step), keys_step), :] = scores
            best = jnp.max(scores.reshape(keys_step // 8, 8, scores.shape[1]), axis=0)
            top[...] = jnp.maximum(top[...], best)
            return inner

        lax.fori_loop(0, pairs_of(plan_ref, i), score, 0)
        peak = jnp.max(top[...], axis=0, keepdims=True)

        def weigh(step, inner):
            first, second, unused = tile_pair(plan_ref, i, step, tiles)
            scores = held[pl.ds(pl.multiple_of(step * keys_step, keys_step), keys_step), :]
            probs = jnp.exp(scores - peak).astype(bf16)
            vals = pair_columns(vown, voth, first, second)
            acc[...] += dot(vals, probs, ((1,), (0,)))
            return inner

        lax.fori_loop(0, pairs_of(plan_ref, i), weigh, 0)
        total = acc[192:193, :]
        lse_ref[i] = peak + jnp.log(total)
        parts = [
            acc[64 * h : 64 * h + 64, TILE * h : TILE * h + TILE]
            / total[:, TILE * h : TILE * h + TILE]
            for h in range(3)
        ]
        heads_t = jnp.concatenate(parts + [jnp.zeros((64, TILE), f32)], axis=0)
        o_ref[here, :] = heads_t.T
        return carry

    lax.fori_loop(0, tiles, one_tile, 0)
    for a in range(spans):
        out_ref[plan_ref[2, a]] = o_ref[span_rows * a : span_rows * (a + 1), :feats].astype(bf16)


def attend(plan, q, own, oth, kpos, meta, spans):
    rows = q.shape[0]
    tiles = rows // TILE
    wide = 3 * TILE
    return pl.pallas_call(
        attend_kernel,
        in_specs=[pl.BlockSpec(memory_space=pltpu.SMEM)]
        + [pl.BlockSpec(memory_space=pltpu.VMEM)] * 5,
        out_specs=[pl.BlockSpec(memory_space=pltpu.VMEM)] * 3,
        out_shape=[
            jax.ShapeDtypeStruct((rows, PAD), f32),
            jax.ShapeDtypeStruct((tiles, 1, wide), f32),
            jax.ShapeDtypeStruct((spans, rows // spans, 192), bf16),
        ],
        scratch_shapes=[
            VMEM((PAD, rows), bf16),
            VMEM((PAD, rows), bf16),
            VMEM((PAD, wide), bf16),
            VMEM((PAD, wide), f32),
            VMEM((8, wide), f32),
            VMEM((2 * rows + 2 * TILE, wide), f32),
        ],
        compiler_params=pltpu.CompilerParams(vmem_limit_bytes=vmem_cap),
        cost_estimate=busy(15),
        name="attend",
    )(plan, q, own, oth, kpos, meta)


def attend_back_kernel(
    plan_ref, q_ref, own_ref, oth_ref, kpos_ref, meta_ref, grad_ref, o_ref, lse_ref,
    dq_ref, down_ref, doth_ref,
    grads, kown, koth, acc_oth, stack, gstack, stack_t, gstack_t, dq_t,
):
    spans, span_rows, feats = grad_ref.shape
    tiles = q_ref.shape[0] // TILE
    kown[...] = own_ref[:, :PAD].T
    koth[...] = oth_ref[:, :PAD].T
    down_ref[...] = jnp.zeros_like(down_ref)
    acc_oth[...] = jnp.zeros_like(acc_oth)
    grads[:, 128:] = jnp.zeros((grads.shape[0], PAD - 128), f32)
    for a in range(spans):
        grads[span_rows * a : span_rows * (a + 1), :feats] = grad_ref[plan_ref[2, a]].astype(f32)

    def one_tile(i, carry):
        here = tile_rows(i)
        grad = grads[here, :]
        grad_low = grad.astype(bf16)
        stack[...] = by_head(q_ref[here, :])
        gstack[...] = by_head(grad_low)
        stack_t[...] = by_head_t(q_ref[here, :])
        gstack_t[...] = by_head_t(grad_low)
        product = (grad * o_ref[here, :]).T
        delta = jnp.concatenate(
            [jnp.sum(product[64 * h : 64 * h + 64], axis=0, keepdims=True) for h in range(3)], axis=1
        )
        lse = lse_ref[i]
        meta = meta_ref[i]
        dq_t[...] = jnp.zeros_like(dq_t)

        def one(step, inner):
            first, second, beyond = tile_pair(plan_ref, i, step, tiles)
            keys = pair_rows(own_ref, oth_ref, first, second, slice(0, PAD))
            vals = pair_rows(own_ref, oth_ref, first, second, slice(PAD, 2 * PAD))
            scores = dot(keys, stack_t[...], ((1,), (0,)))
            allowed = visible_pair(kpos_ref, first, second, beyond, meta)
            probs = jnp.where(allowed, jnp.exp(scores - lse), 0.0)
            d_probs = dot(vals, gstack_t[...], ((1,), (0,)))
            d_scores = (probs * (d_probs - delta)).astype(bf16)
            d_vals = dot(probs.astype(bf16), gstack[...], ((1,), (0,)))
            d_keys = dot(d_scores, stack[...], ((1,), (0,)))
            down_ref[first, :PAD] += d_keys[:TILE]
            down_ref[first, PAD:] += d_vals[:TILE]
            acc_oth[first, :PAD] += d_keys[TILE : 2 * TILE]
            acc_oth[first, PAD:] += d_vals[TILE : 2 * TILE]
            down_ref[second, :PAD] += d_keys[2 * TILE : 3 * TILE]
            down_ref[second, PAD:] += d_vals[2 * TILE : 3 * TILE]
            acc_oth[second, :PAD] += d_keys[3 * TILE :]
            acc_oth[second, PAD:] += d_vals[3 * TILE :]
            dq_t[...] += dot(pair_columns(kown, koth, first, second), d_scores, ((1,), (0,)))
            return inner

        lax.fori_loop(0, pairs_of(plan_ref, i), one, 0)
        parts = [dq_t[64 * h : 64 * h + 64, TILE * h : TILE * h + TILE] for h in range(3)]
        heads_t = jnp.concatenate(parts + [jnp.zeros((64, TILE), f32)], axis=0) * 0.125
        dq_ref[here, :] = heads_t.T.astype(bf16)
        return carry

    lax.fori_loop(0, tiles, one_tile, 0)
    doth_ref[...] = acc_oth[...].astype(bf16)


def attend_back(plan, q, own, oth, kpos, meta, grad, o, lse):
    rows = q.shape[0]
    wide = 3 * TILE
    return pl.pallas_call(
        attend_back_kernel,
        in_specs=[pl.BlockSpec(memory_space=pltpu.SMEM)]
        + [pl.BlockSpec(memory_space=pltpu.VMEM)] * 8,
        out_specs=[pl.BlockSpec(memory_space=pltpu.VMEM)] * 3,
        out_shape=[
            jax.ShapeDtypeStruct((rows, PAD), bf16),
            jax.ShapeDtypeStruct((rows, 2 * PAD), f32),
            jax.ShapeDtypeStruct((rows, 2 * PAD), bf16),
        ],
        scratch_shapes=[
            VMEM((rows, PAD), f32),
            VMEM((PAD, rows), bf16),
            VMEM((PAD, rows), bf16),
            VMEM((rows, 2 * PAD), f32),
            VMEM((wide, PAD), bf16),
            VMEM((wide, PAD), bf16),
            VMEM((PAD, wide), bf16),
            VMEM((PAD, wide), bf16),
            VMEM((PAD, wide), f32),
        ],
        compiler_params=pltpu.CompilerParams(vmem_limit_bytes=vmem_cap),
        cost_estimate=busy(24),
        name="attend_back",
    )(plan, q, own, oth, kpos, meta, grad, o, lse)


def unproject_kernel(
    place_ref, x_ref, dq_ref, down_ref, doth_ref, weight_ref,
    pieces_ref, grad_ref, gain_ref, shift_ref, bias_ref,
):
    i = pl.program_id(0)
    span_rows = pieces_ref.shape[1]

    @pl.when(i == 0)
    def _():
        gain_ref[...] = jnp.zeros_like(gain_ref)
        shift_ref[...] = jnp.zeros_like(shift_ref)
        bias_ref[...] = jnp.zeros_like(bias_ref)

    normed, unused = norm_parts(x_ref[...].astype(f32))
    dkv = (down_ref[...] + doth_ref[...].astype(f32)).astype(bf16)
    grad = jnp.concatenate([dq_ref[...], dkv], axis=1)
    grad_ref[...] = jnp.concatenate(
        [grad[:, :192], grad[:, PAD : PAD + 192], grad[:, 2 * PAD : 2 * PAD + 192], grad[:, 192:PAD]],
        axis=1,
    )
    bias_ref[...] += jnp.sum(grad.astype(f32), axis=0, keepdims=True)
    back = dot(grad, weight_ref[...], ((1,), (1,)))
    gain_ref[...] += jnp.sum(back * normed, axis=0, keepdims=True)
    shift_ref[...] += jnp.sum(back, axis=0, keepdims=True)
    for t in range(4):
        pieces_ref[place_ref[4 * i + t]] = back[span_rows * t : span_rows * (t + 1)].astype(bf16)


def unproject(place, x, dq, down, doth, weight, spans):
    rows, width = x.shape
    step = rows // 4
    pieces = jax.ShapeDtypeStruct((spans, rows // spans, width), bf16)
    grid_spec = pltpu.PrefetchScalarGridSpec(
        num_scalar_prefetch=1,
        grid=(4,),
        in_specs=[
            pl.BlockSpec((step, width), lambda i, *unused: (i, 0)),
            pl.BlockSpec((step, PAD), lambda i, *unused: (i, 0)),
            pl.BlockSpec((step, 2 * PAD), lambda i, *unused: (i, 0)),
            pl.BlockSpec((step, 2 * PAD), lambda i, *unused: (i, 0)),
            full_spec((width, 3 * PAD)),
        ],
        out_specs=[
            full_spec(pieces.shape),
            pl.BlockSpec((step, PACK), lambda i, *unused: (i, 0)),
            full_spec((1, width)),
            full_spec((1, width)),
            full_spec((1, 3 * PAD)),
        ],
    )
    return pl.pallas_call(
        unproject_kernel,
        grid_spec=grid_spec,
        out_shape=[
            pieces,
            jax.ShapeDtypeStruct((rows, PACK), bf16),
            jax.ShapeDtypeStruct((1, width), f32),
            jax.ShapeDtypeStruct((1, width), f32),
            jax.ShapeDtypeStruct((1, 3 * PAD), f32),
        ],
        compiler_params=pltpu.CompilerParams(vmem_limit_bytes=vmem_cap),
        cost_estimate=busy(8),
        name="unproject",
    )(place, x, dq, down, doth, weight)


def halve(value, bit):
    value = value.reshape(2, value.shape[0] // 2, value.shape[1])
    return row(value, bit), row(value, 1 - bit)


def reduce_z(value, z):
    value = value.reshape(4, value.shape[0] // 4, value.shape[1])
    return row(value, z), [row(value, (z + k) % 4) for k in (1, 2, 3)]


def over_z(sends):
    return [send_z(sends[k - 1], k) for k in (1, 2, 3)]


def reduce_plane(value, group):
    value = value.reshape(4, value.shape[0] // 4, value.shape[1])
    return row(value, group), [row(value, group ^ f) for f in (1, 2, 3)]


def over_plane(sends):
    return [send_flip(sends[f - 1], f) for f in (1, 2, 3)]


def gather_z(value):
    pair = jnp.stack([value, send_flip(value, 8)])
    return jnp.concatenate([pair, send_flip(pair, 4)], axis=0)


def spread_once(left, right):
    return jnp.concatenate([left, send_flip(left, 1)], axis=0), jnp.concatenate(
        [right, send_flip(right, 2)], axis=0
    )


def spread_twice(left, right):
    return left, send_flip(left, 2), right, send_flip(right, 1)


def cut_lanes(value, at):
    return value[:, :, :at], value[:, :, at:]


def entry(refs, side, f, k):
    if side == 0:
        return refs[f // 2][4 * (f % 2) + k].astype(f32)
    return refs[2 + f % 2][4 * (f // 2) + k].astype(f32)


def block_of(z, k):
    return ((z & 1) ^ (k >> 1)) * 2 + ((z >> 1) ^ (k & 1))


def chip_of(z, k):
    return z ^ ((k >> 1) + 2 * (k & 1))


def place_proj_kernel(where_ref, *refs):
    parts, out_ref = refs[:4], refs[4]
    z, group = where_ref[0], where_ref[1]
    rows, half = parts[0].shape[1:]
    for f in range(4):
        x, y = (group ^ f) & 1, (group ^ f) >> 1
        for k in range(4):
            at = ((2 * x + y) * 4 + block_of(z, k)) * rows
            out_ref[pl.ds(pl.multiple_of(at, 8), rows), :half] = entry(parts, 0, f, k)
            at = ((2 * y + x) * 4 + block_of(z, k)) * rows
            out_ref[pl.ds(pl.multiple_of(at, 8), rows), half:] = entry(parts, 1, f, k)


def place_rest_kernel(where_ref, *refs):
    parts, fc_ref, out_ref = refs[:4], refs[4], refs[5]
    z, group = where_ref[0], where_ref[1]
    rows, half = parts[0].shape[1:]
    fc_wide = fc_ref.shape[1]
    for f in range(4):
        for k in range(4):
            at = ((group ^ f) * 4 + chip_of(z, k)) * rows
            at = pl.ds(pl.multiple_of(at, 8), rows)
            fc_ref[at, :half] = entry(parts, 0, f, k)
            right = entry(parts, 1, f, k)
            fc_ref[at, half:] = right[:, : fc_wide - half]
            out_ref[at, :] = right[:, fc_wide - half :]


def place_in_kernel(where_ref, *refs):
    parts, in_ref, small_ref, held = refs[:4], refs[4], refs[5], refs[6]
    z, group = where_ref[0], where_ref[1]
    upper = parts[0].shape[1]
    rows = upper + parts[2].shape[1] - 8
    small_ref[...] = jnp.zeros(small_ref.shape, f32)
    for f in range(4):
        for k in range(4):
            block = z ^ k
            held[group ^ f, block, :upper] = entry(parts, 0, f, k)
            right = entry(parts, 1, f, k)
            held[group ^ f, block, upper:rows] = right[:-8]
            small_ref[block] = small_ref[block] + right[-8:]
    for block in range(4):
        for i in range(3):
            at = 192 * i
            columns = [held[g, block, :, at : at + 192] for g in range(4)]
            in_ref[rows * block : rows * (block + 1), 768 * i : 768 * (i + 1)] = jnp.concatenate(
                columns, axis=1
            )


def place(kernel, name, micros, where, parts, shapes, scratch=()):
    return pl.pallas_call(
        kernel,
        in_specs=[pl.BlockSpec(memory_space=pltpu.SMEM)]
        + [pl.BlockSpec(memory_space=pltpu.VMEM)] * len(parts),
        out_specs=[pl.BlockSpec(memory_space=pltpu.VMEM)] * len(shapes),
        out_shape=[jax.ShapeDtypeStruct(shape, f32) for shape in shapes],
        scratch_shapes=list(scratch),
        compiler_params=pltpu.CompilerParams(vmem_limit_bytes=vmem_cap),
        cost_estimate=busy(micros),
        name=name,
    )(where, *parts)


def split_halves(value, w, axis):
    low, high = jnp.split(value, 2, axis)
    return jnp.where(w == 0, low, high), jnp.where(w == 0, high, low)


def grad_dot(left, right):
    return dot(left, right, ((0,), (0,)))


def norm_back(grad, rows, gain):
    normed, inverse = norm_parts(rows)
    scaled = grad * gain
    part = scaled - jnp.mean(scaled, axis=-1, keepdims=True)
    part = part - normed * jnp.mean(scaled * normed, axis=-1, keepdims=True)
    return inverse * part, normed


def by_owner(
    block_input, span_order, doc_lengths, ln1_gain, ln1_bias, w_qkv, qv_bias, w_out, out_bias,
    ln2_gain, ln2_bias, w_fc, fc_bias, w_proj, proj_bias, d_out,
):
    seq_group, seq_dev, width = block_input.shape
    seqs = 2 * seq_group
    span_rows = seq_dev // 2
    chips = span_order.shape[0]
    rows = chips * span_rows
    me = lax.axis_index("ctx")
    w = lax.axis_index("wt")
    z, y, x = me // 4, me // 2 % 2, me % 2
    where = (z, y, x)
    group = me % 4

    second = (row(span_order, me)[0] % 2) != w

    def take_spans(value):
        value = value.reshape(seq_group, 2, span_rows, width)
        keep = jnp.where(second, value[:, 1], value[:, 0])
        give = jnp.where(second, value[:, 0], value[:, 1])
        got = other_core(give)
        return jnp.where(
            w == 0, jnp.concatenate([keep, got], axis=0), jnp.concatenate([got, keep], axis=0)
        )

    def give_spans(value):
        low, high = value[:seq_group], value[seq_group:]
        keep = jnp.where(w == 0, low, high)
        got = other_core(jnp.where(w == 0, high, low))
        first = jnp.where(second, got, keep)
        last = jnp.where(second, keep, got)
        return jnp.concatenate([first, last], axis=1)

    def to_sequence(value):
        got = [send_z(row(value, (z + k) % 4), k) for k in (1, 2, 3)]
        return [row(value, z)] + got

    z_low, z_high = z % 2, z // 2

    def z_first(blocks):
        keep = jnp.stack([row(blocks, z_low + 2 * h) for h in (0, 1)])
        give = jnp.stack([row(blocks, 1 - z_low + 2 * h) for h in (0, 1)])
        return keep, send_flip(give, 4)

    def z_second(keep, got):
        pairs = jnp.stack([keep, got], axis=1)
        here, there = row(pairs, z_high), send_flip(row(pairs, 1 - z_high), 8)
        return jnp.concatenate([here, there], axis=0)

    def by_chip(value):
        return jnp.stack([row(value, (z - s) % 4) for s in range(seqs)])

    def by_source(got):
        return jnp.stack([row(got, z ^ s) for s in range(seqs)])

    kept = to_sequence(take_spans(block_input))
    left, right = jnp.stack(kept[:2]), jnp.stack(kept[2:])
    tokens_low = jnp.concatenate([left, right], axis=0)
    span_order, doc_lengths, d_out, unused = lax.optimization_barrier(
        (span_order, doc_lengths, d_out, (left, right))
    )
    left_x, right_y = send_flip(left, 1), send_flip(right, 2)
    ranks = jnp.arange(rows, dtype=jnp.int32)
    even_pos = 2 * span_rows * (ranks // span_rows) + ranks % span_rows
    own_pos = even_pos + span_rows * w
    oth_pos = even_pos + span_rows * (1 - w)
    kpos = jnp.broadcast_to(jnp.stack([own_pos, oth_pos])[:, :, None], (2, rows, TILE)).astype(jnp.int32)
    left_x, right_y, kpos = lax.optimization_barrier((left_x, right_y, kpos))
    left = jnp.concatenate([left, left_x], axis=0)
    right = jnp.concatenate([right, right_y], axis=0)
    pieces = (left, send_flip(left, 2), right, send_flip(right, 1))
    (
        ln1_gain, ln1_bias, w_qkv, qv_bias, out_bias, ln2_gain, ln2_bias, proj_bias, fc_bias, unused,
    ) = lax.optimization_barrier(
        (
            ln1_gain, ln1_bias, w_qkv, qv_bias, out_bias, ln2_gain, ln2_bias, proj_bias, fc_bias,
            (left, right),
        )
    )
    cot_low = jnp.stack(to_sequence(take_spans(d_out))).reshape(seqs * span_rows, width)
    d_mlp = (branch_scale * cot_low.astype(f32)).astype(bf16)

    chip_ids = jnp.arange(chips, dtype=jnp.int32)
    span_here = jnp.where(span_order[:, 0] % 2 == w, span_order[:, 0], span_order[:, 1]) // 2
    span_ids = jnp.arange(chips, dtype=jnp.int32)
    holder = jnp.sum(
        jnp.where(span_here[None, :] == span_ids[:, None], chip_ids[None, :], 0), axis=1
    ).astype(jnp.int32)
    back_z = (z - holder // 4) % 4
    flip = group ^ (holder % 4)
    order = jnp.where(
        back_z < 2,
        (flip // 2) * 4 + (flip % 2) * 2 + back_z,
        8 + (flip % 2) * 4 + (flip // 2) * 2 + back_z - 2,
    ).astype(jnp.int32)
    order_back = (flip * 4 + back_z).astype(jnp.int32)
    owner = (holder % 4 * 4 + back_z).astype(jnp.int32)

    lengths_oth = other_core(doc_lengths)
    lengths = jnp.where(
        w == 0,
        jnp.concatenate([doc_lengths, lengths_oth], axis=0),
        jnp.concatenate([lengths_oth, doc_lengths], axis=0),
    )
    lengths = row(lengths, z)
    ends = jnp.cumsum(lengths)[:-1]
    starts = jnp.sum(
        jnp.where(own_pos[:, None] >= ends[None, :], lengths[None, :-1], 0), axis=1
    ).astype(jnp.int32)
    tiles = rows // TILE
    own_tiles = own_pos.reshape(tiles, TILE)
    start_tiles = starts.reshape(tiles, TILE)
    meta = jnp.tile(jnp.stack([own_tiles, start_tiles], axis=1), (1, 1, 3)).astype(jnp.int32)
    even_tiles = even_pos.reshape(tiles, TILE)
    low = jnp.sum(
        (even_tiles[None, :, -1] + span_rows < start_tiles[:, 0:1]).astype(jnp.int32), axis=1
    ).astype(jnp.int32)
    high = jnp.sum(
        (even_tiles[None, :, 0] <= own_tiles[:, -1:]).astype(jnp.int32), axis=1
    ).astype(jnp.int32)

    room = jnp.zeros((chips - tiles,), jnp.int32)
    plan = jnp.stack([jnp.concatenate([low, room]), jnp.concatenate([high, room]), owner])

    feats = width // GROUPS
    half = width // 2
    here = jnp.stack([z, group, w]).astype(jnp.int32)
    in_own = jnp.concatenate(
        [
            lax.dynamic_slice_in_dim(w_qkv, width * i + half * (group // 2), half, 1)
            for i in range(3)
        ],
        axis=1,
    )
    in_oth_core = other_core(in_own)
    vectors = [ln1_gain, ln1_bias, qv_bias[0], qv_bias[1], out_bias, ln2_gain, ln2_bias, proj_bias]
    vectors += [fc_bias[half * i : half * (i + 1)] for i in range(4)]
    lines = lax.broadcasted_iota(jnp.int32, (len(vectors), half), 0)
    small = jnp.zeros((len(vectors), half), f32)
    for i, one in enumerate(vectors):
        small = jnp.where(lines == i, jnp.broadcast_to(one.astype(f32), small.shape), small)
    small_oth = other_core(small)

    def vector(index):
        own, oth = small[index : index + 1], small_oth[index : index + 1]
        return jnp.concatenate([jnp.where(w == 0, own, oth), jnp.where(w == 0, oth, own)], axis=1)

    pieces, w_out, w_fc, w_proj, unused = lax.optimization_barrier(
        (pieces, w_out, w_fc, w_proj, (meta, plan, in_oth_core, small_oth, d_mlp))
    )
    out_oth, fc_oth, proj_oth = other_core(w_out), other_core(w_fc), other_core(w_proj)
    x_sorted, normed_one, query, kv_own, weight_in = project(
        order, here, pieces, in_own, in_oth_core, small, small_oth
    )
    query, kv_own, out_oth, fc_oth, proj_oth = lax.optimization_barrier(
        (query, kv_own, out_oth, fc_oth, proj_oth)
    )
    kv_oth = other_core(kv_own)
    attn, lse, attn_send = attend(plan, query, kv_own, kv_oth, kpos, meta, chips)
    attn_got = swap_plane(attn_send.reshape(GROUPS, seqs, span_rows, feats))

    d_mlp = after(d_mlp, attn_send)
    mlp_both = jnp.concatenate([d_mlp, other_core(d_mlp)], axis=0)
    grad_own = dot(d_mlp, w_proj, ((1,), (1,)))
    attn_got = after(attn_got, grad_own, mlp_both).reshape(GROUPS, seqs * span_rows, feats)

    tokens = tokens_low.reshape(seqs * span_rows, width)
    (
        resid, attn_own, attn_oth, normed_own, normed_oth, hidden_own, hidden_oth, d_pre, d_resid, d_branch, d_send, *sums
    ) = middle(
        attn_got, tokens, cot_low, d_mlp, grad_own, proj_oth,
        w_out, out_oth, w_fc, fc_oth, here, small, small_oth,
    )
    d_got = swap_plane(d_send.reshape(GROUPS, seqs, span_rows, feats)).reshape(chips, span_rows, feats)
    hidden_both = jnp.concatenate([hidden_own, other_core(hidden_oth)], axis=0)
    pre_got = other_core(d_pre)
    normed_got_rows = other_core(normed_oth)
    attn_got_rows = other_core(attn_oth)
    low_bit, high_bit = z % 2, z // 2
    branch_got = other_core(d_branch)
    hidden_both = after(hidden_both, d_send)
    grad_proj = grad_dot(hidden_both, mlp_both).astype(bf16)
    proj_left, left_send = halve(grad_proj[:, :half], x)
    proj_right, right_send = halve(grad_proj[:, half:], y)
    left_recv, right_recv = send_flip(left_send, 1), send_flip(right_send, 2)
    normed_own, normed_got_rows, attn_own, attn_got_rows, d_got, unused = lax.optimization_barrier(
        (normed_own, normed_got_rows, attn_own, attn_got_rows, d_got, (left_send, right_send))
    )
    fc_cols = d_pre.shape[1]
    grad_rest = jnp.concatenate(
        [
            (grad_dot(normed_own, d_pre) + grad_dot(normed_got_rows, pre_got)).astype(bf16),
            (grad_dot(attn_own, d_branch) + grad_dot(attn_got_rows, branch_got)).astype(bf16),
        ],
        axis=1,
    )
    rest_keep, rest_sends = reduce_plane(grad_rest, group)
    left_recv, right_recv, unused = lax.optimization_barrier((left_recv, right_recv, rest_sends))
    proj_left, left_send = halve(sum_low(proj_left, left_recv), y)
    proj_right, right_send = halve(sum_low(proj_right, right_recv), x)
    left_recv, right_recv = send_flip(left_send, 2), send_flip(right_send, 1)
    rest_plane = over_plane(rest_sends)

    d_got = after(d_got, left_send, right_send, *rest_sends)
    d_query, d_own, d_oth = attend_back(plan, query, kv_own, kv_oth, kpos, meta, d_got, attn, lse)
    hidden_own, hidden_oth, unused = lax.optimization_barrier((hidden_own, hidden_oth, d_query))
    mlp = dot(hidden_own, w_proj, ((1,), (0,))) + dot(hidden_oth, proj_oth, ((1,), (0,))) + vector(7)
    block_out = (resid + branch_scale * mlp).astype(bf16).reshape(seqs, span_rows, width)
    block_out = by_chip(block_out)
    left_recv, right_recv, rest_plane, d_query, d_oth, block_out = lax.optimization_barrier(
        (left_recv, right_recv, rest_plane, d_query, d_oth, block_out)
    )
    d_recv = other_core(d_oth)
    grad_proj = jnp.concatenate(
        [sum_low(proj_left, left_recv), sum_low(proj_right, right_recv)], axis=1
    )
    proj_keep, proj_send = halve(grad_proj, low_bit)
    proj_recv = send_flip(proj_send, 4)
    rest_keep, rest_sends = reduce_z(sum_low(rest_keep, *rest_plane), z)
    proj_recv, d_recv, rest_sends, block_out = lax.optimization_barrier(
        (proj_recv, d_recv, rest_sends, block_out)
    )
    block_out = z_first(block_out)
    rest_z = over_z(rest_sends)
    proj_keep, proj_send = halve(sum_low(proj_keep, proj_recv), high_bit)
    proj_recv = send_flip(proj_send, 8)
    d_recv = after(d_recv, proj_send)
    d_pieces, d_qkv, part_gain, part_shift, part_bias = unproject(
        order_back, x_sorted, d_query, d_own, d_recv, weight_in, chips
    )
    proj_recv, rest_z, d_pieces, d_qkv, part_gain, part_shift, part_bias, sums, block_out = (
        lax.optimization_barrier(
            (proj_recv, rest_z, d_pieces, d_qkv, part_gain, part_shift, part_bias, sums, block_out)
        )
    )

    proj_shard = sum_low(proj_keep, proj_recv)
    rest_shard = sum_low(rest_keep, *rest_z)
    d_qkv, unused = lax.optimization_barrier((d_qkv, (proj_shard, rest_shard)))
    proj_pair = jnp.stack([proj_shard, send_flip(proj_shard, 8)])
    rest_pair = jnp.stack([rest_shard, send_flip(rest_shard, 8)])
    back_sends = [d_pieces[4 * f : 4 * f + 4] for f in (1, 2, 3)]
    back_x, back_y = send_flip(back_sends[0], 1), send_flip(back_sends[1], 2)
    normed_own, normed_oth = split_halves(normed_one, w, 1)
    in_oth = grad_dot(normed_oth, d_qkv).astype(bf16)
    in_got = other_core(in_oth)
    grads_own, grads_oth = pack(here, part_gain, part_shift, part_bias, sums)
    small_rows = (grads_own + other_core(grads_oth)).astype(bf16).reshape(4, 3, half)
    small_rows = jnp.pad(small_rows, ((0, 0), (0, 5), (0, PACK - half)))
    grad_in = (grad_dot(normed_own, d_qkv) + in_got.astype(f32)).astype(bf16)
    grad_in = jnp.concatenate([grad_in.reshape(4, half // 4, PACK), small_rows], axis=1)
    in_keep, in_send = halve(grad_in.reshape(-1, PACK), high_bit)
    proj_pair, rest_pair, back_x, back_y, back_xy, in_send = lax.optimization_barrier(
        (proj_pair, rest_pair, back_x, back_y, back_sends[2], in_send)
    )
    proj_all = jnp.concatenate([proj_pair, send_flip(proj_pair, 4)], axis=0)
    rest_all = jnp.concatenate([rest_pair, send_flip(rest_pair, 4)], axis=0)
    in_recv = send_flip(in_send, 8)
    back_xy = send_flip(back_xy, 3)
    proj_all, rest_all, in_recv, back_xy = lax.optimization_barrier((proj_all, rest_all, in_recv, back_xy))
    in_keep, in_send = halve(sum_low(in_keep, in_recv), low_bit)
    in_recv = send_flip(in_send, 4)
    proj_once = spread_once(*cut_lanes(proj_all, half))
    rest_once = spread_once(*cut_lanes(rest_all, rest_all.shape[2] // 2))
    proj_once, rest_once, in_recv = lax.optimization_barrier((proj_once, rest_once, in_recv))
    in_shard = sum_low(in_keep, in_recv)
    in_pair = jnp.stack([in_shard, send_flip(in_shard, 4)])
    proj_parts = spread_twice(*proj_once)
    back = sum_low(d_pieces[:4], back_x, back_y, after(back_xy, in_shard))
    block_out, unused = lax.optimization_barrier((block_out, in_shard))
    block_out = z_second(*block_out)
    proj_parts, in_pair, rest_once, back, block_out = lax.optimization_barrier(
        (proj_parts, in_pair, rest_once, back, block_out)
    )
    in_all = jnp.concatenate([in_pair, send_flip(in_pair, 8)], axis=0)
    rest_parts = spread_twice(*rest_once)
    d_first, unused = norm_back(
        back.reshape(seqs * span_rows, width).astype(f32), tokens.astype(f32), vector(0)
    )
    d_input = (d_resid + d_first).astype(bf16).reshape(seqs, span_rows, width)
    d_input = z_first(by_chip(d_input))
    rest_parts, in_all, proj_parts, d_input = lax.optimization_barrier(
        (rest_parts, in_all, proj_parts, d_input)
    )
    in_once = spread_once(in_all[:, :56], in_all[:, 56:])
    in_once, d_input, block_out, proj_parts, rest_parts = lax.optimization_barrier(
        (in_once, d_input, block_out, proj_parts, rest_parts)
    )
    in_parts = spread_twice(*in_once)
    d_input = z_second(*d_input)
    (grad_proj,) = place(
        place_proj_kernel, "place_proj", 5, here, proj_parts, [(fc_cols // 2, width)]
    )
    grad_fc, grad_out = place(
        place_rest_kernel, "place_rest", 5, here, rest_parts, [(half, fc_cols), (half, width)]
    )
    grad_w_qkv, small_all = place(
        place_in_kernel, "place_in", 4, here, in_parts,
        [(half, 3 * width), (4, 8, PACK)],
        [VMEM((4, 4, half // 4, PACK), f32)],
    )

    def piece(index):
        return small_all[index // 3, index % 3, :half]

    return (
        give_spans(by_source(block_out)),
        give_spans(by_source(d_input)).astype(f32),
        piece(0),
        piece(1),
        grad_w_qkv,
        jnp.stack([piece(2), piece(3)]),
        grad_out,
        piece(4),
        piece(5),
        piece(6),
        grad_fc,
        jnp.concatenate([piece(8), piece(9), piece(10), piece(11)]),
        grad_proj,
        piece(7),
    )


def layer_norm(values, gain, shift):
    center = jnp.mean(values, axis=-1, keepdims=True)
    moved = values - center
    spread = jnp.mean(moved * moved, axis=-1, keepdims=True)
    return moved * lax.rsqrt(spread + 1e-05) * gain + shift


def gelu_tanh(values):
    return (
        0.5
        * values
        * (1.0 + jnp.tanh(0.7978845608028654 * (values + 0.044715 * values * values * values)))
    )


def split_count(row_total, limit):
    pieces = 1
    while row_total % pieces != 0 or row_total // pieces > limit:
        pieces += 1
    return pieces


def row_positions(order_table, first_index, row_total, seq_dev, span_rows):
    rows_here = first_index + jnp.arange(row_total, dtype=jnp.int32)
    device_of = rows_here // seq_dev
    half_of = rows_here % seq_dev // span_rows
    slot_index = device_of * 2 + half_of
    flat_order = order_table.reshape(-1)
    table_slots = jnp.arange(flat_order.shape[0], dtype=jnp.int32)
    picked = jnp.sum(
        jnp.where(slot_index[:, None] == table_slots[None, :], flat_order[None, :], 0), axis=1
    )
    return picked * span_rows + rows_here % span_rows


def doc_of(positions, lengths_row):
    ends_at = jnp.cumsum(lengths_row)
    inner_ends = ends_at[:-1]
    return jnp.sum((positions[:, None] >= inner_ends[None, :]).astype(jnp.int32), axis=1)


def visible(query_pos, query_doc, key_pos, key_doc):
    causal = key_pos[None, None, :] <= query_pos[None, :, None]
    same_doc = key_doc[:, None, :] == query_doc[:, :, None]
    return (causal & same_doc)[:, :, None, :]


def per_device(
    block_input,
    span_order,
    doc_lengths,
    ln1_gain,
    ln1_bias,
    w_qkv,
    qv_bias,
    w_out,
    out_bias,
    ln2_gain,
    ln2_bias,
    w_fc,
    fc_bias,
    w_proj,
    proj_bias,
    d_out,
):
    seq_group, seq_dev, width = block_input.shape
    heads = HEADS
    head_dim = width // heads
    span_rows = seq_dev // 2
    score_scale = head_dim ** (-0.5)

    def docs_for(positions):
        return jax.vmap(doc_of, in_axes=(None, 0))(positions, doc_lengths)

    weights_all = (
        lax.all_gather(ln1_gain, "wt", axis=0, tiled=True),
        lax.all_gather(ln1_bias, "wt", axis=0, tiled=True),
        lax.all_gather(w_qkv, "wt", axis=0, tiled=True),
        lax.all_gather(qv_bias, "wt", axis=1, tiled=True),
        lax.all_gather(w_out, "wt", axis=0, tiled=True),
        lax.all_gather(out_bias, "wt", axis=0, tiled=True),
        lax.all_gather(ln2_gain, "wt", axis=0, tiled=True),
        lax.all_gather(ln2_bias, "wt", axis=0, tiled=True),
        lax.all_gather(w_fc, "wt", axis=0, tiled=True),
        lax.all_gather(fc_bias, "wt", axis=0, tiled=True),
        lax.all_gather(w_proj, "wt", axis=0, tiled=True),
        lax.all_gather(proj_bias, "wt", axis=0, tiled=True),
    )
    gain_one = weights_all[0].astype(jnp.float32)
    shift_one = weights_all[1].astype(jnp.float32)
    bias_pair = weights_all[3].astype(jnp.float32)
    bias_out = weights_all[5].astype(jnp.float32)
    gain_two = weights_all[6].astype(jnp.float32)
    shift_two = weights_all[7].astype(jnp.float32)
    bias_fc = weights_all[9].astype(jnp.float32)
    bias_proj = weights_all[11].astype(jnp.float32)
    me_ctx = lax.axis_index("ctx")
    local_pos = row_positions(span_order, me_ctx * seq_dev, seq_dev, seq_dev, span_rows)
    local_doc = docs_for(local_pos)
    tokens_in = block_input.astype(jnp.float32)
    normed_one = layer_norm(tokens_in, gain_one, shift_one).astype(jnp.bfloat16)
    qkv_bias = jnp.concatenate([bias_pair[0], jnp.zeros((width,), jnp.float32), bias_pair[1]])
    projected = (
        jnp.einsum("btd,de->bte", normed_one, weights_all[2], preferred_element_type=jnp.float32)
        + qkv_bias
    )
    projected_low = projected.astype(jnp.bfloat16)
    query_low = projected_low[..., :width]
    key_low = projected_low[..., width : 2 * width]
    value_low = projected_low[..., 2 * width :]
    query_heads = query_low.reshape(seq_group, seq_dev, heads, head_dim)
    key_heads = key_low.reshape(seq_group, seq_dev, heads, head_dim)
    value_heads = value_low.reshape(seq_group, seq_dev, heads, head_dim)
    start_state = (
        jnp.zeros((seq_group, seq_dev, heads, head_dim), jnp.float32),
        jnp.full((seq_group, seq_dev, heads), neg_large, jnp.float32),
        jnp.zeros((seq_group, seq_dev, heads), jnp.float32),
    )
    key_piece = lax.all_gather(key_low, "ctx", axis=1, tiled=True)
    value_piece = lax.all_gather(value_low, "ctx", axis=1, tiled=True)
    piece_rows = key_piece.shape[1]
    key_pos = row_positions(span_order, jnp.int32(0), piece_rows, seq_dev, span_rows)
    key_doc = docs_for(key_pos)
    block_rows = piece_rows // split_count(piece_rows, 1024)

    def one_block(block_index, running):
        acc_sum, run_max, run_total = running
        first_row = block_index * block_rows
        key_block = lax.dynamic_slice_in_dim(key_piece, first_row, block_rows, 1).reshape(
            seq_group, block_rows, heads, head_dim
        )
        value_block = lax.dynamic_slice_in_dim(value_piece, first_row, block_rows, 1).reshape(
            seq_group, block_rows, heads, head_dim
        )
        allowed = visible(
            local_pos,
            local_doc,
            lax.dynamic_slice_in_dim(key_pos, first_row, block_rows, 0),
            lax.dynamic_slice_in_dim(key_doc, first_row, block_rows, 1),
        )
        scores = (
            jnp.einsum(
                "bqhd,bkhd->bqhk", query_heads, key_block, preferred_element_type=jnp.float32
            )
            * score_scale
        )
        scores = jnp.where(allowed, scores, neg_large)
        new_max = jnp.maximum(run_max, jnp.max(scores, axis=-1))
        weights = jnp.where(allowed, jnp.exp(scores - new_max[..., None]), 0.0)
        rescale = jnp.exp(run_max - new_max)
        run_total = run_total * rescale + jnp.sum(weights, axis=-1)
        acc_sum = acc_sum * rescale[..., None] + jnp.einsum(
            "bqhk,bkhd->bqhd",
            weights.astype(jnp.bfloat16),
            value_block,
            preferred_element_type=jnp.float32,
        )
        return (acc_sum, new_max, run_total)

    acc_sum, run_max, run_total = lax.fori_loop(0, piece_rows // block_rows, one_block, start_state)
    attn_heads = acc_sum / run_total[..., None]
    log_total = run_max + jnp.log(run_total)
    attn_out = attn_heads.reshape(seq_group, seq_dev, width)
    attn_low = attn_out.astype(jnp.bfloat16)
    branch_pre = (
        jnp.einsum("btd,de->bte", attn_low, weights_all[4], preferred_element_type=jnp.float32)
        + bias_out
    )
    resid_one = tokens_in + branch_scale * branch_pre
    normed_two = layer_norm(resid_one, gain_two, shift_two).astype(jnp.bfloat16)
    hidden_pre = (
        jnp.einsum("btd,df->btf", normed_two, weights_all[8], preferred_element_type=jnp.float32)
        + bias_fc
    )
    hidden_low = gelu_tanh(hidden_pre).astype(jnp.bfloat16)
    mlp_pre = (
        jnp.einsum("btf,fd->btd", hidden_low, weights_all[10], preferred_element_type=jnp.float32)
        + bias_proj
    )
    block_out = (resid_one + branch_scale * mlp_pre).astype(jnp.bfloat16)
    weights_back = (
        lax.all_gather(ln1_gain, "wt", axis=0, tiled=True),
        lax.all_gather(ln1_bias, "wt", axis=0, tiled=True),
        lax.all_gather(w_qkv, "wt", axis=0, tiled=True),
        lax.all_gather(qv_bias, "wt", axis=1, tiled=True),
        lax.all_gather(w_out, "wt", axis=0, tiled=True),
        lax.all_gather(out_bias, "wt", axis=0, tiled=True),
        lax.all_gather(ln2_gain, "wt", axis=0, tiled=True),
        lax.all_gather(ln2_bias, "wt", axis=0, tiled=True),
        lax.all_gather(w_fc, "wt", axis=0, tiled=True),
        lax.all_gather(fc_bias, "wt", axis=0, tiled=True),
        lax.all_gather(w_proj, "wt", axis=0, tiled=True),
        lax.all_gather(proj_bias, "wt", axis=0, tiled=True),
    )
    back_gain_one = weights_back[0].astype(jnp.float32)
    back_shift_one = weights_back[1].astype(jnp.float32)
    back_gain_two = weights_back[6].astype(jnp.float32)
    back_shift_two = weights_back[7].astype(jnp.float32)
    cotangent = d_out.astype(jnp.float32)
    d_mlp = (branch_scale * cotangent).astype(jnp.bfloat16)
    grad_w_proj = jnp.einsum("btf,btd->fd", hidden_low, d_mlp, preferred_element_type=jnp.float32)
    grad_proj_bias = jnp.sum(d_mlp.astype(jnp.float32), axis=(0, 1))
    d_hidden = jnp.einsum(
        "btd,fd->btf", d_mlp, weights_back[10], preferred_element_type=jnp.float32
    )
    gelu_unused, gelu_pull = jax.vjp(gelu_tanh, hidden_pre)
    d_pre = gelu_pull(d_hidden)[0].astype(jnp.bfloat16)
    grad_w_fc = jnp.einsum("btd,btf->df", normed_two, d_pre, preferred_element_type=jnp.float32)
    grad_fc_bias = jnp.sum(d_pre.astype(jnp.float32), axis=(0, 1))
    d_normed_two = jnp.einsum(
        "btf,df->btd", d_pre, weights_back[8], preferred_element_type=jnp.float32
    )
    norm_unused, norm_pull = jax.vjp(layer_norm, resid_one, back_gain_two, back_shift_two)
    d_resid_part, grad_ln2_gain, grad_ln2_bias = norm_pull(d_normed_two)
    d_resid = cotangent + d_resid_part
    d_branch = (branch_scale * d_resid).astype(jnp.bfloat16)
    grad_w_out = jnp.einsum("btd,bte->de", attn_low, d_branch, preferred_element_type=jnp.float32)
    grad_out_bias = jnp.sum(d_branch.astype(jnp.float32), axis=(0, 1))
    d_attn_low = jnp.einsum(
        "bte,de->btd", d_branch, weights_back[4], preferred_element_type=jnp.float32
    ).astype(jnp.bfloat16)
    d_attn_heads = d_attn_low.reshape(seq_group, seq_dev, heads, head_dim)
    delta = jnp.sum(d_attn_heads.astype(jnp.float32) * attn_heads, axis=-1)
    fold_key_piece = lax.all_gather(key_low, "ctx", axis=1, tiled=True)
    fold_value_piece = lax.all_gather(value_low, "ctx", axis=1, tiled=True)
    piece_rows = fold_key_piece.shape[1]
    fold_key_pos = row_positions(span_order, jnp.int32(0), piece_rows, seq_dev, span_rows)
    fold_key_doc = docs_for(fold_key_pos)
    fold_block_rows = piece_rows // split_count(piece_rows, 1024)

    def one_block(block_index, grad_query):
        first_row = block_index * fold_block_rows
        key_block = lax.dynamic_slice_in_dim(fold_key_piece, first_row, fold_block_rows, 1).reshape(
            seq_group, fold_block_rows, heads, head_dim
        )
        value_block = lax.dynamic_slice_in_dim(
            fold_value_piece, first_row, fold_block_rows, 1
        ).reshape(seq_group, fold_block_rows, heads, head_dim)
        allowed = visible(
            local_pos,
            local_doc,
            lax.dynamic_slice_in_dim(fold_key_pos, first_row, fold_block_rows, 0),
            lax.dynamic_slice_in_dim(fold_key_doc, first_row, fold_block_rows, 1),
        )
        scores = (
            jnp.einsum(
                "bqhd,bkhd->bqhk", query_heads, key_block, preferred_element_type=jnp.float32
            )
            * score_scale
        )
        probs = jnp.where(allowed, jnp.exp(scores - log_total[..., None]), 0.0)
        d_probs = jnp.einsum(
            "bqhd,bkhd->bqhk", d_attn_heads, value_block, preferred_element_type=jnp.float32
        )
        d_scores = (probs * (d_probs - delta[..., None])).astype(jnp.bfloat16)
        return (
            grad_query
            + jnp.einsum("bqhk,bkhd->bqhd", d_scores, key_block, preferred_element_type=jnp.float32)
            * score_scale
        )

    grad_query = lax.fori_loop(
        0,
        piece_rows // fold_block_rows,
        one_block,
        jnp.zeros((seq_group, seq_dev, heads, head_dim), jnp.float32),
    )
    stats_all = (
        lax.all_gather(log_total, "ctx", axis=1, tiled=True),
        lax.all_gather(delta, "ctx", axis=1, tiled=True),
    )
    totals_every = stats_all[0]
    deltas_every = stats_all[1]

    def fold_keys(carried, received, first_index):
        query_piece, grad_piece = received
        piece_rows = query_piece.shape[1]
        query_pos = row_positions(span_order, first_index, piece_rows, seq_dev, span_rows)
        query_doc = docs_for(query_pos)
        block_rows = piece_rows // split_count(piece_rows, 1024)

        def one_block(block_index, running):
            grad_key, grad_value = running
            first_row = block_index * block_rows
            query_block = lax.dynamic_slice_in_dim(query_piece, first_row, block_rows, 1).reshape(
                seq_group, block_rows, heads, head_dim
            )
            grad_block = lax.dynamic_slice_in_dim(grad_piece, first_row, block_rows, 1).reshape(
                seq_group, block_rows, heads, head_dim
            )
            total_block = lax.dynamic_slice_in_dim(totals_every, first_row, block_rows, 1)
            delta_block = lax.dynamic_slice_in_dim(deltas_every, first_row, block_rows, 1)
            allowed = visible(
                lax.dynamic_slice_in_dim(query_pos, first_row, block_rows, 0),
                lax.dynamic_slice_in_dim(query_doc, first_row, block_rows, 1),
                local_pos,
                local_doc,
            )
            scores = (
                jnp.einsum(
                    "bqhd,bkhd->bqhk", query_block, key_heads, preferred_element_type=jnp.float32
                )
                * score_scale
            )
            probs = jnp.where(allowed, jnp.exp(scores - total_block[..., None]), 0.0)
            grad_value = grad_value + jnp.einsum(
                "bqhk,bqhd->bkhd",
                probs.astype(jnp.bfloat16),
                grad_block,
                preferred_element_type=jnp.float32,
            )
            d_probs = jnp.einsum(
                "bqhd,bkhd->bqhk", grad_block, value_heads, preferred_element_type=jnp.float32
            )
            d_scores = (probs * (d_probs - delta_block[..., None])).astype(jnp.bfloat16)
            grad_key = (
                grad_key
                + jnp.einsum(
                    "bqhk,bqhd->bkhd", d_scores, query_block, preferred_element_type=jnp.float32
                )
                * score_scale
            )
            return (grad_key, grad_value)

        return lax.fori_loop(0, piece_rows // block_rows, one_block, carried)

    zero_heads = jnp.zeros((seq_group, seq_dev, heads, head_dim), jnp.float32)
    grad_key, grad_value = fold_keys(
        (zero_heads, zero_heads),
        (
            lax.all_gather(query_low, "ctx", axis=1, tiled=True),
            lax.all_gather(d_attn_low, "ctx", axis=1, tiled=True),
        ),
        jnp.int32(0),
    )
    d_projected = jnp.concatenate(
        [
            grad_query.reshape(seq_group, seq_dev, width),
            grad_key.reshape(seq_group, seq_dev, width),
            grad_value.reshape(seq_group, seq_dev, width),
        ],
        axis=-1,
    ).astype(jnp.bfloat16)
    grad_w_qkv = jnp.einsum(
        "btd,bte->de", normed_one, d_projected, preferred_element_type=jnp.float32
    )
    column_sums = jnp.sum(d_projected.astype(jnp.float32), axis=(0, 1))
    grad_qv_bias = jnp.stack([column_sums[:width], column_sums[2 * width :]])
    d_normed_one = jnp.einsum(
        "bte,de->btd", d_projected, weights_back[2], preferred_element_type=jnp.float32
    )
    first_unused, first_pull = jax.vjp(layer_norm, tokens_in, back_gain_one, back_shift_one)
    d_input_part, grad_ln1_gain, grad_ln1_bias = first_pull(d_normed_one)
    d_input = d_resid + d_input_part
    shares = (
        lax.psum_scatter(
            grad_ln1_gain.astype(jnp.bfloat16), "wt", scatter_dimension=0, tiled=True
        ).astype(jnp.float32),
        lax.psum_scatter(
            grad_ln1_bias.astype(jnp.bfloat16), "wt", scatter_dimension=0, tiled=True
        ).astype(jnp.float32),
        lax.psum_scatter(
            grad_w_qkv.astype(jnp.bfloat16), "wt", scatter_dimension=0, tiled=True
        ).astype(jnp.float32),
        lax.psum_scatter(
            grad_qv_bias.astype(jnp.bfloat16), "wt", scatter_dimension=1, tiled=True
        ).astype(jnp.float32),
        lax.psum_scatter(
            grad_w_out.astype(jnp.bfloat16), "wt", scatter_dimension=0, tiled=True
        ).astype(jnp.float32),
        lax.psum_scatter(
            grad_out_bias.astype(jnp.bfloat16), "wt", scatter_dimension=0, tiled=True
        ).astype(jnp.float32),
        lax.psum_scatter(
            grad_ln2_gain.astype(jnp.bfloat16), "wt", scatter_dimension=0, tiled=True
        ).astype(jnp.float32),
        lax.psum_scatter(
            grad_ln2_bias.astype(jnp.bfloat16), "wt", scatter_dimension=0, tiled=True
        ).astype(jnp.float32),
        lax.psum_scatter(
            grad_w_fc.astype(jnp.bfloat16), "wt", scatter_dimension=0, tiled=True
        ).astype(jnp.float32),
        lax.psum_scatter(
            grad_fc_bias.astype(jnp.bfloat16), "wt", scatter_dimension=0, tiled=True
        ).astype(jnp.float32),
        lax.psum_scatter(
            grad_w_proj.astype(jnp.bfloat16), "wt", scatter_dimension=0, tiled=True
        ).astype(jnp.float32),
        lax.psum_scatter(
            grad_proj_bias.astype(jnp.bfloat16), "wt", scatter_dimension=0, tiled=True
        ).astype(jnp.float32),
    )
    totals = lax.psum(
        (
            shares[0],
            shares[1],
            shares[2],
            shares[3],
            shares[4],
            shares[5],
            shares[6],
            shares[7],
            shares[8],
            shares[9],
            shares[10],
            shares[11],
        ),
        "ctx",
    )
    return (
        block_out,
        d_input,
        totals[0],
        totals[1],
        totals[2],
        totals[3],
        totals[4],
        totals[5],
        totals[6],
        totals[7],
        totals[8],
        totals[9],
        totals[10],
        totals[11],
    )


def solution(mesh):
    placed = (
        P("wt", "ctx", None),
        P(),
        P("wt", None),
        P("wt"),
        P("wt"),
        P("wt", None),
        P(None, "wt"),
        P("wt", None),
        P("wt"),
        P("wt"),
        P("wt"),
        P("wt", None),
        P("wt"),
        P("wt", None),
        P("wt"),
        P("wt", "ctx", None),
    )
    fast = dict(mesh.shape) == {"ctx": 16, "wt": 2}
    return jax.shard_map(
        by_owner if fast else per_device,
        mesh=mesh,
        in_specs=placed,
        out_specs=(
            P("wt", "ctx", None),
            P("wt", "ctx", None),
            P("wt"),
            P("wt"),
            P("wt", None),
            P(None, "wt"),
            P("wt", None),
            P("wt"),
            P("wt"),
            P("wt"),
            P("wt", None),
            P("wt"),
            P("wt", None),
            P("wt"),
        ),
        check_vma=False,
    )
```
